32 devices in a mesh: ckpt: 2 (over y), lat: 4 (over z), col: 4 (over x, core).
Axes of the slice: x: 2, y: 2, z: 4, core: 2. Of those that a mesh axis runs over, the one named last changes fastest.
Arguments:
- code_ids: int32 [1024, 64], P(('ckpt', 'lat')), parts along dimension 0, may hold values from 0 to 32767, as said below
- code_vals: float32 [1024, 64], P(('ckpt', 'lat')), parts along dimension 0, may hold values from 0.2 to 5
- decoder: bfloat16 [65536, 5120], P(('ckpt', 'lat'), 'col'), parts along dimension 0, may hold values from -0.375 to 0.375
- dec_bias: bfloat16 [10240], P(('ckpt', 'col')), parts along dimension 0, may hold values from -3 to 3
- ln_gain: float32 [10240], P(('ckpt', 'col')), parts along dimension 0, may hold values from 0.5 to 1.5
- ln_bias: float32 [10240], P(('ckpt', 'col')), parts along dimension 0, may hold values from -2.5 to 2.5
- w_qkv: bfloat16 [10240, 3, 4096], P(('ckpt', 'col'), None, 'lat'), parts along dimension 0, may hold values from -0.078125 to 0.078125
- cache_kv: bfloat16 [2, 3072, 4096], P(None, ('ckpt', 'col'), 'lat'), parts along dimension 1
- positions: int32 [1024], P('ckpt'), parts along dimension 0, may hold values from 0 to 511, each once
- w_out: bfloat16 [8192, 5120], P(('ckpt', 'lat'), 'col'), parts along dimension 0, may hold values from -0.09375 to 0.09375
Outputs:
- layer_out: bfloat16 [1024, 5120], P(('ckpt', 'lat'), 'col'), parts along dimension 0
The draws below stay inside these ranges and needn't reach their ends.
There are 2 independent parts, one for each index of `ckpt`. The reference program is written for one: setup_inputs(seed, part) draws one part's arguments, and reference() takes and returns one part's arrays. A program takes and returns all parts, laid end to end along the dimension named above; each array names one. Nothing has to cross between parts.
Inputs may be any that keep to these rules, and one draw needn't show every extreme that they name: `code_ids`: the ids within a row are distinct.
All inputs are finite; a program needn't handle non-finite values.
Results may differ from the reference program's by a relative error of at most 0.0085.
The reference program's roundings to bfloat16 on the way count: a program that leaves them out, or rounds other values in their place, can miss the bound.
Values may be sent and summed in bfloat16 or wider, within the bound.
No kernel may reach another device: no remote copies, remote signals or barrier semaphores. Data moves between devices by JAX's collectives and lax.ppermute only.
A program may use at most 128 MiB of HBM per device.

```python
import math
import jax
import jax.numpy as jnp
from jax import lax

D = 5120
LATENTS = 32768
HEADS = 32
HEAD = 128
TOPK = 64
ROWS = 512
CONTEXT = 2048


def draw_code_ids(key, part):
    scores = jax.random.randint(key, (ROWS, LATENTS), 0, 16384, dtype=jnp.int32) * LATENTS
    scores = scores + jnp.arange(LATENTS, dtype=jnp.int32)[None, :]
    scores = scores.at[0, LATENTS - 1].set(2 ** 30).at[ROWS - 1, 0].set(2 ** 30)
    return lax.top_k(scores, TOPK)[1].astype(jnp.int32)


def draw_cache_kv(key, part):
    shape = (2, CONTEXT - ROWS, HEADS * HEAD)
    base = jax.random.normal(key, shape, jnp.float32)
    return base.astype(jnp.bfloat16)


def level_of(key, shape, cuts, smallest, high):
    factor_of, own = 1.0, jax.random.fold_in(key, 6)
    for axis_at, shards_of in cuts:
        draws = jnp.exp(jax.random.uniform(jax.random.fold_in(own, axis_at), (shards_of,), jnp.float32, smallest / len(cuts), high / len(cuts)))
        factor_of = factor_of * jnp.repeat(draws, shape[axis_at] // shards_of).reshape([-1 if axis == axis_at else 1 for axis in range(len(shape))])
    return factor_of


def noise(rng, extent, scale, bound, cuts=(), held_as=jnp.bfloat16):
    gain = level_of(rng, extent, cuts, -0.22, 0.18) if cuts else 1.0
    array = jax.random.normal(rng, extent, jnp.float32) * scale * gain
    return jnp.minimum(jnp.maximum(array, -bound), bound).astype(held_as)


def setup_inputs(seed: int = 0, part: int = 0) -> dict:
    seeds = jax.random.split(jax.random.key(seed), 11)
    part_splits = jax.random.split(jax.random.fold_in(seeds[10], part), 11)
    return {
        "code_ids": draw_code_ids(jax.random.fold_in(jax.random.fold_in(seeds[10], part), 71), part),
        "code_vals": jnp.clip(jnp.exp(math.log(5.0) - 3.218876 * jax.random.uniform(part_splits[1], (ROWS, TOPK), jnp.float32) ** level_of(part_splits[1], (ROWS, TOPK), ((0, 4),), -0.2, 0.2)), 0.2, 5.0),
        "decoder": noise(part_splits[2], (LATENTS, D), (4 * TOPK) ** -0.5, 0.375, ((0, 4), (1, 4))),
        "dec_bias": noise(part_splits[3], (D,), 0.5, 3.0, ((0, 4),)),
        "ln_gain": jnp.clip(1.0 + 0.1 * jax.random.normal(part_splits[4], (D,), jnp.float32), 0.5, 1.5),
        "ln_bias": noise(part_splits[5], (D,), 0.4, 2.5, ((0, 4),), jnp.float32),
        "w_qkv": noise(part_splits[6], (D, 3, HEADS * HEAD), D ** -0.5, 0.078125, ((0, 4), (2, 4))),
        "cache_kv": draw_cache_kv(jax.random.fold_in(jax.random.fold_in(seeds[10], part), 71), part),
        "positions": jax.random.permutation(part_splits[8], ROWS).astype(jnp.int32),
        "w_out": noise(part_splits[9], (HEADS * HEAD, D), (HEADS * HEAD) ** -0.5, 0.09375, ((0, 4), (1, 4))),
    }


def attend_all(queries, keys, values, query_pos, key_pos):
    heads = queries.shape[1] // HEAD
    query_heads = queries.reshape(queries.shape[0], heads, HEAD).astype(jnp.float32)
    key_heads = keys.reshape(keys.shape[0], heads, HEAD).astype(jnp.float32)
    value_heads = values.reshape(values.shape[0], heads, HEAD).astype(jnp.float32)
    scores = jnp.einsum('qhe,khe->hqk', query_heads, key_heads) * (1.0 / math.sqrt(HEAD))
    visible = key_pos[None, None, :] <= query_pos[None, :, None]
    scores = jnp.where(visible, scores, -1e+30)
    highest = lax.optimization_barrier(jnp.max(scores, axis=-1, keepdims=True))
    expo = jnp.exp(scores - highest)
    probs = (expo / lax.optimization_barrier(jnp.sum(expo, axis=-1, keepdims=True))).astype(jnp.bfloat16)
    mixed = jnp.einsum('hqk,khe->qhe', probs.astype(jnp.float32), value_heads)
    return mixed.reshape(queries.shape[0], heads * HEAD).astype(jnp.bfloat16)

def reference(code_ids, code_vals, decoder, dec_bias, ln_gain, ln_bias, w_qkv, cache_kv, positions, w_out):
    row_ids = jnp.broadcast_to(jnp.arange(ROWS, dtype=jnp.int32)[:, None], code_ids.shape)
    codes = jnp.zeros((ROWS, LATENTS), jnp.bfloat16).at[row_ids, code_ids].add(code_vals.astype(jnp.bfloat16))
    decoded = dec_bias.astype(jnp.float32) + jnp.dot(codes, decoder, preferred_element_type=jnp.float32)
    row_mean = lax.optimization_barrier(jnp.sum(decoded, axis=1)) / D
    row_var = lax.optimization_barrier(jnp.sum(decoded * decoded, axis=1)) / D - row_mean * row_mean
    inverse = 1.0 / jnp.sqrt(row_var + 1e-05)
    normed = ((decoded - row_mean[:, None]) * inverse[:, None] * ln_gain + ln_bias).astype(jnp.bfloat16)
    width = HEADS * HEAD
    qkv = jnp.dot(normed, w_qkv.reshape(D, 3 * width), preferred_element_type=jnp.float32).astype(jnp.bfloat16)
    queries = qkv[:, :width]
    keys = jnp.concatenate([cache_kv[0], qkv[:, width:2 * width]], axis=0)
    values = jnp.concatenate([cache_kv[1], qkv[:, 2 * width:]], axis=0)
    cached_len = cache_kv.shape[1]
    query_pos = cached_len + positions.astype(jnp.int32)
    key_pos = jnp.concatenate([jnp.arange(cached_len, dtype=jnp.int32), query_pos])
    attended = attend_all(queries, keys, values, query_pos, key_pos)
    result = decoded + jnp.dot(attended, w_out, preferred_element_type=jnp.float32)
    return result.astype(jnp.bfloat16)
```

```python
import functools
import math

import jax
import jax.numpy as jnp
from jax import lax
from jax.experimental import pallas as pl
from jax.experimental.pallas import tpu as pltpu
from jax.sharding import PartitionSpec as P

D = 5120
HEAD = 128
GROUP = 8
VMEM_BYTES = 48 * 1024 * 1024


def densify_kernel(base_ref, ids_ref, vals_ref, out_ref, *, topk, latents, lanes):
    groups, width = ids_ref.shape
    high = latents // lanes
    base = base_ref[0]
    row_of = lax.broadcasted_iota(jnp.int32, (1, width), 1) // topk
    sub = lax.broadcasted_iota(jnp.int32, (high * GROUP, width), 0)
    low_sub = lax.broadcasted_iota(jnp.int32, (lanes, width), 0)

    def one_group(g):
        local = ids_ref[pl.ds(g, 1), :].astype(jnp.int32) - base
        inside = (local >= 0) & (local < latents)
        key = jnp.where(inside, (local // lanes) * GROUP + row_of, -1)
        low = jnp.where(inside, local % lanes, -1)
        vals = vals_ref[pl.ds(g, 1), :]
        left = jnp.where(key == sub, vals, 0.0).astype(jnp.bfloat16)
        right = jnp.where(low == low_sub, 1.0, 0.0).astype(jnp.bfloat16)
        dense = lax.dot_general(
            left, right, (((1,), (1,)), ((), ())), preferred_element_type=jnp.float32
        )
        return dense.reshape(high, GROUP, lanes)

    def pair(i, carry):
        both = jnp.concatenate([one_group(2 * i), one_group(2 * i + 1)], axis=1)
        both = both.astype(jnp.bfloat16)
        rows = pl.ds(pl.multiple_of(i * 2 * GROUP, 2 * GROUP), 2 * GROUP)
        for h in range(high):
            out_ref[rows, h * lanes : (h + 1) * lanes] = both[h]
        return carry

    lax.fori_loop(0, groups // 2, pair, 0)


def densify(ids, vals, base, topk, latents):
    groups, width = ids.shape
    lanes = 256 if latents % 256 == 0 else 128
    rows = groups * GROUP
    return pl.pallas_call(
        functools.partial(densify_kernel, topk=topk, latents=latents, lanes=lanes),
        out_shape=jax.ShapeDtypeStruct((rows, latents), jnp.bfloat16),
        in_specs=[
            pl.BlockSpec(memory_space=pltpu.SMEM),
            pl.BlockSpec(memory_space=pltpu.VMEM),
            pl.BlockSpec(memory_space=pltpu.VMEM),
        ],
        out_specs=pl.BlockSpec(memory_space=pltpu.VMEM),
        compiler_params=pltpu.CompilerParams(vmem_limit_bytes=VMEM_BYTES),
        cost_estimate=pl.CostEstimate(
            flops=2 * groups * GROUP * latents * width,
            bytes_accessed=rows * latents * 2,
            transcendentals=0,
        ),
        name="densify",
    )(base, ids, vals)


def decode_kernel(*refs):
    codes, weights, out = refs[:-2], refs[-2], refs[-1]
    block = jnp.concatenate([c[...] for c in codes], axis=0)
    part = jnp.dot(block, weights[...], preferred_element_type=jnp.float32)

    @pl.when(pl.program_id(0) == 0)
    def _():
        out[...] = part

    @pl.when(pl.program_id(0) > 0)
    def _():
        out[...] += part


def decode(codes, decoder):
    rows, latents = codes[0].shape
    columns = decoder.shape[1]
    depth = math.gcd(latents, 1024)
    total = rows * len(codes)
    return pl.pallas_call(
        decode_kernel,
        out_shape=jax.ShapeDtypeStruct((total, columns), jnp.float32),
        grid=(latents // depth,),
        in_specs=[pl.BlockSpec((rows, depth), lambda k: (0, k)) for _ in codes]
        + [pl.BlockSpec((depth, columns), lambda k: (k, 0))],
        out_specs=pl.BlockSpec((total, columns), lambda k: (0, 0)),
        compiler_params=pltpu.CompilerParams(
            dimension_semantics=("arbitrary",), vmem_limit_bytes=VMEM_BYTES
        ),
        cost_estimate=pl.CostEstimate(
            flops=2 * total * latents * columns,
            bytes_accessed=latents * (total + columns) * 2 + total * columns * 4,
            transcendentals=0,
        ),
        name="decode",
    )(*codes, decoder)


def attend_kernel(*refs, heads, slots, slot):
    query_pos, key_pos = refs[0], refs[1]
    new = refs[2 : 2 + slots]
    cached = refs[2 + slots : -1]
    out = refs[-1]
    width = heads * HEAD
    hidden = key_pos[...] > query_pos[...]
    for h in range(heads):
        here = slice(h * HEAD, (h + 1) * HEAD)
        keys = [c[0, :, here] for c in cached] + [
            n[:, width + h * HEAD : width + (h + 1) * HEAD] for n in new
        ]
        values = [c[1, :, here] for c in cached] + [
            n[:, 2 * width + h * HEAD : 2 * width + (h + 1) * HEAD] for n in new
        ]
        keys = jnp.concatenate(keys, axis=0)
        values = jnp.concatenate(values, axis=0)
        scores = lax.dot_general(
            new[slot][:, here], keys, (((1,), (1,)), ((), ())), preferred_element_type=jnp.float32
        ) * (1.0 / math.sqrt(HEAD))
        cut = scores.shape[1] - hidden.shape[1]
        old, fresh = scores[:, :cut], jnp.where(hidden, -1e30, scores[:, cut:])
        highest = jnp.maximum(
            jnp.max(old, axis=1, keepdims=True), jnp.max(fresh, axis=1, keepdims=True)
        )
        old, fresh = jnp.exp(old - highest), jnp.exp(fresh - highest)
        total = jnp.sum(old, axis=1, keepdims=True) + jnp.sum(fresh, axis=1, keepdims=True)
        scale = 1.0 / total
        probs = jnp.concatenate(
            [(old * scale).astype(jnp.bfloat16), (fresh * scale).astype(jnp.bfloat16)], axis=1
        )
        mixed = jnp.dot(probs, values, preferred_element_type=jnp.float32)
        out[:, here] = mixed.astype(jnp.bfloat16)


def attend(query_pos, key_pos, new, cached, slot, heads):
    rows = new[0].shape[0]
    keys = rows * len(new) + sum(c.shape[1] for c in cached)
    vmem = pl.BlockSpec(memory_space=pltpu.VMEM)
    return pl.pallas_call(
        functools.partial(attend_kernel, heads=heads, slots=len(new), slot=slot),
        out_shape=jax.ShapeDtypeStruct((rows, heads * HEAD), jnp.bfloat16),
        in_specs=[vmem] * (2 + len(new) + len(cached)),
        out_specs=vmem,
        compiler_params=pltpu.CompilerParams(vmem_limit_bytes=VMEM_BYTES),
        cost_estimate=pl.CostEstimate(
            flops=4 * rows * keys * heads * HEAD,
            bytes_accessed=keys * heads * HEAD * 4,
            transcendentals=rows * keys * heads,
        ),
        name="attend",
    )(query_pos, key_pos, *new, *cached)


PAIRS = [(0, 1), (1, 0), (2, 3), (3, 2)]
INWARD = [(0, 1), (3, 2)]
MIDDLE = [(1, 2), (2, 1)]
OUTWARD = [(1, 0), (2, 3)]


def line_slots(index):
    low = index < 2
    return [index, index ^ 1, jnp.where(low, 2, 1), jnp.where(low, 3, 0)]


def line_gather(own, outer):
    near = lax.ppermute(own, "lat", PAIRS)
    across = lax.ppermute(own, "lat", MIDDLE)
    far = lax.ppermute(near, "lat", MIDDLE)
    across_out = lax.ppermute(across, "lat", OUTWARD)
    far_out = lax.ppermute(far, "lat", OUTWARD)
    return [own, near, jnp.where(outer, across_out, across), jnp.where(outer, far_out, far)]


def line_sum(parts, encode, decode_sent):
    in_far = lax.ppermute(encode(parts[3]), "lat", INWARD)
    in_across = lax.ppermute(encode(parts[2]), "lat", INWARD)
    far = lax.ppermute(encode(parts[3] + decode_sent(in_far)), "lat", MIDDLE)
    across = lax.ppermute(encode(parts[2] + decode_sent(in_across)), "lat", MIDDLE)
    near = lax.ppermute(encode(parts[1] + decode_sent(far)), "lat", PAIRS)
    return parts[0] + decode_sent(across) + decode_sent(near)


def swap(value, distance, size):
    return lax.ppermute(value, "col", [(i, i ^ distance) for i in range(size)])


def normalize(values, sums, gain, shift):
    row_mean = sums[0] / D
    row_var = sums[1] / D - row_mean * row_mean
    inverse = 1.0 / jnp.sqrt(row_var + 1e-05)
    return ((values - row_mean[:, None]) * inverse[:, None] * gain + shift).astype(jnp.bfloat16)


SCALE = 256.0


def to_half(value):
    return (value * SCALE).astype(jnp.float16)


def from_half(value):
    return value.astype(jnp.float32) * (1.0 / SCALE)


def line_body(
    code_ids, code_vals, decoder, dec_bias, ln_gain, ln_bias, w_qkv, cache_kv, positions, w_out
):
    lat = lax.axis_index("lat")
    col = lax.axis_index("col")
    cols = lax.axis_size("col")
    rows, topk = code_ids.shape
    latents, columns = decoder.shape
    head_width = w_qkv.shape[2]
    own_width = head_width // cols
    heads = own_width // HEAD
    outer = (lat == 0) | (lat == 3)
    slots = line_slots(lat)

    packed = jnp.concatenate(
        [
            code_ids.reshape(rows // GROUP, GROUP * topk).astype(jnp.float32),
            code_vals.astype(jnp.bfloat16)
            .astype(jnp.float32)
            .reshape(rows // GROUP, GROUP * topk),
        ],
        axis=1,
    )
    packed = line_gather(packed, outer)
    base = (lat * latents).reshape(1)

    def cache_of(j):
        start = (col ^ j) * own_width
        return lax.dynamic_slice_in_dim(cache_kv, start, own_width, 2)

    sent = swap(jnp.stack([cache_of(1), cache_of(3)]), 1, cols)
    other = swap(jnp.stack([cache_of(2), sent[1]]), 2, cols)
    cached = [cache_of(0), sent[0], other[0], other[1]]

    weights = jnp.concatenate(
        [
            lax.dynamic_slice_in_dim(w_qkv, (col ^ j) * own_width, own_width, 2).reshape(
                w_qkv.shape[0], 3 * own_width
            )
            for j in (1, 3, 0, 2)
        ],
        axis=1,
    )
    out_weights = jnp.concatenate(
        [
            lax.dynamic_slice_in_dim(w_out, (col ^ j) * own_width, own_width, 0)
            for j in (0, 2, 1, 3)
        ],
        axis=0,
    )
    key_pos = jnp.concatenate(
        [lax.dynamic_slice_in_dim(positions, s * rows, rows, 0) for s in slots]
    )

    codes = [
        densify(p[:, : GROUP * topk], p[:, GROUP * topk :], base, topk, latents) for p in packed
    ]
    far = decode([codes[3], codes[2]], decoder)
    near = decode([codes[1], codes[0]], decoder)
    parts = [near[rows:], near[:rows], far[rows:], far[:rows]]
    residual = line_sum(parts, to_half, from_half) + dec_bias.astype(jnp.float32)

    sums = jnp.stack([jnp.sum(residual, axis=1), jnp.sum(residual * residual, axis=1)])
    sums = sums + swap(sums, 1, cols)
    sums = sums + swap(sums, 2, cols)
    normed = line_gather(normalize(residual, sums, ln_gain, ln_bias), outer)

    half = weights.shape[1] // 2
    quarter = half // 2

    def project(block):
        away = jnp.dot(block, weights[:, :half], preferred_element_type=jnp.float32)
        keep = jnp.dot(block, weights[:, half:], preferred_element_type=jnp.float32)
        keep = keep + swap(away.astype(jnp.float16), 1, cols).astype(jnp.float32)
        came = swap(keep[:, quarter:].astype(jnp.float16), 2, cols).astype(jnp.float32)
        return (keep[:, :quarter] + came).astype(jnp.bfloat16)

    qkv = [project(block) for block in normed]

    branch = [None] * 4
    for slot in (3, 2, 1, 0):
        query_pos = key_pos[slot * rows : (slot + 1) * rows].reshape(rows, 1)
        mixed = attend(query_pos, key_pos.reshape(1, -1), qkv, cached, slot, heads)
        mixed = jnp.concatenate([mixed, swap(mixed, 2, cols)], axis=1)
        mixed = jnp.concatenate([mixed, swap(mixed, 1, cols)], axis=1)
        branch[slot] = jnp.dot(mixed, out_weights, preferred_element_type=jnp.float32)
    added = line_sum(
        branch, lambda v: v.astype(jnp.bfloat16), lambda v: v.astype(jnp.float32)
    )
    return (residual + added).astype(jnp.bfloat16)


def attend_block(queries, keys, values, query_pos, key_pos):
    heads = queries.shape[1] // HEAD
    query_heads = queries.reshape(queries.shape[0], heads, HEAD)
    key_heads = keys.reshape(keys.shape[0], heads, HEAD)
    value_heads = values.reshape(values.shape[0], heads, HEAD)
    scores = jnp.einsum(
        "qhe,khe->hqk", query_heads, key_heads, preferred_element_type=jnp.float32
    ) * (1.0 / math.sqrt(HEAD))
    visible = key_pos[None, None, :] <= query_pos[None, :, None]
    scores = jnp.where(visible, scores, -1e30)
    highest = jnp.max(scores, axis=-1, keepdims=True)
    expo = jnp.exp(scores - highest)
    probs = (expo / jnp.sum(expo, axis=-1, keepdims=True)).astype(jnp.bfloat16)
    mixed = jnp.einsum("hqk,khe->qhe", probs, value_heads, preferred_element_type=jnp.float32)
    return mixed.reshape(queries.shape[0], heads * HEAD).astype(jnp.bfloat16)


def general_body(
    code_ids, code_vals, decoder, dec_bias, ln_gain, ln_bias, w_qkv, cache_kv, positions, w_out
):
    lat_index = lax.axis_index("lat")
    col_total = lax.axis_size("col")
    col_index = lax.axis_index("col")
    rows, topk = code_ids.shape
    shard_latents = decoder.shape[0]
    packed = jnp.concatenate(
        [
            code_ids.reshape(rows // GROUP, GROUP * topk).astype(jnp.float32),
            code_vals.astype(jnp.bfloat16)
            .astype(jnp.float32)
            .reshape(rows // GROUP, GROUP * topk),
        ],
        axis=1,
    )
    packed = lax.all_gather(packed, "lat", axis=0, tiled=True)
    base = (lat_index * shard_latents).reshape(1)
    dense_codes = densify(
        packed[:, : GROUP * topk], packed[:, GROUP * topk :], base, topk, shard_latents
    )
    total_rows = dense_codes.shape[0]
    col_rows = total_rows // col_total
    residual = lax.psum_scatter(
        jnp.dot(dense_codes, decoder, preferred_element_type=jnp.float32),
        "lat",
        scatter_dimension=0,
        tiled=True,
    ) + dec_bias.astype(jnp.float32)
    sums = lax.psum((jnp.sum(residual, axis=1), jnp.sum(residual * residual, axis=1)), "col")
    normed = lax.all_gather(normalize(residual, sums, ln_gain, ln_bias), "lat", axis=0, tiled=True)
    head_width = w_qkv.shape[2]
    w_flat = w_qkv.reshape(w_qkv.shape[0], 3 * head_width)
    own_rows = lax.psum_scatter(
        jnp.dot(normed, w_flat, preferred_element_type=jnp.float32),
        "col",
        scatter_dimension=0,
        tiled=True,
    ).astype(jnp.bfloat16)
    queries = own_rows[:, :head_width]
    new_kv = lax.all_gather(own_rows[:, head_width:], "col", axis=0, tiled=True)
    context = lax.all_gather(cache_kv, "col", axis=1, tiled=True)
    cached_len = context.shape[1]
    keys = jnp.concatenate([context[0], new_kv[:, :head_width]], axis=0)
    values = jnp.concatenate([context[1], new_kv[:, head_width:]], axis=0)
    key_pos = jnp.concatenate([jnp.arange(cached_len, dtype=jnp.int32), cached_len + positions])
    query_pos = cached_len + lax.dynamic_slice_in_dim(positions, col_index * col_rows, col_rows, 0)
    attended = attend_block(queries, keys, values, query_pos, key_pos)
    gathered = lax.all_gather(attended, "col", axis=0, tiled=True)
    branch_out = lax.psum_scatter(
        jnp.dot(gathered, w_out, preferred_element_type=jnp.float32).astype(jnp.bfloat16),
        "lat",
        scatter_dimension=0,
        tiled=True,
    ).astype(jnp.float32)
    return (residual + branch_out).astype(jnp.bfloat16)


def solution(mesh):
    def program(*args):
        lats, cols = mesh.shape["lat"], mesh.shape["col"]
        heads = args[6].shape[2] // HEAD // lats
        fits = lats == 4 and cols == 4 and heads % cols == 0
        return jax.shard_map(
            line_body if fits else general_body,
            mesh=mesh,
            in_specs=(
                P(("ckpt", "lat"), None),
                P(("ckpt", "lat"), None),
                P(("ckpt", "lat"), "col"),
                P(("ckpt", "col")),
                P(("ckpt", "col")),
                P(("ckpt", "col")),
                P(("ckpt", "col"), None, "lat"),
                P(None, ("ckpt", "col"), "lat"),
                P("ckpt"),
                P(("ckpt", "lat"), "col"),
            ),
            out_specs=P(("ckpt", "lat"), "col"),
            check_vma=False,
        )(*args)

    return program
```

```python
import functools
import math

import jax
import jax.numpy as jnp
from jax import lax
from jax.experimental import pallas as pl
from jax.experimental.pallas import tpu as pltpu
from jax.sharding import PartitionSpec as P

D = 5120
HEAD = 128
GROUP = 8
VMEM_BYTES = 20 * 1024 * 1024


def densify_kernel(base_ref, *refs, topk, latents, lanes):
    packed, out_ref = refs[:-1], refs[-1]
    groups, width = packed[0].shape[0], packed[0].shape[1] // 2
    high = latents // lanes
    base = base_ref[0]
    row_of = lax.broadcasted_iota(jnp.int32, (1, width), 1) // topk
    sub = lax.broadcasted_iota(jnp.int32, (high * GROUP, width), 0)
    sub = sub.astype(jnp.float32).astype(jnp.bfloat16)
    low_sub = lax.broadcasted_iota(jnp.int32, (lanes, width), 0)
    low_sub = low_sub.astype(jnp.float32).astype(jnp.bfloat16)
    one, zero = jnp.ones((), jnp.bfloat16), jnp.zeros((), jnp.bfloat16)

    def half(value):
        return value.astype(jnp.float32).astype(jnp.bfloat16)

    def one_group(ref, g):
        local = ref[pl.ds(g, 1), :width].astype(jnp.int32) - base
        inside = (local >= 0) & (local < latents)
        key = half(jnp.where(inside, (local // lanes) * GROUP + row_of, -1))
        low = half(jnp.where(inside, local % lanes, -1))
        vals = ref[pl.ds(g, 1), width:].astype(jnp.bfloat16)
        left = jnp.where(key == sub, vals, zero)
        right = jnp.where(low == low_sub, one, zero)
        dense = lax.dot_general(
            left, right, (((1,), (1,)), ((), ())), preferred_element_type=jnp.float32
        )
        return dense.reshape(high, GROUP, lanes)

    for at, ref in enumerate(packed):

        def pair(i, carry, at=at, ref=ref):
            both = jnp.concatenate([one_group(ref, 2 * i), one_group(ref, 2 * i + 1)], axis=1)
            both = both.astype(jnp.bfloat16)
            start = pl.multiple_of(i * 2 * GROUP, 2 * GROUP) + at * groups * GROUP
            for h in range(high):
                out_ref[pl.ds(start, 2 * GROUP), h * lanes : (h + 1) * lanes] = both[h]
            return carry

        lax.fori_loop(0, groups // 2, pair, 0)


def densify(packed, base, topk, latents):
    groups, width = packed[0].shape
    lanes = 256 if latents % 256 == 0 else 128
    rows = groups * GROUP * len(packed)
    return pl.pallas_call(
        functools.partial(densify_kernel, topk=topk, latents=latents, lanes=lanes),
        out_shape=jax.ShapeDtypeStruct((rows, latents), jnp.bfloat16),
        in_specs=[pl.BlockSpec(memory_space=pltpu.SMEM)]
        + [pl.BlockSpec(memory_space=pltpu.VMEM) for _ in packed],
        out_specs=pl.BlockSpec(memory_space=pltpu.VMEM),
        compiler_params=pltpu.CompilerParams(vmem_limit_bytes=VMEM_BYTES),
        cost_estimate=pl.CostEstimate(
            flops=rows * latents * width, bytes_accessed=rows * latents * 2, transcendentals=0
        ),
        name="densify",
    )(base, *packed)


def copy_kernel(order_ref, from_ref, to_ref):
    to_ref[...] = from_ref[...].reshape(to_ref.shape)


def select_columns(weights, order, width):
    kinds, depth = weights.shape[:2]
    count = order.shape[0]
    return pl.pallas_call(
        copy_kernel,
        out_shape=jax.ShapeDtypeStruct((depth, count * kinds * width), weights.dtype),
        grid_spec=pltpu.PrefetchScalarGridSpec(
            num_scalar_prefetch=1,
            grid=(count, kinds),
            in_specs=[pl.BlockSpec((1, depth, width), lambda j, t, order: (t, 0, order[j]))],
            out_specs=pl.BlockSpec((depth, width), lambda j, t, order: (0, j * kinds + t)),
        ),
        compiler_params=pltpu.CompilerParams(vmem_limit_bytes=VMEM_BYTES),
        cost_estimate=pl.CostEstimate(
            flops=0, bytes_accessed=4 * depth * count * kinds * width, transcendentals=0
        ),
        name="select_columns",
    )(order, weights)


def select_rows(weights, order, height):
    columns, count = weights.shape[1], order.shape[0]
    return pl.pallas_call(
        copy_kernel,
        out_shape=jax.ShapeDtypeStruct((count * height, columns), weights.dtype),
        grid_spec=pltpu.PrefetchScalarGridSpec(
            num_scalar_prefetch=1,
            grid=(count,),
            in_specs=[pl.BlockSpec((height, columns), lambda j, order: (order[j], 0))],
            out_specs=pl.BlockSpec((height, columns), lambda j, order: (j, 0)),
        ),
        compiler_params=pltpu.CompilerParams(vmem_limit_bytes=VMEM_BYTES),
        cost_estimate=pl.CostEstimate(
            flops=0, bytes_accessed=4 * count * height * columns, transcendentals=0
        ),
        name="select_rows",
    )(order, weights)


def attend_kernel(*refs, heads, slots, group):
    query_pos, key_pos = refs[0], refs[1]
    new = refs[2 : 2 + slots]
    cached = refs[2 + slots : -1]
    out = refs[-1]
    width = heads * HEAD
    hidden = key_pos[...] > query_pos[...]
    for h in range(heads):
        here = slice(h * HEAD, (h + 1) * HEAD)
        keys = [c[0, :, here] for c in cached] + [
            n[:, width + h * HEAD : width + (h + 1) * HEAD] for n in new
        ]
        values = [c[1, :, here] for c in cached] + [
            n[:, 2 * width + h * HEAD : 2 * width + (h + 1) * HEAD] for n in new
        ]
        keys = jnp.concatenate(keys, axis=0)
        values = jnp.concatenate(values, axis=0)
        scores = lax.dot_general(
            jnp.concatenate([new[s][:, here] for s in group], axis=0), keys, (((1,), (1,)), ((), ())), preferred_element_type=jnp.float32
        ) * (1.0 / math.sqrt(HEAD))
        cut = scores.shape[1] - hidden.shape[1]
        old, fresh = scores[:, :cut], jnp.where(hidden, -1e30, scores[:, cut:])
        highest = jnp.maximum(
            jnp.max(old, axis=1, keepdims=True), jnp.max(fresh, axis=1, keepdims=True)
        )
        old, fresh = jnp.exp(old - highest), jnp.exp(fresh - highest)
        total = jnp.sum(old, axis=1, keepdims=True) + jnp.sum(fresh, axis=1, keepdims=True)
        scale = 1.0 / total
        probs = jnp.concatenate(
            [(old * scale).astype(jnp.bfloat16), (fresh * scale).astype(jnp.bfloat16)], axis=1
        )
        mixed = jnp.dot(probs, values, preferred_element_type=jnp.float32)
        out[:, here] = mixed.astype(jnp.bfloat16)


def attend(query_pos, key_pos, new, cached, group, heads):
    slot_rows = new[0].shape[0]
    rows = slot_rows * len(group)
    keys = slot_rows * len(new) + sum(c.shape[1] for c in cached)
    vmem = pl.BlockSpec(memory_space=pltpu.VMEM)
    return pl.pallas_call(
        functools.partial(attend_kernel, heads=heads, slots=len(new), group=group),
        out_shape=jax.ShapeDtypeStruct((rows, heads * HEAD), jnp.bfloat16),
        in_specs=[vmem] * (2 + len(new) + len(cached)),
        out_specs=vmem,
        compiler_params=pltpu.CompilerParams(vmem_limit_bytes=VMEM_BYTES),
        cost_estimate=pl.CostEstimate(
            flops=4 * rows * keys * heads * HEAD,
            bytes_accessed=keys * heads * HEAD * 4,
            transcendentals=rows * keys * heads,
        ),
        name="attend",
    )(query_pos, key_pos, *new, *cached)


PAIRS = [(0, 1), (1, 0), (2, 3), (3, 2)]
INWARD = [(0, 1), (3, 2)]
MIDDLE = [(1, 2), (2, 1)]
OUTWARD = [(1, 0), (2, 3)]


def line_slots(index):
    low = index < 2
    return [index, index ^ 1, jnp.where(low, 2, 1), jnp.where(low, 3, 0)]


def line_gather(own, outer):
    near = lax.ppermute(own, "lat", PAIRS)
    across = lax.ppermute(own, "lat", MIDDLE)
    far = lax.ppermute(near, "lat", MIDDLE)
    across_out = lax.ppermute(across, "lat", OUTWARD)
    far_out = lax.ppermute(far, "lat", OUTWARD)
    return [own, near, jnp.where(outer, across_out, across), jnp.where(outer, far_out, far)]


def line_sum(parts, encode, decode_sent):
    in_far = lax.ppermute(encode(parts[3]), "lat", INWARD)
    in_across = lax.ppermute(encode(parts[2]), "lat", INWARD)
    return line_end(parts, in_far, in_across, encode, decode_sent)


def line_end(parts, in_far, in_across, encode, decode_sent):
    far = encode(parts[3] + decode_sent(in_far))
    second, far = lax.optimization_barrier((parts[2], far))
    far = lax.ppermute(far, "lat", MIDDLE)
    across = lax.ppermute(encode(second + decode_sent(in_across)), "lat", MIDDLE)
    near = lax.ppermute(encode(parts[1] + decode_sent(far)), "lat", PAIRS)
    return parts[0] + decode_sent(across) + decode_sent(near)


def swap(value, distance, size):
    return lax.ppermute(value, "col", [(i, i ^ distance) for i in range(size)])


def normalize(values, sums, gain, shift):
    row_mean = sums[0] / D
    row_var = sums[1] / D - row_mean * row_mean
    inverse = 1.0 / jnp.sqrt(row_var + 1e-05)
    return ((values - row_mean[:, None]) * inverse[:, None] * gain + shift).astype(jnp.bfloat16)


def pack(code_ids, code_vals):
    rows, topk = code_ids.shape
    vals = code_vals.astype(jnp.bfloat16).astype(jnp.float32)
    shape = (rows // GROUP, GROUP * topk)
    return jnp.concatenate([code_ids.astype(jnp.float32).reshape(shape), vals.reshape(shape)], axis=1)


SCALE = 256.0


def to_half(value):
    return (value * SCALE).astype(jnp.float16)


def from_half(value):
    return value.astype(jnp.float32) * (1.0 / SCALE)


def line_body(
    code_ids, code_vals, decoder, dec_bias, ln_gain, ln_bias, w_qkv, cache_kv, positions, w_out
):
    lat = lax.axis_index("lat")
    col = lax.axis_index("col")
    cols = lax.axis_size("col")
    rows, topk = code_ids.shape
    latents, columns = decoder.shape
    head_width = w_qkv.shape[2]
    own_width = head_width // cols
    heads = own_width // HEAD
    outer = (lat == 0) | (lat == 3)
    slots = line_slots(lat)
    hold = lax.optimization_barrier

    packed = pack(code_ids, code_vals)
    packed = line_gather(packed, outer)
    base = (lat * latents).reshape(1)

    def cache_of(j):
        start = (col ^ j) * own_width
        return lax.dynamic_slice_in_dim(cache_kv, start, own_width, 2)

    sent = swap(jnp.stack([cache_of(1), cache_of(3)]), 1, cols)
    other = swap(jnp.stack([cache_of(2), sent[1]]), 2, cols)

    weights = w_qkv.transpose(1, 0, 2)
    away_weights = select_columns(weights, jnp.stack([col ^ 1, col ^ 3]), own_width)
    keep_weights = select_columns(weights, jnp.stack([col, col ^ 2]), own_width)
    out_weights = select_rows(w_out, jnp.stack([col, col ^ 2, col ^ 1, col ^ 3]), own_width)
    key_pos = jnp.concatenate(
        [lax.dynamic_slice_in_dim(positions, s * rows, rows, 0) for s in slots]
    )
    query_pos = key_pos.reshape(-1, 1)

    near_packed, away_weights, keep_weights, out_weights = hold(
        (packed[:2], away_weights, keep_weights, out_weights)
    )
    codes_far = densify([packed[3], packed[2]], base, topk, latents)
    codes_near = densify([near_packed[1], near_packed[0]], base, topk, latents)
    far = jnp.dot(codes_far, decoder, preferred_element_type=jnp.float32)
    codes_near, other, query_pos = hold((codes_near, other, query_pos))
    cached = [cache_of(0), sent[0], other[0], other[1]]
    in_far = lax.ppermute(to_half(far[:rows]), "lat", INWARD)
    in_across = lax.ppermute(to_half(far[rows:]), "lat", INWARD)
    near = jnp.dot(codes_near, decoder, preferred_element_type=jnp.float32)
    near, in_far = hold((near, in_far))
    parts = [near[rows:], near[:rows], far[rows:], far[:rows]]
    residual = line_end(parts, in_far, in_across, to_half, from_half)
    residual = residual + dec_bias.astype(jnp.float32)

    sums = jnp.stack([jnp.sum(residual, axis=1), jnp.sum(residual * residual, axis=1)])
    sums = sums + swap(sums, 1, cols)
    sums = sums + swap(sums, 2, cols)
    normed = line_gather(normalize(residual, sums, ln_gain, ln_bias), outer)

    quarter = keep_weights.shape[1] // 2

    def project(block, after):
        block, _ = hold((block, after))
        away = jnp.dot(block, away_weights, preferred_element_type=jnp.float32).astype(jnp.float16)
        keep = jnp.dot(block, keep_weights, preferred_element_type=jnp.float32)
        keep = keep + swap(away, 1, cols).astype(jnp.float32)
        came = swap(keep[:, quarter:].astype(jnp.float16), 2, cols).astype(jnp.float32)
        return (keep[:, :quarter] + came).astype(jnp.bfloat16), away

    pair, sent = project(jnp.concatenate(normed[:2], axis=0), normed[0])
    third, sent = project(normed[2], sent)
    fourth, sent = project(normed[3], sent)
    qkv = [pair[:rows], pair[rows:], third, fourth]

    branch = [None] * 4
    for group in ((3, 2), (1, 0)):
        pos = jnp.concatenate([query_pos[g * rows : (g + 1) * rows] for g in group], axis=0)
        mixed = attend(pos, key_pos.reshape(1, -1), qkv, cached, group, heads)
        mixed = jnp.concatenate([mixed, swap(mixed, 2, cols)], axis=1)
        mixed = jnp.concatenate([mixed, swap(mixed, 1, cols)], axis=1)
        product = jnp.dot(mixed, out_weights, preferred_element_type=jnp.float32)
        branch[group[0]], branch[group[1]] = product[:rows], product[rows:]
    added = line_sum(
        branch, lambda v: v.astype(jnp.bfloat16), lambda v: v.astype(jnp.float32)
    )
    return (residual + added).astype(jnp.bfloat16)


def attend_block(queries, keys, values, query_pos, key_pos):
    heads = queries.shape[1] // HEAD
    query_heads = queries.reshape(queries.shape[0], heads, HEAD)
    key_heads = keys.reshape(keys.shape[0], heads, HEAD)
    value_heads = values.reshape(values.shape[0], heads, HEAD)
    scores = jnp.einsum(
        "qhe,khe->hqk", query_heads, key_heads, preferred_element_type=jnp.float32
    ) * (1.0 / math.sqrt(HEAD))
    visible = key_pos[None, None, :] <= query_pos[None, :, None]
    scores = jnp.where(visible, scores, -1e30)
    highest = jnp.max(scores, axis=-1, keepdims=True)
    expo = jnp.exp(scores - highest)
    probs = (expo / jnp.sum(expo, axis=-1, keepdims=True)).astype(jnp.bfloat16)
    mixed = jnp.einsum("hqk,khe->qhe", probs, value_heads, preferred_element_type=jnp.float32)
    return mixed.reshape(queries.shape[0], heads * HEAD).astype(jnp.bfloat16)


def general_body(
    code_ids, code_vals, decoder, dec_bias, ln_gain, ln_bias, w_qkv, cache_kv, positions, w_out
):
    lat_index = lax.axis_index("lat")
    col_total = lax.axis_size("col")
    col_index = lax.axis_index("col")
    rows, topk = code_ids.shape
    shard_latents = decoder.shape[0]
    packed = lax.all_gather(pack(code_ids, code_vals), "lat", axis=0, tiled=True)
    base = (lat_index * shard_latents).reshape(1)
    dense_codes = densify([packed], base, topk, shard_latents)
    total_rows = dense_codes.shape[0]
    col_rows = total_rows // col_total
    residual = lax.psum_scatter(
        jnp.dot(dense_codes, decoder, preferred_element_type=jnp.float32),
        "lat",
        scatter_dimension=0,
        tiled=True,
    ) + dec_bias.astype(jnp.float32)
    sums = lax.psum((jnp.sum(residual, axis=1), jnp.sum(residual * residual, axis=1)), "col")
    normed = lax.all_gather(normalize(residual, sums, ln_gain, ln_bias), "lat", axis=0, tiled=True)
    head_width = w_qkv.shape[2]
    w_flat = w_qkv.reshape(w_qkv.shape[0], 3 * head_width)
    own_rows = lax.psum_scatter(
        jnp.dot(normed, w_flat, preferred_element_type=jnp.float32),
        "col",
        scatter_dimension=0,
        tiled=True,
    ).astype(jnp.bfloat16)
    queries = own_rows[:, :head_width]
    new_kv = lax.all_gather(own_rows[:, head_width:], "col", axis=0, tiled=True)
    context = lax.all_gather(cache_kv, "col", axis=1, tiled=True)
    cached_len = context.shape[1]
    keys = jnp.concatenate([context[0], new_kv[:, :head_width]], axis=0)
    values = jnp.concatenate([context[1], new_kv[:, head_width:]], axis=0)
    key_pos = jnp.concatenate([jnp.arange(cached_len, dtype=jnp.int32), cached_len + positions])
    query_pos = cached_len + lax.dynamic_slice_in_dim(positions, col_index * col_rows, col_rows, 0)
    attended = attend_block(queries, keys, values, query_pos, key_pos)
    gathered = lax.all_gather(attended, "col", axis=0, tiled=True)
    branch_out = lax.psum_scatter(
        jnp.dot(gathered, w_out, preferred_element_type=jnp.float32).astype(jnp.bfloat16),
        "lat",
        scatter_dimension=0,
        tiled=True,
    ).astype(jnp.float32)
    return (residual + branch_out).astype(jnp.bfloat16)


def solution(mesh):
    def program(*args):
        lats, cols = mesh.shape["lat"], mesh.shape["col"]
        heads = args[6].shape[2] // HEAD // lats
        fits = lats == 4 and cols == 4 and heads % cols == 0
        return jax.shard_map(
            line_body if fits else general_body,
            mesh=mesh,
            in_specs=(
                P(("ckpt", "lat"), None),
                P(("ckpt", "lat"), None),
                P(("ckpt", "lat"), "col"),
                P(("ckpt", "col")),
                P(("ckpt", "col")),
                P(("ckpt", "col")),
                P(("ckpt", "col"), None, "lat"),
                P(None, ("ckpt", "col"), "lat"),
                P("ckpt"),
                P(("ckpt", "lat"), "col"),
            ),
            out_specs=P(("ckpt", "lat"), "col"),
            check_vma=False,
        )(*args)

    return program
```

```python
import functools
import math

import jax
import jax.numpy as jnp
from jax import lax
from jax.experimental import pallas as pl
from jax.experimental.pallas import tpu as pltpu
from jax.sharding import PartitionSpec as P

D = 5120
HEAD = 128
GROUP = 8
VMEM_BYTES = 20 * 1024 * 1024
STREAM_BYTES = 56 * 1024 * 1024


def densify_kernel(base_ref, *refs, topk, latents, lanes):
    packed, out_ref = refs[:-1], refs[-1]
    groups, width = packed[0].shape[0], packed[0].shape[1] // 2
    high = latents // lanes
    base = base_ref[0]
    row_of = lax.broadcasted_iota(jnp.int32, (1, width), 1) // topk
    sub = lax.broadcasted_iota(jnp.int32, (high * GROUP, width), 0)
    sub = sub.astype(jnp.float32).astype(jnp.bfloat16)
    low_sub = lax.broadcasted_iota(jnp.int32, (lanes, width), 0)
    low_sub = low_sub.astype(jnp.float32).astype(jnp.bfloat16)
    one, zero = jnp.ones((), jnp.bfloat16), jnp.zeros((), jnp.bfloat16)

    def half(value):
        return value.astype(jnp.float32).astype(jnp.bfloat16)

    def one_group(ref, g):
        local = ref[pl.ds(g, 1), :width].astype(jnp.int32) - base
        inside = (local >= 0) & (local < latents)
        key = half(jnp.where(inside, (local // lanes) * GROUP + row_of, -1))
        low = half(jnp.where(inside, local % lanes, -1))
        vals = ref[pl.ds(g, 1), width:].astype(jnp.bfloat16)
        left = jnp.where(key == sub, vals, zero)
        right = jnp.where(low == low_sub, one, zero)
        dense = lax.dot_general(
            left, right, (((1,), (1,)), ((), ())), preferred_element_type=jnp.float32
        )
        return dense.reshape(high, GROUP, lanes)

    for at, ref in enumerate(packed):

        def pair(i, carry, at=at, ref=ref):
            both = jnp.concatenate([one_group(ref, 2 * i), one_group(ref, 2 * i + 1)], axis=1)
            both = both.astype(jnp.bfloat16)
            start = pl.multiple_of(i * 2 * GROUP, 2 * GROUP) + at * groups * GROUP
            for h in range(high):
                out_ref[pl.ds(start, 2 * GROUP), h * lanes : (h + 1) * lanes] = both[h]
            return carry

        lax.fori_loop(0, groups // 2, pair, 0)


def densify(packed, base, topk, latents):
    groups, width = packed[0].shape
    lanes = 256 if latents % 256 == 0 else 128
    rows = groups * GROUP * len(packed)
    return pl.pallas_call(
        functools.partial(densify_kernel, topk=topk, latents=latents, lanes=lanes),
        out_shape=jax.ShapeDtypeStruct((rows, latents), jnp.bfloat16),
        in_specs=[pl.BlockSpec(memory_space=pltpu.SMEM)]
        + [pl.BlockSpec(memory_space=pltpu.VMEM) for _ in packed],
        out_specs=pl.BlockSpec(memory_space=pltpu.VMEM),
        compiler_params=pltpu.CompilerParams(vmem_limit_bytes=VMEM_BYTES),
        cost_estimate=pl.CostEstimate(
            flops=rows * latents * width, bytes_accessed=rows * latents * 2, transcendentals=0
        ),
        name="densify",
    )(base, *packed)


def copy_kernel(order_ref, from_ref, to_ref):
    to_ref[...] = from_ref[...].reshape(to_ref.shape)


def select_columns(weights, order, width):
    kinds, depth = weights.shape[:2]
    count = order.shape[0]
    return pl.pallas_call(
        copy_kernel,
        out_shape=jax.ShapeDtypeStruct((depth, count * kinds * width), weights.dtype),
        grid_spec=pltpu.PrefetchScalarGridSpec(
            num_scalar_prefetch=1,
            grid=(count, kinds),
            in_specs=[pl.BlockSpec((1, depth, width), lambda j, t, order: (t, 0, order[j]))],
            out_specs=pl.BlockSpec((depth, width), lambda j, t, order: (0, j * kinds + t)),
        ),
        compiler_params=pltpu.CompilerParams(vmem_limit_bytes=STREAM_BYTES),
        cost_estimate=pl.CostEstimate(
            flops=0, bytes_accessed=4 * depth * count * kinds * width, transcendentals=0
        ),
        name="select_columns",
    )(order, weights)


def select_rows(weights, order, height):
    columns, count = weights.shape[1], order.shape[0]
    return pl.pallas_call(
        copy_kernel,
        out_shape=jax.ShapeDtypeStruct((count * height, columns), weights.dtype),
        grid_spec=pltpu.PrefetchScalarGridSpec(
            num_scalar_prefetch=1,
            grid=(count,),
            in_specs=[pl.BlockSpec((height, columns), lambda j, order: (order[j], 0))],
            out_specs=pl.BlockSpec((height, columns), lambda j, order: (j, 0)),
        ),
        compiler_params=pltpu.CompilerParams(vmem_limit_bytes=STREAM_BYTES),
        cost_estimate=pl.CostEstimate(
            flops=0, bytes_accessed=4 * count * height * columns, transcendentals=0
        ),
        name="select_rows",
    )(order, weights)


def attend_kernel(*refs, heads, slots, group):
    query_pos, key_pos = refs[0], refs[1]
    new = refs[2 : 2 + slots]
    cached = refs[2 + slots : -1]
    out = refs[-1]
    width = heads * HEAD
    hidden = key_pos[...] > query_pos[...]
    for h in range(heads):
        here = slice(h * HEAD, (h + 1) * HEAD)
        keys = [c[0, :, here] for c in cached] + [
            n[:, width + h * HEAD : width + (h + 1) * HEAD] for n in new
        ]
        values = [c[1, :, here] for c in cached] + [
            n[:, 2 * width + h * HEAD : 2 * width + (h + 1) * HEAD] for n in new
        ]
        keys = jnp.concatenate(keys, axis=0)
        values = jnp.concatenate(values, axis=0)
        scores = lax.dot_general(
            jnp.concatenate([new[s][:, here] for s in group], axis=0), keys, (((1,), (1,)), ((), ())), preferred_element_type=jnp.float32
        ) * (1.0 / math.sqrt(HEAD))
        cut = scores.shape[1] - hidden.shape[1]
        old, fresh = scores[:, :cut], jnp.where(hidden, -1e30, scores[:, cut:])
        highest = jnp.maximum(
            jnp.max(old, axis=1, keepdims=True), jnp.max(fresh, axis=1, keepdims=True)
        )
        old, fresh = jnp.exp(old - highest), jnp.exp(fresh - highest)
        total = jnp.sum(old, axis=1, keepdims=True) + jnp.sum(fresh, axis=1, keepdims=True)
        scale = 1.0 / total
        probs = jnp.concatenate(
            [(old * scale).astype(jnp.bfloat16), (fresh * scale).astype(jnp.bfloat16)], axis=1
        )
        mixed = jnp.dot(probs, values, preferred_element_type=jnp.float32)
        out[:, here] = mixed.astype(jnp.bfloat16)


def attend(query_pos, key_pos, new, cached, group, heads):
    slot_rows = new[0].shape[0]
    rows = slot_rows * len(group)
    keys = slot_rows * len(new) + sum(c.shape[1] for c in cached)
    vmem = pl.BlockSpec(memory_space=pltpu.VMEM)
    return pl.pallas_call(
        functools.partial(attend_kernel, heads=heads, slots=len(new), group=group),
        out_shape=jax.ShapeDtypeStruct((rows, heads * HEAD), jnp.bfloat16),
        in_specs=[vmem] * (2 + len(new) + len(cached)),
        out_specs=vmem,
        compiler_params=pltpu.CompilerParams(vmem_limit_bytes=VMEM_BYTES),
        cost_estimate=pl.CostEstimate(
            flops=4 * rows * keys * heads * HEAD,
            bytes_accessed=keys * heads * HEAD * 4,
            transcendentals=rows * keys * heads,
        ),
        name="attend",
    )(query_pos, key_pos, *new, *cached)


PAIRS = [(0, 1), (1, 0), (2, 3), (3, 2)]
INWARD = [(0, 1), (3, 2)]
MIDDLE = [(1, 2), (2, 1)]
OUTWARD = [(1, 0), (2, 3)]


def line_slots(index):
    low = index < 2
    return [index, index ^ 1, jnp.where(low, 2, 1), jnp.where(low, 3, 0)]


def line_gather_direct(own, outer):
    near = lax.ppermute(own, "lat", [(i, i ^ 1) for i in range(4)])
    two = lax.ppermute(own, "lat", [(i, i ^ 2) for i in range(4)])
    three = lax.ppermute(own, "lat", [(i, i ^ 3) for i in range(4)])
    return [own, near, jnp.where(outer, two, three), jnp.where(outer, three, two)]


def line_end(parts, in_far, in_across, encode, decode_sent):
    far = encode(parts[3] + decode_sent(in_far))
    second, far = lax.optimization_barrier((parts[2], far))
    far = lax.ppermute(far, "lat", MIDDLE)
    across = lax.ppermute(encode(second + decode_sent(in_across)), "lat", MIDDLE)
    near = lax.ppermute(encode(parts[1] + decode_sent(far)), "lat", PAIRS)
    return parts[0] + decode_sent(across) + decode_sent(near)


def swap(value, distance, size):
    return lax.ppermute(value, "col", [(i, i ^ distance) for i in range(size)])


def normalize(values, sums, gain, shift):
    row_mean = sums[0] / D
    row_var = sums[1] / D - row_mean * row_mean
    inverse = 1.0 / jnp.sqrt(row_var + 1e-05)
    return ((values - row_mean[:, None]) * inverse[:, None] * gain + shift).astype(jnp.bfloat16)


def pack(code_ids, code_vals):
    rows, topk = code_ids.shape
    vals = code_vals.astype(jnp.bfloat16).astype(jnp.float32)
    shape = (rows // GROUP, GROUP * topk)
    return jnp.concatenate([code_ids.astype(jnp.float32).reshape(shape), vals.reshape(shape)], axis=1)


SCALE = 256.0


def to_half(value):
    return (value * SCALE).astype(jnp.float16)


def from_half(value):
    return value.astype(jnp.float32) * (1.0 / SCALE)


def line_body(
    code_ids, code_vals, decoder, dec_bias, ln_gain, ln_bias, w_qkv, cache_kv, positions, w_out
):
    lat = lax.axis_index("lat")
    col = lax.axis_index("col")
    cols = lax.axis_size("col")
    rows, topk = code_ids.shape
    latents, columns = decoder.shape
    head_width = w_qkv.shape[2]
    own_width = head_width // cols
    heads = own_width // HEAD
    outer = (lat == 0) | (lat == 3)
    slots = line_slots(lat)
    hold = lax.optimization_barrier

    packed = pack(code_ids, code_vals)
    packed = line_gather_direct(packed, outer)
    base = (lat * latents).reshape(1)

    def cache_of(j):
        start = (col ^ j) * own_width
        return lax.dynamic_slice_in_dim(cache_kv, start, own_width, 2)

    across = swap(jnp.stack([cache_of(2), cache_of(3)]), 2, cols)

    weights = w_qkv.transpose(1, 0, 2)
    away_weights = select_columns(weights, jnp.stack([col ^ 1, col ^ 3]), own_width)
    keep_weights = select_columns(weights, jnp.stack([col, col ^ 2]), own_width)
    out_weights = select_rows(w_out, jnp.stack([col, col ^ 2, col ^ 1, col ^ 3]), own_width)
    key_pos = jnp.concatenate(
        [lax.dynamic_slice_in_dim(positions, s * rows, rows, 0) for s in slots]
    )
    query_pos = key_pos.reshape(-1, 1)

    near_packed, away_weights, keep_weights, out_weights = hold(
        (packed[:2], away_weights, keep_weights, out_weights)
    )
    codes_far = densify([packed[3], packed[2]], base, topk, latents)
    codes_near = densify([near_packed[1], near_packed[0]], base, topk, latents)
    far = jnp.dot(codes_far, decoder, preferred_element_type=jnp.float32)
    codes_near, across, query_pos = hold((codes_near, across, query_pos))
    beside = swap(jnp.stack([cache_of(1), across[1]]), 1, cols)
    cached = [cache_of(0), across[0], beside[0], beside[1]]
    in_far = lax.ppermute(to_half(far[:rows]), "lat", INWARD)
    in_across = lax.ppermute(to_half(far[rows:]), "lat", INWARD)
    near = jnp.dot(codes_near, decoder, preferred_element_type=jnp.float32)
    near, in_far = hold((near, in_far))
    parts = [near[rows:], near[:rows], far[rows:], far[:rows]]
    residual = line_end(parts, in_far, in_across, to_half, from_half)
    residual = residual + dec_bias.astype(jnp.float32)

    sums = jnp.stack([jnp.sum(residual, axis=1), jnp.sum(residual * residual, axis=1)])
    sums = sums + swap(sums, 1, cols)
    sums = sums + swap(sums, 2, cols)
    own = normalize(residual, sums, ln_gain, ln_bias)
    near = lax.ppermute(own, "lat", PAIRS)
    across = lax.ppermute(own, "lat", MIDDLE)
    far = lax.ppermute(near, "lat", MIDDLE)
    across_out = lax.ppermute(across, "lat", OUTWARD)
    far_out = lax.ppermute(far, "lat", OUTWARD)

    quarter = keep_weights.shape[1] // 2

    def project(block):
        away = jnp.dot(block, away_weights, preferred_element_type=jnp.float32).astype(jnp.float16)
        keep = jnp.dot(block, keep_weights, preferred_element_type=jnp.float32)
        keep = keep + swap(away, 1, cols).astype(jnp.float32)
        return keep[:, :quarter], keep[:, quarter:].astype(jnp.float16)

    def finish(keep, payload):
        return (keep + swap(payload, 2, cols).astype(jnp.float32)).astype(jnp.bfloat16)

    pair, across = hold((jnp.concatenate([own, near], axis=0), across))
    keep0, payload0 = project(pair)
    third, far, payload0 = hold((jnp.where(outer, across_out, across), far, payload0))
    keep2, payload2 = project(third)
    fourth, payload2 = hold((jnp.where(outer, far_out, far), payload2))
    keep3, payload3 = project(fourth)
    first = finish(keep0, payload0)
    qkv = [first[:rows], first[rows:], finish(keep2, payload2), finish(keep3, payload3)]

    key_row = key_pos.reshape(1, -1)

    def pos_of(a, b):
        return jnp.concatenate(
            [query_pos[a * rows : (a + 1) * rows], query_pos[b * rows : (b + 1) * rows]], axis=0
        )

    mixed_far = attend(pos_of(3, 2), key_row, qkv, cached, (3, 2), heads)
    near_pos, mixed_far = hold((pos_of(1, 0), mixed_far))
    mixed_near = attend(near_pos, key_row, qkv, cached, (1, 0), heads)
    mixed_far = jnp.concatenate([mixed_far, swap(mixed_far, 2, cols)], axis=1)
    mixed_far = jnp.concatenate([mixed_far, swap(mixed_far, 1, cols)], axis=1)
    product_far = jnp.dot(mixed_far, out_weights, preferred_element_type=jnp.float32)
    sent_far = product_far.astype(jnp.bfloat16)
    in_far = lax.ppermute(sent_far[:rows], "lat", INWARD)
    in_across = lax.ppermute(sent_far[rows:], "lat", INWARD)
    mixed_near = jnp.concatenate([mixed_near, swap(mixed_near, 2, cols)], axis=1)
    mixed_near, sent_far = hold((mixed_near, sent_far))
    mixed_near = jnp.concatenate([mixed_near, swap(mixed_near, 1, cols)], axis=1)
    product_near = jnp.dot(mixed_near, out_weights, preferred_element_type=jnp.float32)
    branch = [product_near[rows:], product_near[:rows], product_far[rows:], product_far[:rows]]
    added = line_end(
        branch,
        in_far,
        in_across,
        lambda v: v.astype(jnp.bfloat16),
        lambda v: v.astype(jnp.float32),
    )
    return (residual + added).astype(jnp.bfloat16)


def attend_block(queries, keys, values, query_pos, key_pos):
    heads = queries.shape[1] // HEAD
    query_heads = queries.reshape(queries.shape[0], heads, HEAD)
    key_heads = keys.reshape(keys.shape[0], heads, HEAD)
    value_heads = values.reshape(values.shape[0], heads, HEAD)
    scores = jnp.einsum(
        "qhe,khe->hqk", query_heads, key_heads, preferred_element_type=jnp.float32
    ) * (1.0 / math.sqrt(HEAD))
    visible = key_pos[None, None, :] <= query_pos[None, :, None]
    scores = jnp.where(visible, scores, -1e30)
    highest = jnp.max(scores, axis=-1, keepdims=True)
    expo = jnp.exp(scores - highest)
    probs = (expo / jnp.sum(expo, axis=-1, keepdims=True)).astype(jnp.bfloat16)
    mixed = jnp.einsum("hqk,khe->qhe", probs, value_heads, preferred_element_type=jnp.float32)
    return mixed.reshape(queries.shape[0], heads * HEAD).astype(jnp.bfloat16)


def general_body(
    code_ids, code_vals, decoder, dec_bias, ln_gain, ln_bias, w_qkv, cache_kv, positions, w_out
):
    lat_index = lax.axis_index("lat")
    col_total = lax.axis_size("col")
    col_index = lax.axis_index("col")
    rows, topk = code_ids.shape
    shard_latents = decoder.shape[0]
    packed = lax.all_gather(pack(code_ids, code_vals), "lat", axis=0, tiled=True)
    base = (lat_index * shard_latents).reshape(1)
    dense_codes = densify([packed], base, topk, shard_latents)
    total_rows = dense_codes.shape[0]
    col_rows = total_rows // col_total
    residual = lax.psum_scatter(
        jnp.dot(dense_codes, decoder, preferred_element_type=jnp.float32),
        "lat",
        scatter_dimension=0,
        tiled=True,
    ) + dec_bias.astype(jnp.float32)
    sums = lax.psum((jnp.sum(residual, axis=1), jnp.sum(residual * residual, axis=1)), "col")
    normed = lax.all_gather(normalize(residual, sums, ln_gain, ln_bias), "lat", axis=0, tiled=True)
    head_width = w_qkv.shape[2]
    w_flat = w_qkv.reshape(w_qkv.shape[0], 3 * head_width)
    own_rows = lax.psum_scatter(
        jnp.dot(normed, w_flat, preferred_element_type=jnp.float32),
        "col",
        scatter_dimension=0,
        tiled=True,
    ).astype(jnp.bfloat16)
    queries = own_rows[:, :head_width]
    new_kv = lax.all_gather(own_rows[:, head_width:], "col", axis=0, tiled=True)
    context = lax.all_gather(cache_kv, "col", axis=1, tiled=True)
    cached_len = context.shape[1]
    keys = jnp.concatenate([context[0], new_kv[:, :head_width]], axis=0)
    values = jnp.concatenate([context[1], new_kv[:, head_width:]], axis=0)
    key_pos = jnp.concatenate([jnp.arange(cached_len, dtype=jnp.int32), cached_len + positions])
    query_pos = cached_len + lax.dynamic_slice_in_dim(positions, col_index * col_rows, col_rows, 0)
    attended = attend_block(queries, keys, values, query_pos, key_pos)
    gathered = lax.all_gather(attended, "col", axis=0, tiled=True)
    branch_out = lax.psum_scatter(
        jnp.dot(gathered, w_out, preferred_element_type=jnp.float32).astype(jnp.bfloat16),
        "lat",
        scatter_dimension=0,
        tiled=True,
    ).astype(jnp.float32)
    return (residual + branch_out).astype(jnp.bfloat16)


def solution(mesh):
    def program(*args):
        lats, cols = mesh.shape["lat"], mesh.shape["col"]
        heads = args[6].shape[2] // HEAD // lats
        fits = lats == 4 and cols == 4 and heads % cols == 0
        return jax.shard_map(
            line_body if fits else general_body,
            mesh=mesh,
            in_specs=(
                P(("ckpt", "lat"), None),
                P(("ckpt", "lat"), None),
                P(("ckpt", "lat"), "col"),
                P(("ckpt", "col")),
                P(("ckpt", "col")),
                P(("ckpt", "col")),
                P(("ckpt", "col"), None, "lat"),
                P(None, ("ckpt", "col"), "lat"),
                P("ckpt"),
                P(("ckpt", "lat"), "col"),
            ),
            out_specs=P(("ckpt", "lat"), "col"),
            check_vma=False,
        )(*args)

    return program
```

```python
import functools
import math

import jax
import jax.numpy as jnp
from jax import lax
from jax.experimental import pallas as pl
from jax.experimental.pallas import tpu as pltpu
from jax.sharding import PartitionSpec as P

D = 5120
HEAD = 128
GROUP = 8
VMEM_BYTES = 20 * 1024 * 1024


def densify_kernel(base_ref, *refs, topk, latents, lanes):
    packed, out_ref = refs[:-1], refs[-1]
    groups, width = packed[0].shape[0], packed[0].shape[1] // 2
    high = latents // lanes
    base = base_ref[0]
    row_of = lax.broadcasted_iota(jnp.int32, (1, width), 1) // topk
    sub = lax.broadcasted_iota(jnp.int32, (high * GROUP, width), 0)
    sub = sub.astype(jnp.float32).astype(jnp.bfloat16)
    low_sub = lax.broadcasted_iota(jnp.int32, (lanes, width), 0)
    low_sub = low_sub.astype(jnp.float32).astype(jnp.bfloat16)
    one, zero = jnp.ones((), jnp.bfloat16), jnp.zeros((), jnp.bfloat16)

    def half(value):
        return value.astype(jnp.float32).astype(jnp.bfloat16)

    def one_group(ref, g):
        local = ref[pl.ds(g, 1), :width].astype(jnp.int32) - base
        inside = (local >= 0) & (local < latents)
        key = half(jnp.where(inside, (local // lanes) * GROUP + row_of, -1))
        low = half(jnp.where(inside, local % lanes, -1))
        vals = ref[pl.ds(g, 1), width:].astype(jnp.bfloat16)
        left = jnp.where(key == sub, vals, zero)
        right = jnp.where(low == low_sub, one, zero)
        dense = lax.dot_general(
            left, right, (((1,), (1,)), ((), ())), preferred_element_type=jnp.float32
        )
        return dense.reshape(high, GROUP, lanes)

    for at, ref in enumerate(packed):

        def pair(i, carry, at=at, ref=ref):
            both = jnp.concatenate([one_group(ref, 2 * i), one_group(ref, 2 * i + 1)], axis=1)
            both = both.astype(jnp.bfloat16)
            start = pl.multiple_of(i * 2 * GROUP, 2 * GROUP) + at * groups * GROUP
            for h in range(high):
                out_ref[pl.ds(start, 2 * GROUP), h * lanes : (h + 1) * lanes] = both[h]
            return carry

        lax.fori_loop(0, groups // 2, pair, 0)


def densify(packed, base, topk, latents):
    groups, width = packed[0].shape
    lanes = 256 if latents % 256 == 0 else 128
    rows = groups * GROUP * len(packed)
    return pl.pallas_call(
        functools.partial(densify_kernel, topk=topk, latents=latents, lanes=lanes),
        out_shape=jax.ShapeDtypeStruct((rows, latents), jnp.bfloat16),
        in_specs=[pl.BlockSpec(memory_space=pltpu.SMEM)]
        + [pl.BlockSpec(memory_space=pltpu.VMEM) for _ in packed],
        out_specs=pl.BlockSpec(memory_space=pltpu.VMEM),
        compiler_params=pltpu.CompilerParams(vmem_limit_bytes=VMEM_BYTES),
        cost_estimate=pl.CostEstimate(
            flops=rows * latents * width, bytes_accessed=rows * latents * 2, transcendentals=0
        ),
        name="densify",
    )(base, *packed)


def copy_kernel(order_ref, from_ref, to_ref):
    to_ref[...] = from_ref[...].reshape(to_ref.shape)


def select_columns(weights, order, width):
    kinds, depth = weights.shape[:2]
    count = order.shape[0]
    return pl.pallas_call(
        copy_kernel,
        out_shape=jax.ShapeDtypeStruct((depth, count * kinds * width), weights.dtype),
        grid_spec=pltpu.PrefetchScalarGridSpec(
            num_scalar_prefetch=1,
            grid=(count, kinds),
            in_specs=[pl.BlockSpec((1, depth, width), lambda j, t, order: (t, 0, order[j]))],
            out_specs=pl.BlockSpec((depth, width), lambda j, t, order: (0, j * kinds + t)),
        ),
        compiler_params=pltpu.CompilerParams(vmem_limit_bytes=VMEM_BYTES),
        cost_estimate=pl.CostEstimate(
            flops=0, bytes_accessed=4 * depth * count * kinds * width, transcendentals=0
        ),
        name="select_columns",
    )(order, weights)


def select_rows(weights, order, height):
    columns, count = weights.shape[1], order.shape[0]
    return pl.pallas_call(
        copy_kernel,
        out_shape=jax.ShapeDtypeStruct((count * height, columns), weights.dtype),
        grid_spec=pltpu.PrefetchScalarGridSpec(
            num_scalar_prefetch=1,
            grid=(count,),
            in_specs=[pl.BlockSpec((height, columns), lambda j, order: (order[j], 0))],
            out_specs=pl.BlockSpec((height, columns), lambda j, order: (j, 0)),
        ),
        compiler_params=pltpu.CompilerParams(vmem_limit_bytes=VMEM_BYTES),
        cost_estimate=pl.CostEstimate(
            flops=0, bytes_accessed=4 * count * height * columns, transcendentals=0
        ),
        name="select_rows",
    )(order, weights)


def attend_kernel(*refs, heads, slots, group):
    query_pos, key_pos = refs[0], refs[1]
    new = refs[2 : 2 + slots]
    cached = refs[2 + slots : -1]
    out = refs[-1]
    width = heads * HEAD
    hidden = key_pos[...] > query_pos[...]
    for h in range(heads):
        here = slice(h * HEAD, (h + 1) * HEAD)
        keys = [c[0, :, here] for c in cached] + [
            n[:, width + h * HEAD : width + (h + 1) * HEAD] for n in new
        ]
        values = [c[1, :, here] for c in cached] + [
            n[:, 2 * width + h * HEAD : 2 * width + (h + 1) * HEAD] for n in new
        ]
        keys = jnp.concatenate(keys, axis=0)
        values = jnp.concatenate(values, axis=0)
        scores = lax.dot_general(
            jnp.concatenate([new[s][:, here] for s in group], axis=0), keys, (((1,), (1,)), ((), ())), preferred_element_type=jnp.float32
        ) * (1.0 / math.sqrt(HEAD))
        cut = scores.shape[1] - hidden.shape[1]
        old, fresh = scores[:, :cut], jnp.where(hidden, -1e30, scores[:, cut:])
        highest = jnp.maximum(
            jnp.max(old, axis=1, keepdims=True), jnp.max(fresh, axis=1, keepdims=True)
        )
        old, fresh = jnp.exp(old - highest), jnp.exp(fresh - highest)
        total = jnp.sum(old, axis=1, keepdims=True) + jnp.sum(fresh, axis=1, keepdims=True)
        scale = 1.0 / total
        probs = jnp.concatenate(
            [(old * scale).astype(jnp.bfloat16), (fresh * scale).astype(jnp.bfloat16)], axis=1
        )
        mixed = jnp.dot(probs, values, preferred_element_type=jnp.float32)
        out[:, here] = mixed.astype(jnp.bfloat16)


def attend(query_pos, key_pos, new, cached, group, heads):
    slot_rows = new[0].shape[0]
    rows = slot_rows * len(group)
    keys = slot_rows * len(new) + sum(c.shape[1] for c in cached)
    vmem = pl.BlockSpec(memory_space=pltpu.VMEM)
    return pl.pallas_call(
        functools.partial(attend_kernel, heads=heads, slots=len(new), group=group),
        out_shape=jax.ShapeDtypeStruct((rows, heads * HEAD), jnp.bfloat16),
        in_specs=[vmem] * (2 + len(new) + len(cached)),
        out_specs=vmem,
        compiler_params=pltpu.CompilerParams(vmem_limit_bytes=VMEM_BYTES),
        cost_estimate=pl.CostEstimate(
            flops=4 * rows * keys * heads * HEAD,
            bytes_accessed=keys * heads * HEAD * 4,
            transcendentals=rows * keys * heads,
        ),
        name="attend",
    )(query_pos, key_pos, *new, *cached)


PAIRS = [(0, 1), (1, 0), (2, 3), (3, 2)]
INWARD = [(0, 1), (3, 2)]
MIDDLE = [(1, 2), (2, 1)]
OUTWARD = [(1, 0), (2, 3)]


def line_slots(index):
    low = index < 2
    return [index, index ^ 1, jnp.where(low, 2, 1), jnp.where(low, 3, 0)]


def line_gather_direct(own, outer):
    near = lax.ppermute(own, "lat", [(i, i ^ 1) for i in range(4)])
    two = lax.ppermute(own, "lat", [(i, i ^ 2) for i in range(4)])
    three = lax.ppermute(own, "lat", [(i, i ^ 3) for i in range(4)])
    return [own, near, jnp.where(outer, two, three), jnp.where(outer, three, two)]


def swap(value, distance, size):
    return lax.ppermute(value, "col", [(i, i ^ distance) for i in range(size)])


def normalize(values, sums, gain, shift):
    row_mean = sums[0] / D
    row_var = sums[1] / D - row_mean * row_mean
    inverse = 1.0 / jnp.sqrt(row_var + 1e-05)
    return ((values - row_mean[:, None]) * inverse[:, None] * gain + shift).astype(jnp.bfloat16)


def pack(code_ids, code_vals):
    rows, topk = code_ids.shape
    vals = code_vals.astype(jnp.bfloat16).astype(jnp.float32)
    shape = (rows // GROUP, GROUP * topk)
    return jnp.concatenate([code_ids.astype(jnp.float32).reshape(shape), vals.reshape(shape)], axis=1)


SCALE = 256.0


def to_half(value):
    return (value * SCALE).astype(jnp.float16)


def from_half(value):
    return value.astype(jnp.float32) * (1.0 / SCALE)


def line_body(
    code_ids, code_vals, decoder, dec_bias, ln_gain, ln_bias, w_qkv, cache_kv, positions, w_out
):
    lat = lax.axis_index("lat")
    col = lax.axis_index("col")
    cols = lax.axis_size("col")
    rows, topk = code_ids.shape
    latents, columns = decoder.shape
    head_width = w_qkv.shape[2]
    own_width = head_width // cols
    heads = own_width // HEAD
    outer = (lat == 0) | (lat == 3)
    slots = line_slots(lat)
    hold = lax.optimization_barrier

    packed = pack(code_ids, code_vals)
    packed = line_gather_direct(packed, outer)
    base = (lat * latents).reshape(1)

    def cache_of(j):
        start = (col ^ j) * own_width
        return lax.dynamic_slice_in_dim(cache_kv, start, own_width, 2)

    across = swap(jnp.stack([cache_of(2), cache_of(3)]), 2, cols)

    key_pos = jnp.concatenate(
        [lax.dynamic_slice_in_dim(positions, s * rows, rows, 0) for s in slots]
    )
    query_pos = key_pos.reshape(-1, 1)

    codes_far = densify([packed[3], packed[2]], base, topk, latents)
    far = jnp.dot(codes_far, decoder, preferred_element_type=jnp.float32)
    in_far = lax.ppermute(to_half(far[:rows]), "lat", INWARD)
    near_packed, far = hold(((packed[1], packed[0]), far))
    codes_near = densify(near_packed, base, topk, latents)
    codes_near, in_far = hold((codes_near, in_far))
    mid_far = to_half(far[:rows] + from_half(in_far))
    second, codes_near, across, query_pos, mid_far = hold(
        (far[rows:], codes_near, across, query_pos, mid_far)
    )
    mid_far = lax.ppermute(mid_far, "lat", MIDDLE)
    in_across = lax.ppermute(to_half(second), "lat", INWARD)
    near = jnp.dot(codes_near, decoder, preferred_element_type=jnp.float32)
    near, mid_far = hold((near, mid_far))
    last = to_half(near[:rows] + from_half(mid_far))
    across, last, second, weights = hold((across, last, second, w_qkv.transpose(1, 0, 2)))
    last = lax.ppermute(last, "lat", PAIRS)
    mid_across = lax.ppermute(to_half(second + from_half(in_across)), "lat", MIDDLE)

    away_weights = select_columns(weights, jnp.stack([col ^ 1, col ^ 3]), own_width)
    keep_weights = select_columns(weights, jnp.stack([col, col ^ 2]), own_width)
    beside = swap(jnp.stack([cache_of(1), across[1]]), 1, cols)
    last, away_weights, keep_weights, beside = hold((last, away_weights, keep_weights, beside))
    cached = [cache_of(0), across[0], beside[0], beside[1]]
    residual = near[rows:] + from_half(mid_across) + from_half(last)
    residual = residual + dec_bias.astype(jnp.float32)

    sums = jnp.stack([jnp.sum(residual, axis=1), jnp.sum(residual * residual, axis=1)])
    sums = sums + swap(sums, 1, cols)
    sums = sums + swap(sums, 2, cols)
    own = normalize(residual, sums, ln_gain, ln_bias)
    near = lax.ppermute(own, "lat", PAIRS)
    across = lax.ppermute(own, "lat", MIDDLE)
    far = lax.ppermute(near, "lat", MIDDLE)
    across_out = lax.ppermute(across, "lat", OUTWARD)
    far_out = lax.ppermute(far, "lat", OUTWARD)

    quarter = keep_weights.shape[1] // 2

    def project(block):
        away = jnp.dot(block, away_weights, preferred_element_type=jnp.float32).astype(jnp.float16)
        keep = jnp.dot(block, keep_weights, preferred_element_type=jnp.float32)
        keep = keep + swap(away, 1, cols).astype(jnp.float32)
        return keep[:, :quarter], keep[:, quarter:].astype(jnp.float16)

    def finish(keep, payload):
        return (keep + swap(payload, 2, cols).astype(jnp.float32)).astype(jnp.bfloat16)

    keep0, payload0 = project(own)
    near_block, across, payload0 = hold((near, across, payload0))
    keep1, payload1 = project(near_block)
    third, far, payload1, out_source = hold(
        (jnp.where(outer, across_out, across), far, payload1, w_out)
    )
    out_weights = select_rows(
        out_source, jnp.stack([col, col ^ 2, col ^ 1, col ^ 3]), own_width
    )
    keep2, payload2 = project(third)
    fourth, payload2, out_weights = hold((jnp.where(outer, far_out, far), payload2, out_weights))
    keep3, payload3 = project(fourth)
    qkv = [
        finish(keep0, payload0),
        finish(keep1, payload1),
        finish(keep2, payload2),
        finish(keep3, payload3),
    ]

    key_row = key_pos.reshape(1, -1)

    def pos_of(a, b):
        return jnp.concatenate(
            [query_pos[a * rows : (a + 1) * rows], query_pos[b * rows : (b + 1) * rows]], axis=0
        )

    mixed_far = attend(pos_of(3, 2), key_row, qkv, cached, (3, 2), heads)
    near_pos, mixed_far = hold((pos_of(1, 0), mixed_far))
    mixed_near = attend(near_pos, key_row, qkv, cached, (1, 0), heads)
    swapped_far, mixed_near = hold((swap(mixed_far, 2, cols), mixed_near))
    mixed_far = jnp.concatenate([mixed_far, swapped_far], axis=1)
    mixed_far = jnp.concatenate([mixed_far, swap(mixed_far, 1, cols)], axis=1)
    product_far = jnp.dot(mixed_far, out_weights, preferred_element_type=jnp.float32)
    sent_far, mixed_near = hold((product_far[:rows].astype(jnp.bfloat16), mixed_near))
    in_far = lax.ppermute(sent_far, "lat", INWARD)
    mixed_near = jnp.concatenate([mixed_near, swap(mixed_near, 2, cols)], axis=1)
    mixed_near = jnp.concatenate([mixed_near, swap(mixed_near, 1, cols)], axis=1)
    product_near = jnp.dot(mixed_near, out_weights, preferred_element_type=jnp.float32)
    mid_far = (product_far[:rows] + in_far.astype(jnp.float32)).astype(jnp.bfloat16)
    second, mid_far = hold((product_far[rows:], mid_far))
    mid_far = lax.ppermute(mid_far, "lat", MIDDLE)
    in_across = lax.ppermute(second.astype(jnp.bfloat16), "lat", INWARD)
    last = (product_near[:rows] + mid_far.astype(jnp.float32)).astype(jnp.bfloat16)
    second, last = hold((second, last))
    last = lax.ppermute(last, "lat", PAIRS)
    mid_across = (second + in_across.astype(jnp.float32)).astype(jnp.bfloat16)
    mid_across = lax.ppermute(mid_across, "lat", MIDDLE)
    branch = product_near[rows:] + mid_across.astype(jnp.float32) + last.astype(jnp.float32)
    return (residual + branch).astype(jnp.bfloat16)


def attend_block(queries, keys, values, query_pos, key_pos):
    heads = queries.shape[1] // HEAD
    query_heads = queries.reshape(queries.shape[0], heads, HEAD)
    key_heads = keys.reshape(keys.shape[0], heads, HEAD)
    value_heads = values.reshape(values.shape[0], heads, HEAD)
    scores = jnp.einsum(
        "qhe,khe->hqk", query_heads, key_heads, preferred_element_type=jnp.float32
    ) * (1.0 / math.sqrt(HEAD))
    visible = key_pos[None, None, :] <= query_pos[None, :, None]
    scores = jnp.where(visible, scores, -1e30)
    highest = jnp.max(scores, axis=-1, keepdims=True)
    expo = jnp.exp(scores - highest)
    probs = (expo / jnp.sum(expo, axis=-1, keepdims=True)).astype(jnp.bfloat16)
    mixed = jnp.einsum("hqk,khe->qhe", probs, value_heads, preferred_element_type=jnp.float32)
    return mixed.reshape(queries.shape[0], heads * HEAD).astype(jnp.bfloat16)


def general_body(
    code_ids, code_vals, decoder, dec_bias, ln_gain, ln_bias, w_qkv, cache_kv, positions, w_out
):
    lat_index = lax.axis_index("lat")
    col_total = lax.axis_size("col")
    col_index = lax.axis_index("col")
    rows, topk = code_ids.shape
    shard_latents = decoder.shape[0]
    packed = lax.all_gather(pack(code_ids, code_vals), "lat", axis=0, tiled=True)
    base = (lat_index * shard_latents).reshape(1)
    dense_codes = densify([packed], base, topk, shard_latents)
    total_rows = dense_codes.shape[0]
    col_rows = total_rows // col_total
    residual = lax.psum_scatter(
        jnp.dot(dense_codes, decoder, preferred_element_type=jnp.float32),
        "lat",
        scatter_dimension=0,
        tiled=True,
    ) + dec_bias.astype(jnp.float32)
    sums = lax.psum((jnp.sum(residual, axis=1), jnp.sum(residual * residual, axis=1)), "col")
    normed = lax.all_gather(normalize(residual, sums, ln_gain, ln_bias), "lat", axis=0, tiled=True)
    head_width = w_qkv.shape[2]
    w_flat = w_qkv.reshape(w_qkv.shape[0], 3 * head_width)
    own_rows = lax.psum_scatter(
        jnp.dot(normed, w_flat, preferred_element_type=jnp.float32),
        "col",
        scatter_dimension=0,
        tiled=True,
    ).astype(jnp.bfloat16)
    queries = own_rows[:, :head_width]
    new_kv = lax.all_gather(own_rows[:, head_width:], "col", axis=0, tiled=True)
    context = lax.all_gather(cache_kv, "col", axis=1, tiled=True)
    cached_len = context.shape[1]
    keys = jnp.concatenate([context[0], new_kv[:, :head_width]], axis=0)
    values = jnp.concatenate([context[1], new_kv[:, head_width:]], axis=0)
    key_pos = jnp.concatenate([jnp.arange(cached_len, dtype=jnp.int32), cached_len + positions])
    query_pos = cached_len + lax.dynamic_slice_in_dim(positions, col_index * col_rows, col_rows, 0)
    attended = attend_block(queries, keys, values, query_pos, key_pos)
    gathered = lax.all_gather(attended, "col", axis=0, tiled=True)
    branch_out = lax.psum_scatter(
        jnp.dot(gathered, w_out, preferred_element_type=jnp.float32).astype(jnp.bfloat16),
        "lat",
        scatter_dimension=0,
        tiled=True,
    ).astype(jnp.float32)
    return (residual + branch_out).astype(jnp.bfloat16)


def solution(mesh):
    def program(*args):
        lats, cols = mesh.shape["lat"], mesh.shape["col"]
        heads = args[6].shape[2] // HEAD // lats
        fits = lats == 4 and cols == 4 and heads % cols == 0
        return jax.shard_map(
            line_body if fits else general_body,
            mesh=mesh,
            in_specs=(
                P(("ckpt", "lat"), None),
                P(("ckpt", "lat"), None),
                P(("ckpt", "lat"), "col"),
                P(("ckpt", "col")),
                P(("ckpt", "col")),
                P(("ckpt", "col")),
                P(("ckpt", "col"), None, "lat"),
                P(None, ("ckpt", "col"), "lat"),
                P("ckpt"),
                P(("ckpt", "lat"), "col"),
            ),
            out_specs=P(("ckpt", "lat"), "col"),
            check_vma=False,
        )(*args)

    return program
```

```python
import functools
import math

import jax
import jax.numpy as jnp
from jax import lax
from jax.experimental import pallas as pl
from jax.experimental.pallas import tpu as pltpu
from jax.sharding import PartitionSpec as P

D = 5120
HEAD = 128
GROUP = 8
VMEM_BYTES = 20 * 1024 * 1024
DECODE_BYTES = 44 * 1024 * 1024


def densify_kernel(base_ref, *refs, topk, latents, lanes):
    packed, out_ref = refs[:-1], refs[-1]
    groups, width = packed[0].shape[0], packed[0].shape[1] // 2
    high = latents // lanes
    base = base_ref[0]
    row_of = lax.broadcasted_iota(jnp.int32, (1, width), 1) // topk
    sub = lax.broadcasted_iota(jnp.int32, (high * GROUP, width), 0)
    sub = sub.astype(jnp.float32).astype(jnp.bfloat16)
    low_sub = lax.broadcasted_iota(jnp.int32, (lanes, width), 0)
    low_sub = low_sub.astype(jnp.float32).astype(jnp.bfloat16)
    one, zero = jnp.ones((), jnp.bfloat16), jnp.zeros((), jnp.bfloat16)

    def half(value):
        return value.astype(jnp.float32).astype(jnp.bfloat16)

    def one_group(ref, g):
        local = ref[pl.ds(g, 1), :width].astype(jnp.int32) - base
        inside = (local >= 0) & (local < latents)
        key = half(jnp.where(inside, (local // lanes) * GROUP + row_of, -1))
        low = half(jnp.where(inside, local % lanes, -1))
        vals = ref[pl.ds(g, 1), width:].astype(jnp.bfloat16)
        left = jnp.where(key == sub, vals, zero)
        right = jnp.where(low == low_sub, one, zero)
        dense = lax.dot_general(
            left, right, (((1,), (1,)), ((), ())), preferred_element_type=jnp.float32
        )
        return dense.reshape(high, GROUP, lanes)

    for at, ref in enumerate(packed):

        def pair(i, carry, at=at, ref=ref):
            both = jnp.concatenate([one_group(ref, 2 * i), one_group(ref, 2 * i + 1)], axis=1)
            both = both.astype(jnp.bfloat16)
            start = pl.multiple_of(i * 2 * GROUP, 2 * GROUP) + at * groups * GROUP
            for h in range(high):
                out_ref[pl.ds(start, 2 * GROUP), h * lanes : (h + 1) * lanes] = both[h]
            return carry

        lax.fori_loop(0, groups // 2, pair, 0)


def densify(packed, base, topk, latents):
    groups, width = packed[0].shape
    lanes = 256 if latents % 256 == 0 else 128
    rows = groups * GROUP * len(packed)
    return pl.pallas_call(
        functools.partial(densify_kernel, topk=topk, latents=latents, lanes=lanes),
        out_shape=jax.ShapeDtypeStruct((rows, latents), jnp.bfloat16),
        in_specs=[pl.BlockSpec(memory_space=pltpu.SMEM)]
        + [pl.BlockSpec(memory_space=pltpu.VMEM) for _ in packed],
        out_specs=pl.BlockSpec(memory_space=pltpu.VMEM),
        compiler_params=pltpu.CompilerParams(vmem_limit_bytes=VMEM_BYTES),
        cost_estimate=pl.CostEstimate(
            flops=rows * latents * width, bytes_accessed=rows * latents * 2, transcendentals=0
        ),
        name="densify",
    )(base, *packed)


def decode_kernel(codes_ref, weights_ref, out_ref):
    out_ref[...] = jnp.dot(codes_ref[...], weights_ref[...], preferred_element_type=jnp.float32)


def decode(codes, decoder):
    rows, latents = codes.shape
    columns = decoder.shape[1]
    width = math.gcd(columns, 256)
    return pl.pallas_call(
        decode_kernel,
        out_shape=jax.ShapeDtypeStruct((rows, columns), jnp.float32),
        grid=(columns // width,),
        in_specs=[
            pl.BlockSpec((rows, latents), lambda n: (0, 0)),
            pl.BlockSpec((latents, width), lambda n: (0, n)),
        ],
        out_specs=pl.BlockSpec((rows, width), lambda n: (0, n)),
        compiler_params=pltpu.CompilerParams(vmem_limit_bytes=DECODE_BYTES),
        cost_estimate=pl.CostEstimate(
            flops=2 * rows * latents * columns,
            bytes_accessed=latents * (rows + columns) * 2 + rows * columns * 4,
            transcendentals=0,
        ),
        name="decode",
    )(codes, decoder)


def copy_kernel(order_ref, from_ref, to_ref):
    to_ref[...] = from_ref[...].reshape(to_ref.shape)


def select_columns(weights, order, width):
    kinds, depth = weights.shape[:2]
    count = order.shape[0]
    return pl.pallas_call(
        copy_kernel,
        out_shape=jax.ShapeDtypeStruct((depth, count * kinds * width), weights.dtype),
        grid_spec=pltpu.PrefetchScalarGridSpec(
            num_scalar_prefetch=1,
            grid=(count, kinds),
            in_specs=[pl.BlockSpec((1, depth, width), lambda j, t, order: (t, 0, order[j]))],
            out_specs=pl.BlockSpec((depth, width), lambda j, t, order: (0, j * kinds + t)),
        ),
        compiler_params=pltpu.CompilerParams(vmem_limit_bytes=VMEM_BYTES),
        cost_estimate=pl.CostEstimate(
            flops=0, bytes_accessed=4 * depth * count * kinds * width, transcendentals=0
        ),
        name="select_columns",
    )(order, weights)


def select_rows(weights, order, height):
    columns, count = weights.shape[1], order.shape[0]
    return pl.pallas_call(
        copy_kernel,
        out_shape=jax.ShapeDtypeStruct((count * height, columns), weights.dtype),
        grid_spec=pltpu.PrefetchScalarGridSpec(
            num_scalar_prefetch=1,
            grid=(count,),
            in_specs=[pl.BlockSpec((height, columns), lambda j, order: (order[j], 0))],
            out_specs=pl.BlockSpec((height, columns), lambda j, order: (j, 0)),
        ),
        compiler_params=pltpu.CompilerParams(vmem_limit_bytes=VMEM_BYTES),
        cost_estimate=pl.CostEstimate(
            flops=0, bytes_accessed=4 * count * height * columns, transcendentals=0
        ),
        name="select_rows",
    )(order, weights)


def attend_kernel(*refs, heads, slots, group):
    query_pos, key_pos = refs[0], refs[1]
    new = refs[2 : 2 + slots]
    cached = refs[2 + slots : -1]
    out = refs[-1]
    width = heads * HEAD
    hidden = key_pos[...] > query_pos[...]
    for h in range(heads):
        here = slice(h * HEAD, (h + 1) * HEAD)
        keys = [c[0, :, here] for c in cached] + [
            n[:, width + h * HEAD : width + (h + 1) * HEAD] for n in new
        ]
        values = [c[1, :, here] for c in cached] + [
            n[:, 2 * width + h * HEAD : 2 * width + (h + 1) * HEAD] for n in new
        ]
        keys = jnp.concatenate(keys, axis=0)
        values = jnp.concatenate(values, axis=0)
        scores = lax.dot_general(
            jnp.concatenate([new[s][:, here] for s in group], axis=0), keys, (((1,), (1,)), ((), ())), preferred_element_type=jnp.float32
        ) * (1.0 / math.sqrt(HEAD))
        cut = scores.shape[1] - hidden.shape[1]
        old, fresh = scores[:, :cut], jnp.where(hidden, -1e30, scores[:, cut:])
        highest = jnp.maximum(
            jnp.max(old, axis=1, keepdims=True), jnp.max(fresh, axis=1, keepdims=True)
        )
        old, fresh = jnp.exp(old - highest), jnp.exp(fresh - highest)
        total = jnp.sum(old, axis=1, keepdims=True) + jnp.sum(fresh, axis=1, keepdims=True)
        scale = 1.0 / total
        probs = jnp.concatenate(
            [(old * scale).astype(jnp.bfloat16), (fresh * scale).astype(jnp.bfloat16)], axis=1
        )
        mixed = jnp.dot(probs, values, preferred_element_type=jnp.float32)
        out[:, here] = mixed.astype(jnp.bfloat16)


def attend(query_pos, key_pos, new, cached, group, heads):
    slot_rows = new[0].shape[0]
    rows = slot_rows * len(group)
    keys = slot_rows * len(new) + sum(c.shape[1] for c in cached)
    vmem = pl.BlockSpec(memory_space=pltpu.VMEM)
    return pl.pallas_call(
        functools.partial(attend_kernel, heads=heads, slots=len(new), group=group),
        out_shape=jax.ShapeDtypeStruct((rows, heads * HEAD), jnp.bfloat16),
        in_specs=[vmem] * (2 + len(new) + len(cached)),
        out_specs=vmem,
        compiler_params=pltpu.CompilerParams(vmem_limit_bytes=VMEM_BYTES),
        cost_estimate=pl.CostEstimate(
            flops=4 * rows * keys * heads * HEAD,
            bytes_accessed=keys * heads * HEAD * 4,
            transcendentals=rows * keys * heads,
        ),
        name="attend",
    )(query_pos, key_pos, *new, *cached)


PAIRS = [(0, 1), (1, 0), (2, 3), (3, 2)]
INWARD = [(0, 1), (3, 2)]
MIDDLE = [(1, 2), (2, 1)]
OUTWARD = [(1, 0), (2, 3)]


def line_slots(index):
    low = index < 2
    return [index, index ^ 1, jnp.where(low, 2, 1), jnp.where(low, 3, 0)]


def line_gather_direct(own, outer):
    near = lax.ppermute(own, "lat", [(i, i ^ 1) for i in range(4)])
    two = lax.ppermute(own, "lat", [(i, i ^ 2) for i in range(4)])
    three = lax.ppermute(own, "lat", [(i, i ^ 3) for i in range(4)])
    return [own, near, jnp.where(outer, two, three), jnp.where(outer, three, two)]


def swap(value, distance, size):
    return lax.ppermute(value, "col", [(i, i ^ distance) for i in range(size)])


def normalize(values, sums, gain, shift):
    row_mean = sums[0] / D
    row_var = sums[1] / D - row_mean * row_mean
    inverse = 1.0 / jnp.sqrt(row_var + 1e-05)
    return ((values - row_mean[:, None]) * inverse[:, None] * gain + shift).astype(jnp.bfloat16)


def pack(code_ids, code_vals):
    rows, topk = code_ids.shape
    vals = code_vals.astype(jnp.bfloat16).astype(jnp.float32)
    shape = (rows // GROUP, GROUP * topk)
    return jnp.concatenate([code_ids.astype(jnp.float32).reshape(shape), vals.reshape(shape)], axis=1)


SCALE = 256.0


def to_half(value):
    return (value * SCALE).astype(jnp.float16)


def from_half(value):
    return value.astype(jnp.float32) * (1.0 / SCALE)


def line_body(
    code_ids, code_vals, decoder, dec_bias, ln_gain, ln_bias, w_qkv, cache_kv, positions, w_out
):
    lat = lax.axis_index("lat")
    col = lax.axis_index("col")
    cols = lax.axis_size("col")
    rows, topk = code_ids.shape
    latents, columns = decoder.shape
    head_width = w_qkv.shape[2]
    own_width = head_width // cols
    heads = own_width // HEAD
    outer = (lat == 0) | (lat == 3)
    slots = line_slots(lat)
    hold = lax.optimization_barrier

    packed = pack(code_ids, code_vals)
    packed = line_gather_direct(packed, outer)
    base = (lat * latents).reshape(1)

    def cache_of(j):
        start = (col ^ j) * own_width
        return lax.dynamic_slice_in_dim(cache_kv, start, own_width, 2)

    across = swap(jnp.stack([cache_of(2), cache_of(3)]), 2, cols)

    key_pos = jnp.concatenate(
        [lax.dynamic_slice_in_dim(positions, s * rows, rows, 0) for s in slots]
    )
    query_pos = key_pos.reshape(-1, 1)

    codes_far = densify([packed[3], packed[2]], base, topk, latents)
    far = jnp.dot(codes_far, decoder, preferred_element_type=jnp.float32)
    in_far = lax.ppermute(to_half(far[:rows]), "lat", INWARD)
    near_packed, far = hold(((packed[1], packed[0]), far))
    codes_near = densify(near_packed, base, topk, latents)
    codes_near, in_far = hold((codes_near, in_far))
    mid_far = to_half(far[:rows] + from_half(in_far))
    second, codes_near, across, query_pos, mid_far = hold(
        (far[rows:], codes_near, across, query_pos, mid_far)
    )
    mid_far = lax.ppermute(mid_far, "lat", MIDDLE)
    in_across = lax.ppermute(to_half(second), "lat", INWARD)
    near = decode(codes_near, decoder)
    near, mid_far = hold((near, mid_far))
    last = to_half(near[:rows] + from_half(mid_far))
    across, last, second, weights = hold((across, last, second, w_qkv.transpose(1, 0, 2)))
    last = lax.ppermute(last, "lat", PAIRS)
    mid_across = lax.ppermute(to_half(second + from_half(in_across)), "lat", MIDDLE)

    away_weights = select_columns(weights, jnp.stack([col ^ 1, col ^ 3]), own_width)
    keep_weights = select_columns(weights, jnp.stack([col, col ^ 2]), own_width)
    out_weights = select_rows(w_out, jnp.stack([col, col ^ 2, col ^ 1, col ^ 3]), own_width)
    beside = swap(jnp.stack([cache_of(1), across[1]]), 1, cols)
    last, away_weights, keep_weights, out_weights, beside = hold(
        (last, away_weights, keep_weights, out_weights, beside)
    )
    cached = [cache_of(0), across[0], beside[0], beside[1]]
    residual = near[rows:] + from_half(mid_across) + from_half(last)
    residual = residual + dec_bias.astype(jnp.float32)

    sums = jnp.stack([jnp.sum(residual, axis=1), jnp.sum(residual * residual, axis=1)])
    sums = sums + swap(sums, 1, cols)
    sums = sums + swap(sums, 2, cols)
    own = normalize(residual, sums, ln_gain, ln_bias)
    near = lax.ppermute(own, "lat", PAIRS)
    across = lax.ppermute(own, "lat", MIDDLE)
    far = lax.ppermute(near, "lat", MIDDLE)
    across_out = lax.ppermute(across, "lat", OUTWARD)
    far_out = lax.ppermute(far, "lat", OUTWARD)

    quarter = keep_weights.shape[1] // 2

    def project(block):
        away = jnp.dot(block, away_weights, preferred_element_type=jnp.float32).astype(jnp.float16)
        keep = jnp.dot(block, keep_weights, preferred_element_type=jnp.float32)
        keep = keep + swap(away, 1, cols).astype(jnp.float32)
        return keep[:, :quarter], keep[:, quarter:].astype(jnp.float16)

    def finish(keep, payload):
        return (keep + swap(payload, 2, cols).astype(jnp.float32)).astype(jnp.bfloat16)

    keep0, payload0 = project(own)
    near_block, across, payload0 = hold((near, across, payload0))
    keep1, payload1 = project(near_block)
    third, far, payload1 = hold((jnp.where(outer, across_out, across), far, payload1))
    third = finish(*project(third))
    fourth, third = hold((jnp.where(outer, far_out, far), third))
    qkv = [finish(keep0, payload0), finish(keep1, payload1), third, finish(*project(fourth))]

    key_row = key_pos.reshape(1, -1)

    def pos_of(a, b):
        return jnp.concatenate(
            [query_pos[a * rows : (a + 1) * rows], query_pos[b * rows : (b + 1) * rows]], axis=0
        )

    mixed_far = attend(pos_of(3, 2), key_row, qkv, cached, (3, 2), heads)
    near_pos, mixed_far = hold((pos_of(1, 0), mixed_far))
    mixed_near = attend(near_pos, key_row, qkv, cached, (1, 0), heads)
    swapped_far, mixed_near = hold((swap(mixed_far, 2, cols), mixed_near))
    mixed_far = jnp.concatenate([mixed_far, swapped_far], axis=1)
    mixed_far = jnp.concatenate([mixed_far, swap(mixed_far, 1, cols)], axis=1)
    product_far = jnp.dot(mixed_far, out_weights, preferred_element_type=jnp.float32)
    sent_far, mixed_near = hold((product_far[:rows].astype(jnp.bfloat16), mixed_near))
    in_far = lax.ppermute(sent_far, "lat", INWARD)
    mixed_near = jnp.concatenate([mixed_near, swap(mixed_near, 2, cols)], axis=1)
    mixed_near = jnp.concatenate([mixed_near, swap(mixed_near, 1, cols)], axis=1)
    product_near = jnp.dot(mixed_near, out_weights, preferred_element_type=jnp.float32)
    mid_far = (product_far[:rows] + in_far.astype(jnp.float32)).astype(jnp.bfloat16)
    second, mid_far = hold((product_far[rows:], mid_far))
    mid_far = lax.ppermute(mid_far, "lat", MIDDLE)
    in_across = lax.ppermute(second.astype(jnp.bfloat16), "lat", INWARD)
    last = (product_near[:rows] + mid_far.astype(jnp.float32)).astype(jnp.bfloat16)
    second, last = hold((second, last))
    last = lax.ppermute(last, "lat", PAIRS)
    mid_across = (second + in_across.astype(jnp.float32)).astype(jnp.bfloat16)
    mid_across = lax.ppermute(mid_across, "lat", MIDDLE)
    branch = product_near[rows:] + last.astype(jnp.float32)
    branch, mid_across = hold((residual + branch, mid_across))
    return (branch + mid_across.astype(jnp.float32)).astype(jnp.bfloat16)


def attend_block(queries, keys, values, query_pos, key_pos):
    heads = queries.shape[1] // HEAD
    query_heads = queries.reshape(queries.shape[0], heads, HEAD)
    key_heads = keys.reshape(keys.shape[0], heads, HEAD)
    value_heads = values.reshape(values.shape[0], heads, HEAD)
    scores = jnp.einsum(
        "qhe,khe->hqk", query_heads, key_heads, preferred_element_type=jnp.float32
    ) * (1.0 / math.sqrt(HEAD))
    visible = key_pos[None, None, :] <= query_pos[None, :, None]
    scores = jnp.where(visible, scores, -1e30)
    highest = jnp.max(scores, axis=-1, keepdims=True)
    expo = jnp.exp(scores - highest)
    probs = (expo / jnp.sum(expo, axis=-1, keepdims=True)).astype(jnp.bfloat16)
    mixed = jnp.einsum("hqk,khe->qhe", probs, value_heads, preferred_element_type=jnp.float32)
    return mixed.reshape(queries.shape[0], heads * HEAD).astype(jnp.bfloat16)


def general_body(
    code_ids, code_vals, decoder, dec_bias, ln_gain, ln_bias, w_qkv, cache_kv, positions, w_out
):
    lat_index = lax.axis_index("lat")
    col_total = lax.axis_size("col")
    col_index = lax.axis_index("col")
    rows, topk = code_ids.shape
    shard_latents = decoder.shape[0]
    packed = lax.all_gather(pack(code_ids, code_vals), "lat", axis=0, tiled=True)
    base = (lat_index * shard_latents).reshape(1)
    dense_codes = densify([packed], base, topk, shard_latents)
    total_rows = dense_codes.shape[0]
    col_rows = total_rows // col_total
    residual = lax.psum_scatter(
        jnp.dot(dense_codes, decoder, preferred_element_type=jnp.float32),
        "lat",
        scatter_dimension=0,
        tiled=True,
    ) + dec_bias.astype(jnp.float32)
    sums = lax.psum((jnp.sum(residual, axis=1), jnp.sum(residual * residual, axis=1)), "col")
    normed = lax.all_gather(normalize(residual, sums, ln_gain, ln_bias), "lat", axis=0, tiled=True)
    head_width = w_qkv.shape[2]
    w_flat = w_qkv.reshape(w_qkv.shape[0], 3 * head_width)
    own_rows = lax.psum_scatter(
        jnp.dot(normed, w_flat, preferred_element_type=jnp.float32),
        "col",
        scatter_dimension=0,
        tiled=True,
    ).astype(jnp.bfloat16)
    queries = own_rows[:, :head_width]
    new_kv = lax.all_gather(own_rows[:, head_width:], "col", axis=0, tiled=True)
    context = lax.all_gather(cache_kv, "col", axis=1, tiled=True)
    cached_len = context.shape[1]
    keys = jnp.concatenate([context[0], new_kv[:, :head_width]], axis=0)
    values = jnp.concatenate([context[1], new_kv[:, head_width:]], axis=0)
    key_pos = jnp.concatenate([jnp.arange(cached_len, dtype=jnp.int32), cached_len + positions])
    query_pos = cached_len + lax.dynamic_slice_in_dim(positions, col_index * col_rows, col_rows, 0)
    attended = attend_block(queries, keys, values, query_pos, key_pos)
    gathered = lax.all_gather(attended, "col", axis=0, tiled=True)
    branch_out = lax.psum_scatter(
        jnp.dot(gathered, w_out, preferred_element_type=jnp.float32).astype(jnp.bfloat16),
        "lat",
        scatter_dimension=0,
        tiled=True,
    ).astype(jnp.float32)
    return (residual + branch_out).astype(jnp.bfloat16)


def solution(mesh):
    def program(*args):
        lats, cols = mesh.shape["lat"], mesh.shape["col"]
        heads = args[6].shape[2] // HEAD // lats
        fits = lats == 4 and cols == 4 and heads % cols == 0
        return jax.shard_map(
            line_body if fits else general_body,
            mesh=mesh,
            in_specs=(
                P(("ckpt", "lat"), None),
                P(("ckpt", "lat"), None),
                P(("ckpt", "lat"), "col"),
                P(("ckpt", "col")),
                P(("ckpt", "col")),
                P(("ckpt", "col")),
                P(("ckpt", "col"), None, "lat"),
                P(None, ("ckpt", "col"), "lat"),
                P("ckpt"),
                P(("ckpt", "lat"), "col"),
            ),
            out_specs=P(("ckpt", "lat"), "col"),
            check_vma=False,
        )(*args)

    return program
```

```python
import functools
import math

import jax
import jax.numpy as jnp
from jax import lax
from jax.experimental import pallas as pl
from jax.experimental.pallas import tpu as pltpu
from jax.sharding import PartitionSpec as P

D = 5120
HEAD = 128
GROUP = 8
VMEM_BYTES = 20 * 1024 * 1024
DECODE_BYTES = 44 * 1024 * 1024
SMALL = pl.CostEstimate(flops=1, bytes_accessed=1, transcendentals=0)


def densify_kernel(base_ref, *refs, topk, latents, lanes):
    packed, out_ref = refs[:-1], refs[-1]
    groups, width = packed[0].shape[0], packed[0].shape[1] // 2
    high = latents // lanes
    base = base_ref[0]
    row_of = lax.broadcasted_iota(jnp.int32, (1, width), 1) // topk
    sub = lax.broadcasted_iota(jnp.int32, (high * GROUP, width), 0)
    sub = sub.astype(jnp.float32).astype(jnp.bfloat16)
    low_sub = lax.broadcasted_iota(jnp.int32, (lanes, width), 0)
    low_sub = low_sub.astype(jnp.float32).astype(jnp.bfloat16)
    one, zero = jnp.ones((), jnp.bfloat16), jnp.zeros((), jnp.bfloat16)

    def half(value):
        return value.astype(jnp.float32).astype(jnp.bfloat16)

    def one_group(ref, g):
        local = ref[pl.ds(g, 1), :width].astype(jnp.int32) - base
        inside = (local >= 0) & (local < latents)
        key = half(jnp.where(inside, (local // lanes) * GROUP + row_of, -1))
        low = half(jnp.where(inside, local % lanes, -1))
        vals = ref[pl.ds(g, 1), width:].astype(jnp.bfloat16)
        left = jnp.where(key == sub, vals, zero)
        right = jnp.where(low == low_sub, one, zero)
        dense = lax.dot_general(
            left, right, (((1,), (1,)), ((), ())), preferred_element_type=jnp.float32
        )
        return dense.reshape(high, GROUP, lanes)

    for at, ref in enumerate(packed):

        def pair(i, carry, at=at, ref=ref):
            both = jnp.concatenate([one_group(ref, 2 * i), one_group(ref, 2 * i + 1)], axis=1)
            both = both.astype(jnp.bfloat16)
            start = pl.multiple_of(i * 2 * GROUP, 2 * GROUP) + at * groups * GROUP
            for h in range(high):
                out_ref[pl.ds(start, 2 * GROUP), h * lanes : (h + 1) * lanes] = both[h]
            return carry

        lax.fori_loop(0, groups // 2, pair, 0)


def densify(packed, base, topk, latents):
    groups, width = packed[0].shape
    lanes = 256 if latents % 256 == 0 else 128
    rows = groups * GROUP * len(packed)
    return pl.pallas_call(
        functools.partial(densify_kernel, topk=topk, latents=latents, lanes=lanes),
        out_shape=jax.ShapeDtypeStruct((rows, latents), jnp.bfloat16),
        in_specs=[pl.BlockSpec(memory_space=pltpu.SMEM)]
        + [pl.BlockSpec(memory_space=pltpu.VMEM) for _ in packed],
        out_specs=pl.BlockSpec(memory_space=pltpu.VMEM),
        compiler_params=pltpu.CompilerParams(vmem_limit_bytes=VMEM_BYTES),
        cost_estimate=pl.CostEstimate(
            flops=rows * latents * width, bytes_accessed=rows * latents * 2, transcendentals=0
        ),
        name="densify",
    )(base, *packed)


def decode_kernel(codes_ref, weights_ref, out_ref):
    out_ref[...] = jnp.dot(codes_ref[...], weights_ref[...], preferred_element_type=jnp.float32)


def decode(codes, decoder):
    rows, latents = codes.shape
    columns = decoder.shape[1]
    width = math.gcd(columns, 256)
    return pl.pallas_call(
        decode_kernel,
        out_shape=jax.ShapeDtypeStruct((rows, columns), jnp.float32),
        grid=(columns // width,),
        in_specs=[
            pl.BlockSpec((rows, latents), lambda n: (0, 0)),
            pl.BlockSpec((latents, width), lambda n: (0, n)),
        ],
        out_specs=pl.BlockSpec((rows, width), lambda n: (0, n)),
        compiler_params=pltpu.CompilerParams(vmem_limit_bytes=DECODE_BYTES),
        cost_estimate=SMALL,
        name="decode",
    )(codes, decoder)


def copy_kernel(order_ref, from_ref, to_ref):
    to_ref[...] = from_ref[...].reshape(to_ref.shape)


def select_columns(weights, order, width):
    kinds, depth = weights.shape[:2]
    count = order.shape[0]
    return pl.pallas_call(
        copy_kernel,
        out_shape=jax.ShapeDtypeStruct((depth, count * kinds * width), weights.dtype),
        grid_spec=pltpu.PrefetchScalarGridSpec(
            num_scalar_prefetch=1,
            grid=(count, kinds),
            in_specs=[pl.BlockSpec((1, depth, width), lambda j, t, order: (t, 0, order[j]))],
            out_specs=pl.BlockSpec((depth, width), lambda j, t, order: (0, j * kinds + t)),
        ),
        compiler_params=pltpu.CompilerParams(vmem_limit_bytes=VMEM_BYTES),
        cost_estimate=pl.CostEstimate(
            flops=0, bytes_accessed=4 * depth * count * kinds * width, transcendentals=0
        ),
        name="select_columns",
    )(order, weights)


def select_rows(weights, order, height):
    columns, count = weights.shape[1], order.shape[0]
    return pl.pallas_call(
        copy_kernel,
        out_shape=jax.ShapeDtypeStruct((count * height, columns), weights.dtype),
        grid_spec=pltpu.PrefetchScalarGridSpec(
            num_scalar_prefetch=1,
            grid=(count,),
            in_specs=[pl.BlockSpec((height, columns), lambda j, order: (order[j], 0))],
            out_specs=pl.BlockSpec((height, columns), lambda j, order: (j, 0)),
        ),
        compiler_params=pltpu.CompilerParams(vmem_limit_bytes=VMEM_BYTES),
        cost_estimate=pl.CostEstimate(
            flops=0, bytes_accessed=4 * count * height * columns, transcendentals=0
        ),
        name="select_rows",
    )(order, weights)


def attend_kernel(*refs, heads, slots, group):
    query_pos, key_pos = refs[0], refs[1]
    new = refs[2 : 2 + slots]
    cached = refs[2 + slots : -1]
    out = refs[-1]
    width = heads * HEAD
    hidden = key_pos[...] > query_pos[...]
    for h in range(heads):
        here = slice(h * HEAD, (h + 1) * HEAD)
        keys = [c[0, :, here] for c in cached] + [
            n[:, width + h * HEAD : width + (h + 1) * HEAD] for n in new
        ]
        values = [c[1, :, here] for c in cached] + [
            n[:, 2 * width + h * HEAD : 2 * width + (h + 1) * HEAD] for n in new
        ]
        keys = jnp.concatenate(keys, axis=0)
        values = jnp.concatenate(values, axis=0)
        scores = lax.dot_general(
            jnp.concatenate([new[s][:, here] for s in group], axis=0), keys, (((1,), (1,)), ((), ())), preferred_element_type=jnp.float32
        ) * (1.0 / math.sqrt(HEAD))
        cut = scores.shape[1] - hidden.shape[1]
        old, fresh = scores[:, :cut], jnp.where(hidden, -1e30, scores[:, cut:])
        highest = jnp.maximum(
            jnp.max(old, axis=1, keepdims=True), jnp.max(fresh, axis=1, keepdims=True)
        )
        old, fresh = jnp.exp(old - highest), jnp.exp(fresh - highest)
        total = jnp.sum(old, axis=1, keepdims=True) + jnp.sum(fresh, axis=1, keepdims=True)
        scale = 1.0 / total
        probs = jnp.concatenate(
            [(old * scale).astype(jnp.bfloat16), (fresh * scale).astype(jnp.bfloat16)], axis=1
        )
        mixed = jnp.dot(probs, values, preferred_element_type=jnp.float32)
        out[:, here] = mixed.astype(jnp.bfloat16)


def attend(query_pos, key_pos, new, cached, group, heads):
    slot_rows = new[0].shape[0]
    rows = slot_rows * len(group)
    keys = slot_rows * len(new) + sum(c.shape[1] for c in cached)
    vmem = pl.BlockSpec(memory_space=pltpu.VMEM)
    return pl.pallas_call(
        functools.partial(attend_kernel, heads=heads, slots=len(new), group=group),
        out_shape=jax.ShapeDtypeStruct((rows, heads * HEAD), jnp.bfloat16),
        in_specs=[vmem] * (2 + len(new) + len(cached)),
        out_specs=vmem,
        compiler_params=pltpu.CompilerParams(vmem_limit_bytes=VMEM_BYTES),
        cost_estimate=pl.CostEstimate(
            flops=4 * rows * keys * heads * HEAD,
            bytes_accessed=keys * heads * HEAD * 4,
            transcendentals=rows * keys * heads,
        ),
        name="attend",
    )(query_pos, key_pos, *new, *cached)


def across_line(value, distance):
    return lax.ppermute(value, "lat", [(i, i ^ distance) for i in range(lax.axis_size("lat"))])


def swap(value, distance, size):
    return lax.ppermute(value, "col", [(i, i ^ distance) for i in range(size)])


def normalize(values, sums, gain, shift):
    row_mean = sums[0] / D
    row_var = sums[1] / D - row_mean * row_mean
    inverse = 1.0 / jnp.sqrt(row_var + 1e-05)
    return ((values - row_mean[:, None]) * inverse[:, None] * gain + shift).astype(jnp.bfloat16)


def pack(code_ids, code_vals):
    rows, topk = code_ids.shape
    vals = code_vals.astype(jnp.bfloat16).astype(jnp.float32)
    shape = (rows // GROUP, GROUP * topk)
    return jnp.concatenate([code_ids.astype(jnp.float32).reshape(shape), vals.reshape(shape)], axis=1)


SCALE = 256.0


def to_half(value):
    return (value * SCALE).astype(jnp.float16)


def from_half(value):
    return value.astype(jnp.float32) * (1.0 / SCALE)


def line_body(
    code_ids, code_vals, decoder, dec_bias, ln_gain, ln_bias, w_qkv, cache_kv, positions, w_out
):
    lat = lax.axis_index("lat")
    col = lax.axis_index("col")
    cols = lax.axis_size("col")
    rows, topk = code_ids.shape
    latents, columns = decoder.shape
    head_width = w_qkv.shape[2]
    own_width = head_width // cols
    heads = own_width // HEAD
    hold = lax.optimization_barrier

    packed = pack(code_ids, code_vals)
    packed = [packed, *(across_line(packed, j) for j in (1, 2, 3))]
    base = (lat * latents).reshape(1)

    def cache_of(j):
        start = (col ^ j) * own_width
        return lax.dynamic_slice_in_dim(cache_kv, start, own_width, 2)

    across = swap(jnp.stack([cache_of(2), cache_of(3)]), 2, cols)

    key_pos = jnp.concatenate(
        [lax.dynamic_slice_in_dim(positions, (lat ^ j) * rows, rows, 0) for j in range(4)]
    )
    query_pos = key_pos.reshape(-1, 1)

    codes = densify([packed[2], packed[1]], base, topk, latents)
    early = jnp.dot(codes, decoder, preferred_element_type=jnp.float32)
    late_packed, sent2, sent1 = hold(
        ((packed[3], packed[0]), to_half(early[:rows]), to_half(early[rows:]))
    )
    came2 = across_line(sent2, 2)
    came1 = across_line(sent1, 1)
    codes = densify(late_packed, base, topk, latents)
    codes, across, query_pos = hold((codes, across, query_pos))
    late = decode(codes, decoder)
    sent3, came2, came1, weights, out_source = hold(
        (to_half(late[:rows]), came2, came1, w_qkv.transpose(1, 0, 2), w_out)
    )
    came3 = across_line(sent3, 3)

    away_weights = select_columns(weights, jnp.stack([col ^ 1, col ^ 3]), own_width)
    keep_weights = select_columns(weights, jnp.stack([col, col ^ 2]), own_width)
    beside = swap(jnp.stack([cache_of(1), across[1]]), 1, cols)
    out_weights = select_rows(out_source, jnp.stack([col, col ^ 2, col ^ 1, col ^ 3]), own_width)
    came3, away_weights, keep_weights, out_weights, beside = hold(
        (came3, away_weights, keep_weights, out_weights, beside)
    )
    cached = [cache_of(0), across[0], beside[0], beside[1]]
    residual = late[rows:] + from_half(came1) + from_half(came2) + from_half(came3)
    residual = residual + dec_bias.astype(jnp.float32)

    sums = jnp.stack([jnp.sum(residual, axis=1), jnp.sum(residual * residual, axis=1)])
    sums = sums + swap(sums, 1, cols)
    sums = sums + swap(sums, 2, cols)
    own = normalize(residual, sums, ln_gain, ln_bias)
    near = across_line(own, 1)
    across = across_line(own, 2)
    own_again, near, across = hold((own, near, across))
    far = across_line(own_again, 3)

    quarter = keep_weights.shape[1] // 2

    def project(block):
        away = jnp.dot(block, away_weights, preferred_element_type=jnp.float32).astype(jnp.float16)
        keep = jnp.dot(block, keep_weights, preferred_element_type=jnp.float32)
        keep = keep + swap(away, 1, cols).astype(jnp.float32)
        return keep[:, :quarter], keep[:, quarter:].astype(jnp.float16)

    def finish(keep, payload):
        return (keep + swap(payload, 2, cols).astype(jnp.float32)).astype(jnp.bfloat16)

    keep0, payload0 = project(own)
    middle, payload0 = hold((jnp.concatenate([near, across], axis=0), payload0))
    first = finish(keep0, payload0)
    keep1, payload1 = project(middle)
    first, payload1 = hold((first, payload1))
    far, middle = hold((far, finish(keep1, payload1)))
    qkv = [first, middle[:rows], middle[rows:], finish(*project(far))]

    key_row = key_pos.reshape(1, -1)

    def pos_of(a, b):
        return jnp.concatenate(
            [query_pos[a * rows : (a + 1) * rows], query_pos[b * rows : (b + 1) * rows]], axis=0
        )

    early = attend(pos_of(2, 1), key_row, qkv, cached, (2, 1), heads)
    late_pos, early = hold((pos_of(3, 0), early))
    late = attend(late_pos, key_row, qkv, cached, (3, 0), heads)
    swapped, late = hold((swap(early, 2, cols), late))
    early = jnp.concatenate([early, swapped], axis=1)
    early = jnp.concatenate([early, swap(early, 1, cols)], axis=1)
    early = jnp.dot(early, out_weights, preferred_element_type=jnp.float32).astype(jnp.bfloat16)
    sent2, sent1, late = hold((early[:rows], early[rows:], late))
    came2 = across_line(sent2, 2)
    came1 = across_line(sent1, 1)
    late = jnp.concatenate([late, swap(late, 2, cols)], axis=1)
    late = jnp.concatenate([late, swap(late, 1, cols)], axis=1)
    late, came2, came1 = hold((late, came2, came1))
    late = jnp.dot(late, out_weights, preferred_element_type=jnp.float32)
    came3 = across_line(late[:rows].astype(jnp.bfloat16), 3)
    branch = late[rows:] + came1.astype(jnp.float32) + came2.astype(jnp.float32)
    return (residual + branch + came3.astype(jnp.float32)).astype(jnp.bfloat16)


def attend_block(queries, keys, values, query_pos, key_pos):
    heads = queries.shape[1] // HEAD
    query_heads = queries.reshape(queries.shape[0], heads, HEAD)
    key_heads = keys.reshape(keys.shape[0], heads, HEAD)
    value_heads = values.reshape(values.shape[0], heads, HEAD)
    scores = jnp.einsum(
        "qhe,khe->hqk", query_heads, key_heads, preferred_element_type=jnp.float32
    ) * (1.0 / math.sqrt(HEAD))
    visible = key_pos[None, None, :] <= query_pos[None, :, None]
    scores = jnp.where(visible, scores, -1e30)
    highest = jnp.max(scores, axis=-1, keepdims=True)
    expo = jnp.exp(scores - highest)
    probs = (expo / jnp.sum(expo, axis=-1, keepdims=True)).astype(jnp.bfloat16)
    mixed = jnp.einsum("hqk,khe->qhe", probs, value_heads, preferred_element_type=jnp.float32)
    return mixed.reshape(queries.shape[0], heads * HEAD).astype(jnp.bfloat16)


def general_body(
    code_ids, code_vals, decoder, dec_bias, ln_gain, ln_bias, w_qkv, cache_kv, positions, w_out
):
    lat_index = lax.axis_index("lat")
    col_total = lax.axis_size("col")
    col_index = lax.axis_index("col")
    rows, topk = code_ids.shape
    shard_latents = decoder.shape[0]
    packed = lax.all_gather(pack(code_ids, code_vals), "lat", axis=0, tiled=True)
    base = (lat_index * shard_latents).reshape(1)
    dense_codes = densify([packed], base, topk, shard_latents)
    total_rows = dense_codes.shape[0]
    col_rows = total_rows // col_total
    residual = lax.psum_scatter(
        jnp.dot(dense_codes, decoder, preferred_element_type=jnp.float32),
        "lat",
        scatter_dimension=0,
        tiled=True,
    ) + dec_bias.astype(jnp.float32)
    sums = lax.psum((jnp.sum(residual, axis=1), jnp.sum(residual * residual, axis=1)), "col")
    normed = lax.all_gather(normalize(residual, sums, ln_gain, ln_bias), "lat", axis=0, tiled=True)
    head_width = w_qkv.shape[2]
    w_flat = w_qkv.reshape(w_qkv.shape[0], 3 * head_width)
    own_rows = lax.psum_scatter(
        jnp.dot(normed, w_flat, preferred_element_type=jnp.float32),
        "col",
        scatter_dimension=0,
        tiled=True,
    ).astype(jnp.bfloat16)
    queries = own_rows[:, :head_width]
    new_kv = lax.all_gather(own_rows[:, head_width:], "col", axis=0, tiled=True)
    context = lax.all_gather(cache_kv, "col", axis=1, tiled=True)
    cached_len = context.shape[1]
    keys = jnp.concatenate([context[0], new_kv[:, :head_width]], axis=0)
    values = jnp.concatenate([context[1], new_kv[:, head_width:]], axis=0)
    key_pos = jnp.concatenate([jnp.arange(cached_len, dtype=jnp.int32), cached_len + positions])
    query_pos = cached_len + lax.dynamic_slice_in_dim(positions, col_index * col_rows, col_rows, 0)
    attended = attend_block(queries, keys, values, query_pos, key_pos)
    gathered = lax.all_gather(attended, "col", axis=0, tiled=True)
    branch_out = lax.psum_scatter(
        jnp.dot(gathered, w_out, preferred_element_type=jnp.float32).astype(jnp.bfloat16),
        "lat",
        scatter_dimension=0,
        tiled=True,
    ).astype(jnp.float32)
    return (residual + branch_out).astype(jnp.bfloat16)


def solution(mesh):
    def program(*args):
        lats, cols = mesh.shape["lat"], mesh.shape["col"]
        heads = args[6].shape[2] // HEAD // lats
        fits = lats == 4 and cols == 4 and heads % cols == 0
        return jax.shard_map(
            line_body if fits else general_body,
            mesh=mesh,
            in_specs=(
                P(("ckpt", "lat"), None),
                P(("ckpt", "lat"), None),
                P(("ckpt", "lat"), "col"),
                P(("ckpt", "col")),
                P(("ckpt", "col")),
                P(("ckpt", "col")),
                P(("ckpt", "col"), None, "lat"),
                P(None, ("ckpt", "col"), "lat"),
                P("ckpt"),
                P(("ckpt", "lat"), "col"),
            ),
            out_specs=P(("ckpt", "lat"), "col"),
            check_vma=False,
        )(*args)

    return program
```

```python
import functools
import math

import jax
import jax.numpy as jnp
from jax import lax
from jax.experimental import pallas as pl
from jax.experimental.pallas import tpu as pltpu
from jax.sharding import PartitionSpec as P

D = 5120
HEAD = 128
GROUP = 8
VMEM_BYTES = 20 * 1024 * 1024
DECODE_BYTES = 44 * 1024 * 1024
SMALL = pl.CostEstimate(flops=1, bytes_accessed=1, transcendentals=0)


def densify_kernel(base_ref, *refs, topk, latents, lanes):
    packed, out_ref = refs[:-1], refs[-1]
    groups, width = packed[0].shape[0], packed[0].shape[1] // 2
    high = latents // lanes
    base = base_ref[0]
    row_of = lax.broadcasted_iota(jnp.int32, (1, width), 1) // topk
    sub = lax.broadcasted_iota(jnp.int32, (high * GROUP, width), 0)
    sub = sub.astype(jnp.float32).astype(jnp.bfloat16)
    low_sub = lax.broadcasted_iota(jnp.int32, (lanes, width), 0)
    low_sub = low_sub.astype(jnp.float32).astype(jnp.bfloat16)
    one, zero = jnp.ones((), jnp.bfloat16), jnp.zeros((), jnp.bfloat16)

    def half(value):
        return value.astype(jnp.float32).astype(jnp.bfloat16)

    def one_group(ref, g):
        local = ref[pl.ds(g, 1), :width].astype(jnp.int32) - base
        inside = (local >= 0) & (local < latents)
        key = half(jnp.where(inside, (local // lanes) * GROUP + row_of, -1))
        low = half(jnp.where(inside, local % lanes, -1))
        vals = ref[pl.ds(g, 1), width:].astype(jnp.bfloat16)
        left = jnp.where(key == sub, vals, zero)
        right = jnp.where(low == low_sub, one, zero)
        dense = lax.dot_general(
            left, right, (((1,), (1,)), ((), ())), preferred_element_type=jnp.float32
        )
        return dense.reshape(high, GROUP, lanes)

    for at, ref in enumerate(packed):

        def pair(i, carry, at=at, ref=ref):
            both = jnp.concatenate([one_group(ref, 2 * i), one_group(ref, 2 * i + 1)], axis=1)
            both = both.astype(jnp.bfloat16)
            start = pl.multiple_of(i * 2 * GROUP, 2 * GROUP) + at * groups * GROUP
            for h in range(high):
                out_ref[pl.ds(start, 2 * GROUP), h * lanes : (h + 1) * lanes] = both[h]
            return carry

        lax.fori_loop(0, groups // 2, pair, 0)


def densify(packed, base, topk, latents):
    groups, width = packed[0].shape
    lanes = 256 if latents % 256 == 0 else 128
    rows = groups * GROUP * len(packed)
    return pl.pallas_call(
        functools.partial(densify_kernel, topk=topk, latents=latents, lanes=lanes),
        out_shape=jax.ShapeDtypeStruct((rows, latents), jnp.bfloat16),
        in_specs=[pl.BlockSpec(memory_space=pltpu.SMEM)]
        + [pl.BlockSpec(memory_space=pltpu.VMEM) for _ in packed],
        out_specs=pl.BlockSpec(memory_space=pltpu.VMEM),
        compiler_params=pltpu.CompilerParams(vmem_limit_bytes=VMEM_BYTES),
        cost_estimate=pl.CostEstimate(
            flops=rows * latents * width, bytes_accessed=rows * latents * 2, transcendentals=0
        ),
        name="densify",
    )(base, *packed)


def decode_kernel(codes_ref, weights_ref, out_ref):
    out_ref[...] = jnp.dot(codes_ref[...], weights_ref[...], preferred_element_type=jnp.float32)


def decode(codes, decoder):
    rows, latents = codes.shape
    columns = decoder.shape[1]
    width = math.gcd(columns, 256)
    return pl.pallas_call(
        decode_kernel,
        out_shape=jax.ShapeDtypeStruct((rows, columns), jnp.float32),
        grid=(columns // width,),
        in_specs=[
            pl.BlockSpec((rows, latents), lambda n: (0, 0)),
            pl.BlockSpec((latents, width), lambda n: (0, n)),
        ],
        out_specs=pl.BlockSpec((rows, width), lambda n: (0, n)),
        compiler_params=pltpu.CompilerParams(vmem_limit_bytes=DECODE_BYTES),
        cost_estimate=SMALL,
        name="decode",
    )(codes, decoder)


def copy_kernel(order_ref, from_ref, to_ref):
    to_ref[...] = from_ref[...].reshape(to_ref.shape)


def select_columns(weights, order, width):
    kinds, depth = weights.shape[:2]
    count = order.shape[0]
    return pl.pallas_call(
        copy_kernel,
        out_shape=jax.ShapeDtypeStruct((depth, count * kinds * width), weights.dtype),
        grid_spec=pltpu.PrefetchScalarGridSpec(
            num_scalar_prefetch=1,
            grid=(count, kinds),
            in_specs=[pl.BlockSpec((1, depth, width), lambda j, t, order: (t, 0, order[j]))],
            out_specs=pl.BlockSpec((depth, width), lambda j, t, order: (0, j * kinds + t)),
        ),
        compiler_params=pltpu.CompilerParams(vmem_limit_bytes=VMEM_BYTES),
        cost_estimate=pl.CostEstimate(
            flops=0, bytes_accessed=4 * depth * count * kinds * width, transcendentals=0
        ),
        name="select_columns",
    )(order, weights)


def select_rows(weights, order, height):
    columns, count = weights.shape[1], order.shape[0]
    return pl.pallas_call(
        copy_kernel,
        out_shape=jax.ShapeDtypeStruct((count * height, columns), weights.dtype),
        grid_spec=pltpu.PrefetchScalarGridSpec(
            num_scalar_prefetch=1,
            grid=(count,),
            in_specs=[pl.BlockSpec((height, columns), lambda j, order: (order[j], 0))],
            out_specs=pl.BlockSpec((height, columns), lambda j, order: (j, 0)),
        ),
        compiler_params=pltpu.CompilerParams(vmem_limit_bytes=VMEM_BYTES),
        cost_estimate=pl.CostEstimate(
            flops=0, bytes_accessed=4 * count * height * columns, transcendentals=0
        ),
        name="select_rows",
    )(order, weights)


def attend_kernel(*refs, heads, slots, group):
    query_pos, key_pos = refs[0], refs[1]
    new = refs[2 : 2 + slots]
    cached = refs[2 + slots : -1]
    out = refs[-1]
    width = heads * HEAD
    hidden = key_pos[...] > query_pos[...]
    for h in range(heads):
        here = slice(h * HEAD, (h + 1) * HEAD)
        keys = [c[0, :, here] for c in cached] + [
            n[:, width + h * HEAD : width + (h + 1) * HEAD] for n in new
        ]
        values = [c[1, :, here] for c in cached] + [
            n[:, 2 * width + h * HEAD : 2 * width + (h + 1) * HEAD] for n in new
        ]
        keys = jnp.concatenate(keys, axis=0)
        values = jnp.concatenate(values, axis=0)
        scores = lax.dot_general(
            jnp.concatenate([new[s][:, here] for s in group], axis=0), keys, (((1,), (1,)), ((), ())), preferred_element_type=jnp.float32
        ) * (1.0 / math.sqrt(HEAD))
        cut = scores.shape[1] - hidden.shape[1]
        old, fresh = scores[:, :cut], jnp.where(hidden, -1e30, scores[:, cut:])
        highest = jnp.maximum(
            jnp.max(old, axis=1, keepdims=True), jnp.max(fresh, axis=1, keepdims=True)
        )
        old, fresh = jnp.exp(old - highest), jnp.exp(fresh - highest)
        total = jnp.sum(old, axis=1, keepdims=True) + jnp.sum(fresh, axis=1, keepdims=True)
        scale = 1.0 / total
        probs = jnp.concatenate(
            [(old * scale).astype(jnp.bfloat16), (fresh * scale).astype(jnp.bfloat16)], axis=1
        )
        mixed = jnp.dot(probs, values, preferred_element_type=jnp.float32)
        out[:, here] = mixed.astype(jnp.bfloat16)


def attend(query_pos, key_pos, new, cached, group, heads):
    slot_rows = new[0].shape[0]
    rows = slot_rows * len(group)
    keys = slot_rows * len(new) + sum(c.shape[1] for c in cached)
    vmem = pl.BlockSpec(memory_space=pltpu.VMEM)
    return pl.pallas_call(
        functools.partial(attend_kernel, heads=heads, slots=len(new), group=group),
        out_shape=jax.ShapeDtypeStruct((rows, heads * HEAD), jnp.bfloat16),
        in_specs=[vmem] * (2 + len(new) + len(cached)),
        out_specs=vmem,
        compiler_params=pltpu.CompilerParams(vmem_limit_bytes=VMEM_BYTES),
        cost_estimate=pl.CostEstimate(
            flops=4 * rows * keys * heads * HEAD,
            bytes_accessed=keys * heads * HEAD * 4,
            transcendentals=rows * keys * heads,
        ),
        name="attend",
    )(query_pos, key_pos, *new, *cached)


PAIRS = [(0, 1), (1, 0), (2, 3), (3, 2)]
INWARD = [(0, 1), (3, 2)]
MIDDLE = [(1, 2), (2, 1)]
OUTWARD = [(1, 0), (2, 3)]


def line_slots(index):
    low = index < 2
    return [index, index ^ 1, jnp.where(low, 2, 1), jnp.where(low, 3, 0)]


def line_gather_direct(own, outer):
    near = lax.ppermute(own, "lat", [(i, i ^ 1) for i in range(4)])
    two = lax.ppermute(own, "lat", [(i, i ^ 2) for i in range(4)])
    three = lax.ppermute(own, "lat", [(i, i ^ 3) for i in range(4)])
    return [own, near, jnp.where(outer, two, three), jnp.where(outer, three, two)]


def swap(value, distance, size):
    return lax.ppermute(value, "col", [(i, i ^ distance) for i in range(size)])


def normalize(values, sums, gain, shift):
    row_mean = sums[0] / D
    row_var = sums[1] / D - row_mean * row_mean
    inverse = 1.0 / jnp.sqrt(row_var + 1e-05)
    return ((values - row_mean[:, None]) * inverse[:, None] * gain + shift).astype(jnp.bfloat16)


def pack(code_ids, code_vals):
    rows, topk = code_ids.shape
    vals = code_vals.astype(jnp.bfloat16).astype(jnp.float32)
    shape = (rows // GROUP, GROUP * topk)
    return jnp.concatenate([code_ids.astype(jnp.float32).reshape(shape), vals.reshape(shape)], axis=1)


SCALE = 256.0


def to_half(value):
    return (value * SCALE).astype(jnp.float16)


def from_half(value):
    return value.astype(jnp.float32) * (1.0 / SCALE)


def line_body(
    code_ids, code_vals, decoder, dec_bias, ln_gain, ln_bias, w_qkv, cache_kv, positions, w_out
):
    lat = lax.axis_index("lat")
    col = lax.axis_index("col")
    cols = lax.axis_size("col")
    rows, topk = code_ids.shape
    latents, columns = decoder.shape
    head_width = w_qkv.shape[2]
    own_width = head_width // cols
    heads = own_width // HEAD
    outer = (lat == 0) | (lat == 3)
    slots = line_slots(lat)
    hold = lax.optimization_barrier

    packed = pack(code_ids, code_vals)
    packed = line_gather_direct(packed, outer)
    base = (lat * latents).reshape(1)

    def cache_of(j):
        start = (col ^ j) * own_width
        return lax.dynamic_slice_in_dim(cache_kv, start, own_width, 2)

    across = swap(jnp.stack([cache_of(2), cache_of(3)]), 2, cols)

    key_pos = jnp.concatenate(
        [lax.dynamic_slice_in_dim(positions, s * rows, rows, 0) for s in slots]
    )
    query_pos = key_pos.reshape(-1, 1)

    far = jnp.dot(
        densify([packed[3]], base, topk, latents), decoder, preferred_element_type=jnp.float32
    )
    packed2, sent = hold((packed[2], to_half(far)))
    in_far = lax.ppermute(sent, "lat", INWARD)
    second = decode(densify([packed2], base, topk, latents), decoder)
    second, in_far = hold((second, in_far))
    near_packed, sent_far, sent_across = hold(
        ((packed[1], packed[0]), to_half(far + from_half(in_far)), to_half(second))
    )
    mid_far = lax.ppermute(sent_far, "lat", MIDDLE)
    in_across = lax.ppermute(sent_across, "lat", INWARD)
    codes_near = densify(near_packed, base, topk, latents)
    codes_near, across, query_pos = hold((codes_near, across, query_pos))
    near = decode(codes_near, decoder)
    near, mid_far, in_across = hold((near, mid_far, in_across))
    last = to_half(near[:rows] + from_half(mid_far))
    across, last, second, weights = hold((across, last, second, w_qkv.transpose(1, 0, 2)))
    last = lax.ppermute(last, "lat", PAIRS)
    mid_across = lax.ppermute(to_half(second + from_half(in_across)), "lat", MIDDLE)

    away_weights = select_columns(weights, jnp.stack([col ^ 1, col ^ 3]), own_width)
    keep_weights = select_columns(weights, jnp.stack([col, col ^ 2]), own_width)
    out_weights = select_rows(w_out, jnp.stack([col, col ^ 2, col ^ 1, col ^ 3]), own_width)
    beside = swap(jnp.stack([cache_of(1), across[1]]), 1, cols)
    last, away_weights, keep_weights, out_weights, beside = hold(
        (last, away_weights, keep_weights, out_weights, beside)
    )
    cached = [cache_of(0), across[0], beside[0], beside[1]]
    residual = near[rows:] + from_half(mid_across) + from_half(last)
    residual = residual + dec_bias.astype(jnp.float32)

    sums = jnp.stack([jnp.sum(residual, axis=1), jnp.sum(residual * residual, axis=1)])
    sums = sums + swap(sums, 1, cols)
    sums = sums + swap(sums, 2, cols)
    own = normalize(residual, sums, ln_gain, ln_bias)
    near = lax.ppermute(own, "lat", PAIRS)
    across = lax.ppermute(own, "lat", MIDDLE)
    far = lax.ppermute(near, "lat", MIDDLE)
    across_out = lax.ppermute(across, "lat", OUTWARD)
    far_out = lax.ppermute(far, "lat", OUTWARD)

    quarter = keep_weights.shape[1] // 2

    def project(block):
        away = jnp.dot(block, away_weights, preferred_element_type=jnp.float32).astype(jnp.float16)
        keep = jnp.dot(block, keep_weights, preferred_element_type=jnp.float32)
        keep = keep + swap(away, 1, cols).astype(jnp.float32)
        return keep[:, :quarter], keep[:, quarter:].astype(jnp.float16)

    def finish(keep, payload):
        return (keep + swap(payload, 2, cols).astype(jnp.float32)).astype(jnp.bfloat16)

    keep0, payload0 = project(own)
    near_block, across, payload0 = hold((near, across, payload0))
    keep1, payload1 = project(near_block)
    third, far, payload1, first = hold(
        (jnp.where(outer, across_out, across), far, payload1, finish(keep0, payload0))
    )
    keep2, payload2 = project(third)
    second, payload2 = hold((finish(keep1, payload1), payload2))
    third = finish(keep2, payload2)
    fourth, third = hold((jnp.where(outer, far_out, far), third))
    qkv = [first, second, third, finish(*project(fourth))]

    key_row = key_pos.reshape(1, -1)

    def pos_of(a, b):
        return jnp.concatenate(
            [query_pos[a * rows : (a + 1) * rows], query_pos[b * rows : (b + 1) * rows]], axis=0
        )

    mixed_far = attend(pos_of(3, 2), key_row, qkv, cached, (3, 2), heads)
    near_pos, mixed_far = hold((pos_of(1, 0), mixed_far))
    mixed_near = attend(near_pos, key_row, qkv, cached, (1, 0), heads)
    swapped_far, mixed_near = hold((swap(mixed_far, 2, cols), mixed_near))
    mixed_far = jnp.concatenate([mixed_far, swapped_far], axis=1)
    mixed_far = jnp.concatenate([mixed_far, swap(mixed_far, 1, cols)], axis=1)
    product_far = jnp.dot(mixed_far, out_weights, preferred_element_type=jnp.float32)
    sent_far, mixed_near = hold((product_far[:rows].astype(jnp.bfloat16), mixed_near))
    in_far = lax.ppermute(sent_far, "lat", INWARD)
    mixed_near = jnp.concatenate([mixed_near, swap(mixed_near, 2, cols)], axis=1)
    mixed_near = jnp.concatenate([mixed_near, swap(mixed_near, 1, cols)], axis=1)
    product_near = jnp.dot(mixed_near, out_weights, preferred_element_type=jnp.float32)
    mid_far = (product_far[:rows] + in_far.astype(jnp.float32)).astype(jnp.bfloat16)
    second, mid_far = hold((product_far[rows:], mid_far))
    mid_far = lax.ppermute(mid_far, "lat", MIDDLE)
    in_across = lax.ppermute(second.astype(jnp.bfloat16), "lat", INWARD)
    last = (product_near[:rows] + mid_far.astype(jnp.float32)).astype(jnp.bfloat16)
    second, last = hold((second, last))
    last = lax.ppermute(last, "lat", PAIRS)
    mid_across = (second + in_across.astype(jnp.float32)).astype(jnp.bfloat16)
    mid_across = lax.ppermute(mid_across, "lat", MIDDLE)
    branch = product_near[rows:] + last.astype(jnp.float32)
    branch, mid_across = hold((residual + branch, mid_across))
    return (branch + mid_across.astype(jnp.float32)).astype(jnp.bfloat16)


def attend_block(queries, keys, values, query_pos, key_pos):
    heads = queries.shape[1] // HEAD
    query_heads = queries.reshape(queries.shape[0], heads, HEAD)
    key_heads = keys.reshape(keys.shape[0], heads, HEAD)
    value_heads = values.reshape(values.shape[0], heads, HEAD)
    scores = jnp.einsum(
        "qhe,khe->hqk", query_heads, key_heads, preferred_element_type=jnp.float32
    ) * (1.0 / math.sqrt(HEAD))
    visible = key_pos[None, None, :] <= query_pos[None, :, None]
    scores = jnp.where(visible, scores, -1e30)
    highest = jnp.max(scores, axis=-1, keepdims=True)
    expo = jnp.exp(scores - highest)
    probs = (expo / jnp.sum(expo, axis=-1, keepdims=True)).astype(jnp.bfloat16)
    mixed = jnp.einsum("hqk,khe->qhe", probs, value_heads, preferred_element_type=jnp.float32)
    return mixed.reshape(queries.shape[0], heads * HEAD).astype(jnp.bfloat16)


def general_body(
    code_ids, code_vals, decoder, dec_bias, ln_gain, ln_bias, w_qkv, cache_kv, positions, w_out
):
    lat_index = lax.axis_index("lat")
    col_total = lax.axis_size("col")
    col_index = lax.axis_index("col")
    rows, topk = code_ids.shape
    shard_latents = decoder.shape[0]
    packed = lax.all_gather(pack(code_ids, code_vals), "lat", axis=0, tiled=True)
    base = (lat_index * shard_latents).reshape(1)
    dense_codes = densify([packed], base, topk, shard_latents)
    total_rows = dense_codes.shape[0]
    col_rows = total_rows // col_total
    residual = lax.psum_scatter(
        jnp.dot(dense_codes, decoder, preferred_element_type=jnp.float32),
        "lat",
        scatter_dimension=0,
        tiled=True,
    ) + dec_bias.astype(jnp.float32)
    sums = lax.psum((jnp.sum(residual, axis=1), jnp.sum(residual * residual, axis=1)), "col")
    normed = lax.all_gather(normalize(residual, sums, ln_gain, ln_bias), "lat", axis=0, tiled=True)
    head_width = w_qkv.shape[2]
    w_flat = w_qkv.reshape(w_qkv.shape[0], 3 * head_width)
    own_rows = lax.psum_scatter(
        jnp.dot(normed, w_flat, preferred_element_type=jnp.float32),
        "col",
        scatter_dimension=0,
        tiled=True,
    ).astype(jnp.bfloat16)
    queries = own_rows[:, :head_width]
    new_kv = lax.all_gather(own_rows[:, head_width:], "col", axis=0, tiled=True)
    context = lax.all_gather(cache_kv, "col", axis=1, tiled=True)
    cached_len = context.shape[1]
    keys = jnp.concatenate([context[0], new_kv[:, :head_width]], axis=0)
    values = jnp.concatenate([context[1], new_kv[:, head_width:]], axis=0)
    key_pos = jnp.concatenate([jnp.arange(cached_len, dtype=jnp.int32), cached_len + positions])
    query_pos = cached_len + lax.dynamic_slice_in_dim(positions, col_index * col_rows, col_rows, 0)
    attended = attend_block(queries, keys, values, query_pos, key_pos)
    gathered = lax.all_gather(attended, "col", axis=0, tiled=True)
    branch_out = lax.psum_scatter(
        jnp.dot(gathered, w_out, preferred_element_type=jnp.float32).astype(jnp.bfloat16),
        "lat",
        scatter_dimension=0,
        tiled=True,
    ).astype(jnp.float32)
    return (residual + branch_out).astype(jnp.bfloat16)


def solution(mesh):
    def program(*args):
        lats, cols = mesh.shape["lat"], mesh.shape["col"]
        heads = args[6].shape[2] // HEAD // lats
        fits = lats == 4 and cols == 4 and heads % cols == 0
        return jax.shard_map(
            line_body if fits else general_body,
            mesh=mesh,
            in_specs=(
                P(("ckpt", "lat"), None),
                P(("ckpt", "lat"), None),
                P(("ckpt", "lat"), "col"),
                P(("ckpt", "col")),
                P(("ckpt", "col")),
                P(("ckpt", "col")),
                P(("ckpt", "col"), None, "lat"),
                P(None, ("ckpt", "col"), "lat"),
                P("ckpt"),
                P(("ckpt", "lat"), "col"),
            ),
            out_specs=P(("ckpt", "lat"), "col"),
            check_vma=False,
        )(*args)

    return program
```

```python
import functools
import math

import jax
import jax.numpy as jnp
from jax import lax
from jax.experimental import pallas as pl
from jax.experimental.pallas import tpu as pltpu
from jax.sharding import PartitionSpec as P

D = 5120
HEAD = 128
GROUP = 8
VMEM_BYTES = 20 * 1024 * 1024
DECODE_BYTES = 44 * 1024 * 1024
SMALL = pl.CostEstimate(flops=1, bytes_accessed=1, transcendentals=0)


def densify_kernel(base_ref, *refs, topk, latents, lanes):
    packed, out_ref = refs[:-1], refs[-1]
    groups, width = packed[0].shape[0], packed[0].shape[1] // 2
    high = latents // lanes
    base = base_ref[0]
    row_of = lax.broadcasted_iota(jnp.int32, (1, width), 1) // topk
    sub = lax.broadcasted_iota(jnp.int32, (high * GROUP, width), 0)
    sub = sub.astype(jnp.float32).astype(jnp.bfloat16)
    low_sub = lax.broadcasted_iota(jnp.int32, (lanes, width), 0)
    low_sub = low_sub.astype(jnp.float32).astype(jnp.bfloat16)
    one, zero = jnp.ones((), jnp.bfloat16), jnp.zeros((), jnp.bfloat16)

    def half(value):
        return value.astype(jnp.float32).astype(jnp.bfloat16)

    def one_group(ref, g):
        local = ref[pl.ds(g, 1), :width].astype(jnp.int32) - base
        inside = (local >= 0) & (local < latents)
        key = half(jnp.where(inside, (local // lanes) * GROUP + row_of, -1))
        low = half(jnp.where(inside, local % lanes, -1))
        vals = ref[pl.ds(g, 1), width:].astype(jnp.bfloat16)
        left = jnp.where(key == sub, vals, zero)
        right = jnp.where(low == low_sub, one, zero)
        dense = lax.dot_general(
            left, right, (((1,), (1,)), ((), ())), preferred_element_type=jnp.float32
        )
        return dense.reshape(high, GROUP, lanes)

    for at, ref in enumerate(packed):

        def pair(i, carry, at=at, ref=ref):
            both = jnp.concatenate([one_group(ref, 2 * i), one_group(ref, 2 * i + 1)], axis=1)
            both = both.astype(jnp.bfloat16)
            start = pl.multiple_of(i * 2 * GROUP, 2 * GROUP) + at * groups * GROUP
            for h in range(high):
                out_ref[pl.ds(start, 2 * GROUP), h * lanes : (h + 1) * lanes] = both[h]
            return carry

        lax.fori_loop(0, groups // 2, pair, 0)


def densify(packed, base, topk, latents):
    groups, width = packed[0].shape
    lanes = 256 if latents % 256 == 0 else 128
    rows = groups * GROUP * len(packed)
    return pl.pallas_call(
        functools.partial(densify_kernel, topk=topk, latents=latents, lanes=lanes),
        out_shape=jax.ShapeDtypeStruct((rows, latents), jnp.bfloat16),
        in_specs=[pl.BlockSpec(memory_space=pltpu.SMEM)]
        + [pl.BlockSpec(memory_space=pltpu.VMEM) for _ in packed],
        out_specs=pl.BlockSpec(memory_space=pltpu.VMEM),
        compiler_params=pltpu.CompilerParams(vmem_limit_bytes=VMEM_BYTES),
        cost_estimate=pl.CostEstimate(
            flops=rows * latents * width, bytes_accessed=rows * latents * 2, transcendentals=0
        ),
        name="densify",
    )(base, *packed)


def decode_kernel(codes_ref, weights_ref, *rest):
    out_ref = rest[-1]
    out_ref[...] = jnp.dot(codes_ref[...], weights_ref[...], preferred_element_type=jnp.float32)


def decode(codes, decoder, first, count, into=None):
    rows, latents = codes.shape
    columns = decoder.shape[1]
    width = math.gcd(columns, 256)
    here = pl.BlockSpec((rows, width), lambda n: (0, first + n))
    operands = [codes, decoder] + ([] if into is None else [into])
    return pl.pallas_call(
        decode_kernel,
        out_shape=jax.ShapeDtypeStruct((rows, columns), jnp.float32),
        grid=(count,),
        in_specs=[
            pl.BlockSpec((rows, latents), lambda n: (0, 0)),
            pl.BlockSpec((latents, width), lambda n: (0, first + n)),
        ]
        + ([] if into is None else [pl.BlockSpec(memory_space=pl.ANY)]),
        out_specs=here,
        input_output_aliases={} if into is None else {2: 0},
        compiler_params=pltpu.CompilerParams(vmem_limit_bytes=DECODE_BYTES),
        cost_estimate=SMALL,
        name="decode",
    )(*operands)


def copy_kernel(order_ref, from_ref, to_ref):
    to_ref[...] = from_ref[...].reshape(to_ref.shape)


def select_columns(weights, order, width):
    kinds, depth = weights.shape[:2]
    count = order.shape[0]
    return pl.pallas_call(
        copy_kernel,
        out_shape=jax.ShapeDtypeStruct((depth, count * kinds * width), weights.dtype),
        grid_spec=pltpu.PrefetchScalarGridSpec(
            num_scalar_prefetch=1,
            grid=(count, kinds),
            in_specs=[pl.BlockSpec((1, depth, width), lambda j, t, order: (t, 0, order[j]))],
            out_specs=pl.BlockSpec((depth, width), lambda j, t, order: (0, j * kinds + t)),
        ),
        compiler_params=pltpu.CompilerParams(vmem_limit_bytes=VMEM_BYTES),
        cost_estimate=pl.CostEstimate(
            flops=0, bytes_accessed=4 * depth * count * kinds * width, transcendentals=0
        ),
        name="select_columns",
    )(order, weights)


def select_rows(weights, order, height):
    columns, count = weights.shape[1], order.shape[0]
    return pl.pallas_call(
        copy_kernel,
        out_shape=jax.ShapeDtypeStruct((count * height, columns), weights.dtype),
        grid_spec=pltpu.PrefetchScalarGridSpec(
            num_scalar_prefetch=1,
            grid=(count,),
            in_specs=[pl.BlockSpec((height, columns), lambda j, order: (order[j], 0))],
            out_specs=pl.BlockSpec((height, columns), lambda j, order: (j, 0)),
        ),
        compiler_params=pltpu.CompilerParams(vmem_limit_bytes=VMEM_BYTES),
        cost_estimate=pl.CostEstimate(
            flops=0, bytes_accessed=4 * count * height * columns, transcendentals=0
        ),
        name="select_rows",
    )(order, weights)


def attend_kernel(*refs, heads, slots, group):
    query_pos, key_pos = refs[0], refs[1]
    new = refs[2 : 2 + slots]
    cached = refs[2 + slots : -1]
    out = refs[-1]
    width = heads * HEAD
    hidden = key_pos[...] > query_pos[...]
    for h in range(heads):
        here = slice(h * HEAD, (h + 1) * HEAD)
        keys = [c[0, :, here] for c in cached] + [
            n[:, width + h * HEAD : width + (h + 1) * HEAD] for n in new
        ]
        values = [c[1, :, here] for c in cached] + [
            n[:, 2 * width + h * HEAD : 2 * width + (h + 1) * HEAD] for n in new
        ]
        keys = jnp.concatenate(keys, axis=0)
        values = jnp.concatenate(values, axis=0)
        scores = lax.dot_general(
            jnp.concatenate([new[s][:, here] for s in group], axis=0), keys, (((1,), (1,)), ((), ())), preferred_element_type=jnp.float32
        ) * (1.0 / math.sqrt(HEAD))
        cut = scores.shape[1] - hidden.shape[1]
        old, fresh = scores[:, :cut], jnp.where(hidden, -1e30, scores[:, cut:])
        highest = jnp.maximum(
            jnp.max(old, axis=1, keepdims=True), jnp.max(fresh, axis=1, keepdims=True)
        )
        old, fresh = jnp.exp(old - highest), jnp.exp(fresh - highest)
        total = jnp.sum(old, axis=1, keepdims=True) + jnp.sum(fresh, axis=1, keepdims=True)
        scale = 1.0 / total
        probs = jnp.concatenate(
            [(old * scale).astype(jnp.bfloat16), (fresh * scale).astype(jnp.bfloat16)], axis=1
        )
        mixed = jnp.dot(probs, values, preferred_element_type=jnp.float32)
        out[:, here] = mixed.astype(jnp.bfloat16)


def attend(query_pos, key_pos, new, cached, group, heads):
    slot_rows = new[0].shape[0]
    rows = slot_rows * len(group)
    keys = slot_rows * len(new) + sum(c.shape[1] for c in cached)
    vmem = pl.BlockSpec(memory_space=pltpu.VMEM)
    return pl.pallas_call(
        functools.partial(attend_kernel, heads=heads, slots=len(new), group=group),
        out_shape=jax.ShapeDtypeStruct((rows, heads * HEAD), jnp.bfloat16),
        in_specs=[vmem] * (2 + len(new) + len(cached)),
        out_specs=vmem,
        compiler_params=pltpu.CompilerParams(vmem_limit_bytes=VMEM_BYTES),
        cost_estimate=pl.CostEstimate(
            flops=4 * rows * keys * heads * HEAD,
            bytes_accessed=keys * heads * HEAD * 4,
            transcendentals=rows * keys * heads,
        ),
        name="attend",
    )(query_pos, key_pos, *new, *cached)


PAIRS = [(0, 1), (1, 0), (2, 3), (3, 2)]
INWARD = [(0, 1), (3, 2)]
MIDDLE = [(1, 2), (2, 1)]
OUTWARD = [(1, 0), (2, 3)]


def line_slots(index):
    low = index < 2
    return [index, index ^ 1, jnp.where(low, 2, 1), jnp.where(low, 3, 0)]


def line_gather_direct(own, outer):
    near = lax.ppermute(own, "lat", [(i, i ^ 1) for i in range(4)])
    two = lax.ppermute(own, "lat", [(i, i ^ 2) for i in range(4)])
    three = lax.ppermute(own, "lat", [(i, i ^ 3) for i in range(4)])
    return [own, near, jnp.where(outer, two, three), jnp.where(outer, three, two)]


def swap(value, distance, size):
    return lax.ppermute(value, "col", [(i, i ^ distance) for i in range(size)])


def normalize(values, sums, gain, shift):
    row_mean = sums[0] / D
    row_var = sums[1] / D - row_mean * row_mean
    inverse = 1.0 / jnp.sqrt(row_var + 1e-05)
    return ((values - row_mean[:, None]) * inverse[:, None] * gain + shift).astype(jnp.bfloat16)


def pack(code_ids, code_vals):
    rows, topk = code_ids.shape
    vals = code_vals.astype(jnp.bfloat16).astype(jnp.float32)
    shape = (rows // GROUP, GROUP * topk)
    return jnp.concatenate([code_ids.astype(jnp.float32).reshape(shape), vals.reshape(shape)], axis=1)


SCALE = 256.0


def to_half(value):
    return (value * SCALE).astype(jnp.float16)


def from_half(value):
    return value.astype(jnp.float32) * (1.0 / SCALE)


def line_body(
    code_ids, code_vals, decoder, dec_bias, ln_gain, ln_bias, w_qkv, cache_kv, positions, w_out
):
    lat = lax.axis_index("lat")
    col = lax.axis_index("col")
    cols = lax.axis_size("col")
    rows, topk = code_ids.shape
    latents, columns = decoder.shape
    head_width = w_qkv.shape[2]
    own_width = head_width // cols
    heads = own_width // HEAD
    outer = (lat == 0) | (lat == 3)
    slots = line_slots(lat)
    hold = lax.optimization_barrier

    packed = pack(code_ids, code_vals)
    packed = line_gather_direct(packed, outer)
    base = (lat * latents).reshape(1)

    def cache_of(j):
        start = (col ^ j) * own_width
        return lax.dynamic_slice_in_dim(cache_kv, start, own_width, 2)

    across = swap(jnp.stack([cache_of(2), cache_of(3)]), 2, cols)

    key_pos = jnp.concatenate(
        [lax.dynamic_slice_in_dim(positions, s * rows, rows, 0) for s in slots]
    )
    query_pos = key_pos.reshape(-1, 1)

    codes_far = densify([packed[3], packed[2]], base, topk, latents)
    far = jnp.dot(codes_far, decoder, preferred_element_type=jnp.float32)
    near_packed, sent = hold(((packed[1], packed[0]), to_half(far[:rows])))
    in_far = lax.ppermute(sent, "lat", INWARD)
    codes_near = densify(near_packed, base, topk, latents)
    blocks = columns // math.gcd(columns, 256)
    ahead = blocks * 2 // 5
    near = decode(codes_near, decoder, 0, ahead)
    near, in_far = hold((near, in_far))
    mid_far = to_half(far[:rows] + from_half(in_far))
    second, near, codes_near, across, query_pos, mid_far = hold(
        (far[rows:], near, codes_near, across, query_pos, mid_far)
    )
    mid_far = lax.ppermute(mid_far, "lat", MIDDLE)
    in_across = lax.ppermute(to_half(second), "lat", INWARD)
    near = decode(codes_near, decoder, ahead, blocks - ahead, into=near)
    near, mid_far, in_across = hold((near, mid_far, in_across))
    last = to_half(near[:rows] + from_half(mid_far))
    across, last, second, weights = hold((across, last, second, w_qkv.transpose(1, 0, 2)))
    last = lax.ppermute(last, "lat", PAIRS)
    mid_across = lax.ppermute(to_half(second + from_half(in_across)), "lat", MIDDLE)

    away_weights = select_columns(weights, jnp.stack([col ^ 1, col ^ 3]), own_width)
    keep_weights = select_columns(weights, jnp.stack([col, col ^ 2]), own_width)
    out_weights = select_rows(w_out, jnp.stack([col, col ^ 2, col ^ 1, col ^ 3]), own_width)
    beside = swap(jnp.stack([cache_of(1), across[1]]), 1, cols)
    last, away_weights, keep_weights, out_weights, beside = hold(
        (last, away_weights, keep_weights, out_weights, beside)
    )
    cached = [cache_of(0), across[0], beside[0], beside[1]]
    residual = near[rows:] + from_half(mid_across) + from_half(last)
    residual = residual + dec_bias.astype(jnp.float32)

    sums = jnp.stack([jnp.sum(residual, axis=1), jnp.sum(residual * residual, axis=1)])
    sums = sums + swap(sums, 1, cols)
    sums = sums + swap(sums, 2, cols)
    own = normalize(residual, sums, ln_gain, ln_bias)
    near = lax.ppermute(own, "lat", PAIRS)
    across = lax.ppermute(own, "lat", MIDDLE)
    far = lax.ppermute(near, "lat", MIDDLE)
    across_out = lax.ppermute(across, "lat", OUTWARD)
    far_out = lax.ppermute(far, "lat", OUTWARD)

    quarter = keep_weights.shape[1] // 2

    def project(block):
        away = jnp.dot(block, away_weights, preferred_element_type=jnp.float32).astype(jnp.float16)
        keep = jnp.dot(block, keep_weights, preferred_element_type=jnp.float32)
        keep = keep + swap(away, 1, cols).astype(jnp.float32)
        return keep[:, :quarter], keep[:, quarter:].astype(jnp.float16)

    def finish(keep, payload):
        return (keep + swap(payload, 2, cols).astype(jnp.float32)).astype(jnp.bfloat16)

    keep0, payload0 = project(own)
    near_block, across, payload0 = hold((near, across, payload0))
    keep1, payload1 = project(near_block)
    third, far, payload1, first = hold(
        (jnp.where(outer, across_out, across), far, payload1, finish(keep0, payload0))
    )
    keep2, payload2 = project(third)
    second, payload2 = hold((finish(keep1, payload1), payload2))
    third = finish(keep2, payload2)
    fourth, third = hold((jnp.where(outer, far_out, far), third))
    qkv = [first, second, third, finish(*project(fourth))]

    key_row = key_pos.reshape(1, -1)

    def pos_of(a, b):
        return jnp.concatenate(
            [query_pos[a * rows : (a + 1) * rows], query_pos[b * rows : (b + 1) * rows]], axis=0
        )

    mixed_far = attend(pos_of(3, 2), key_row, qkv, cached, (3, 2), heads)
    near_pos, mixed_far = hold((pos_of(1, 0), mixed_far))
    mixed_near = attend(near_pos, key_row, qkv, cached, (1, 0), heads)
    swapped_far, mixed_near = hold((swap(mixed_far, 2, cols), mixed_near))
    mixed_far = jnp.concatenate([mixed_far, swapped_far], axis=1)
    mixed_far = jnp.concatenate([mixed_far, swap(mixed_far, 1, cols)], axis=1)
    product_far = jnp.dot(mixed_far, out_weights, preferred_element_type=jnp.float32)
    sent_far, mixed_near = hold((product_far[:rows].astype(jnp.bfloat16), mixed_near))
    in_far = lax.ppermute(sent_far, "lat", INWARD)
    mixed_near = jnp.concatenate([mixed_near, swap(mixed_near, 2, cols)], axis=1)
    mixed_near = jnp.concatenate([mixed_near, swap(mixed_near, 1, cols)], axis=1)
    product_near = jnp.dot(mixed_near, out_weights, preferred_element_type=jnp.float32)
    mid_far = (product_far[:rows] + in_far.astype(jnp.float32)).astype(jnp.bfloat16)
    second, mid_far = hold((product_far[rows:], mid_far))
    mid_far = lax.ppermute(mid_far, "lat", MIDDLE)
    in_across = lax.ppermute(second.astype(jnp.bfloat16), "lat", INWARD)
    last = (product_near[:rows] + mid_far.astype(jnp.float32)).astype(jnp.bfloat16)
    second, last = hold((second, last))
    last = lax.ppermute(last, "lat", PAIRS)
    mid_across = (second + in_across.astype(jnp.float32)).astype(jnp.bfloat16)
    mid_across = lax.ppermute(mid_across, "lat", MIDDLE)
    branch = product_near[rows:] + last.astype(jnp.float32)
    branch, mid_across = hold((residual + branch, mid_across))
    return (branch + mid_across.astype(jnp.float32)).astype(jnp.bfloat16)


def attend_block(queries, keys, values, query_pos, key_pos):
    heads = queries.shape[1] // HEAD
    query_heads = queries.reshape(queries.shape[0], heads, HEAD)
    key_heads = keys.reshape(keys.shape[0], heads, HEAD)
    value_heads = values.reshape(values.shape[0], heads, HEAD)
    scores = jnp.einsum(
        "qhe,khe->hqk", query_heads, key_heads, preferred_element_type=jnp.float32
    ) * (1.0 / math.sqrt(HEAD))
    visible = key_pos[None, None, :] <= query_pos[None, :, None]
    scores = jnp.where(visible, scores, -1e30)
    highest = jnp.max(scores, axis=-1, keepdims=True)
    expo = jnp.exp(scores - highest)
    probs = (expo / jnp.sum(expo, axis=-1, keepdims=True)).astype(jnp.bfloat16)
    mixed = jnp.einsum("hqk,khe->qhe", probs, value_heads, preferred_element_type=jnp.float32)
    return mixed.reshape(queries.shape[0], heads * HEAD).astype(jnp.bfloat16)


def general_body(
    code_ids, code_vals, decoder, dec_bias, ln_gain, ln_bias, w_qkv, cache_kv, positions, w_out
):
    lat_index = lax.axis_index("lat")
    col_total = lax.axis_size("col")
    col_index = lax.axis_index("col")
    rows, topk = code_ids.shape
    shard_latents = decoder.shape[0]
    packed = lax.all_gather(pack(code_ids, code_vals), "lat", axis=0, tiled=True)
    base = (lat_index * shard_latents).reshape(1)
    dense_codes = densify([packed], base, topk, shard_latents)
    total_rows = dense_codes.shape[0]
    col_rows = total_rows // col_total
    residual = lax.psum_scatter(
        jnp.dot(dense_codes, decoder, preferred_element_type=jnp.float32),
        "lat",
        scatter_dimension=0,
        tiled=True,
    ) + dec_bias.astype(jnp.float32)
    sums = lax.psum((jnp.sum(residual, axis=1), jnp.sum(residual * residual, axis=1)), "col")
    normed = lax.all_gather(normalize(residual, sums, ln_gain, ln_bias), "lat", axis=0, tiled=True)
    head_width = w_qkv.shape[2]
    w_flat = w_qkv.reshape(w_qkv.shape[0], 3 * head_width)
    own_rows = lax.psum_scatter(
        jnp.dot(normed, w_flat, preferred_element_type=jnp.float32),
        "col",
        scatter_dimension=0,
        tiled=True,
    ).astype(jnp.bfloat16)
    queries = own_rows[:, :head_width]
    new_kv = lax.all_gather(own_rows[:, head_width:], "col", axis=0, tiled=True)
    context = lax.all_gather(cache_kv, "col", axis=1, tiled=True)
    cached_len = context.shape[1]
    keys = jnp.concatenate([context[0], new_kv[:, :head_width]], axis=0)
    values = jnp.concatenate([context[1], new_kv[:, head_width:]], axis=0)
    key_pos = jnp.concatenate([jnp.arange(cached_len, dtype=jnp.int32), cached_len + positions])
    query_pos = cached_len + lax.dynamic_slice_in_dim(positions, col_index * col_rows, col_rows, 0)
    attended = attend_block(queries, keys, values, query_pos, key_pos)
    gathered = lax.all_gather(attended, "col", axis=0, tiled=True)
    branch_out = lax.psum_scatter(
        jnp.dot(gathered, w_out, preferred_element_type=jnp.float32).astype(jnp.bfloat16),
        "lat",
        scatter_dimension=0,
        tiled=True,
    ).astype(jnp.float32)
    return (residual + branch_out).astype(jnp.bfloat16)


def solution(mesh):
    def program(*args):
        lats, cols = mesh.shape["lat"], mesh.shape["col"]
        heads = args[6].shape[2] // HEAD // lats
        fits = lats == 4 and cols == 4 and heads % cols == 0
        return jax.shard_map(
            line_body if fits else general_body,
            mesh=mesh,
            in_specs=(
                P(("ckpt", "lat"), None),
                P(("ckpt", "lat"), None),
                P(("ckpt", "lat"), "col"),
                P(("ckpt", "col")),
                P(("ckpt", "col")),
                P(("ckpt", "col")),
                P(("ckpt", "col"), None, "lat"),
                P(None, ("ckpt", "col"), "lat"),
                P("ckpt"),
                P(("ckpt", "lat"), "col"),
            ),
            out_specs=P(("ckpt", "lat"), "col"),
            check_vma=False,
        )(*args)

    return program
```

```python
import functools
import math

import jax
import jax.numpy as jnp
from jax import lax
from jax.experimental import pallas as pl
from jax.experimental.pallas import tpu as pltpu
from jax.sharding import PartitionSpec as P

D = 5120
HEAD = 128
GROUP = 8
VMEM_BYTES = 20 * 1024 * 1024
DECODE_BYTES = 44 * 1024 * 1024
SMALL = pl.CostEstimate(flops=1, bytes_accessed=1, transcendentals=0)


def densify_kernel(base_ref, *refs, topk, latents, lanes):
    packed, out_ref = refs[:-1], refs[-1]
    groups, width = packed[0].shape[0], packed[0].shape[1] // 2
    high = latents // lanes
    base = base_ref[0]
    row_of = lax.broadcasted_iota(jnp.int32, (1, width), 1) // topk
    sub = lax.broadcasted_iota(jnp.int32, (high * GROUP, width), 0)
    sub = sub.astype(jnp.float32).astype(jnp.bfloat16)
    low_sub = lax.broadcasted_iota(jnp.int32, (lanes, width), 0)
    low_sub = low_sub.astype(jnp.float32).astype(jnp.bfloat16)
    one, zero = jnp.ones((), jnp.bfloat16), jnp.zeros((), jnp.bfloat16)

    def half(value):
        return value.astype(jnp.float32).astype(jnp.bfloat16)

    def one_group(ref, g):
        local = ref[pl.ds(g, 1), :width].astype(jnp.int32) - base
        inside = (local >= 0) & (local < latents)
        key = half(jnp.where(inside, (local // lanes) * GROUP + row_of, -1))
        low = half(jnp.where(inside, local % lanes, -1))
        vals = ref[pl.ds(g, 1), width:].astype(jnp.bfloat16)
        left = jnp.where(key == sub, vals, zero)
        right = jnp.where(low == low_sub, one, zero)
        dense = lax.dot_general(
            left, right, (((1,), (1,)), ((), ())), preferred_element_type=jnp.float32
        )
        return dense.reshape(high, GROUP, lanes)

    for at, ref in enumerate(packed):

        def pair(i, carry, at=at, ref=ref):
            both = jnp.concatenate([one_group(ref, 2 * i), one_group(ref, 2 * i + 1)], axis=1)
            both = both.astype(jnp.bfloat16)
            start = pl.multiple_of(i * 2 * GROUP, 2 * GROUP) + at * groups * GROUP
            for h in range(high):
                out_ref[pl.ds(start, 2 * GROUP), h * lanes : (h + 1) * lanes] = both[h]
            return carry

        lax.fori_loop(0, groups // 2, pair, 0)


def densify(packed, base, topk, latents):
    groups, width = packed[0].shape
    lanes = 256 if latents % 256 == 0 else 128
    rows = groups * GROUP * len(packed)
    return pl.pallas_call(
        functools.partial(densify_kernel, topk=topk, latents=latents, lanes=lanes),
        out_shape=jax.ShapeDtypeStruct((rows, latents), jnp.bfloat16),
        in_specs=[pl.BlockSpec(memory_space=pltpu.SMEM)]
        + [pl.BlockSpec(memory_space=pltpu.VMEM) for _ in packed],
        out_specs=pl.BlockSpec(memory_space=pltpu.VMEM),
        compiler_params=pltpu.CompilerParams(vmem_limit_bytes=VMEM_BYTES),
        cost_estimate=pl.CostEstimate(
            flops=rows * latents * width, bytes_accessed=rows * latents * 2, transcendentals=0
        ),
        name="densify",
    )(base, *packed)


def decode_kernel(codes_ref, weights_ref, *rest):
    out_ref = rest[-1]
    out_ref[...] = jnp.dot(codes_ref[...], weights_ref[...], preferred_element_type=jnp.float32)


def decode(codes, decoder, first, count, into=None):
    rows, latents = codes.shape
    columns = decoder.shape[1]
    width = math.gcd(columns, 256)
    here = pl.BlockSpec((rows, width), lambda n: (0, first + n))
    operands = [codes, decoder] + ([] if into is None else [into])
    return pl.pallas_call(
        decode_kernel,
        out_shape=jax.ShapeDtypeStruct((rows, columns), jnp.float32),
        grid=(count,),
        in_specs=[
            pl.BlockSpec((rows, latents), lambda n: (0, 0)),
            pl.BlockSpec((latents, width), lambda n: (0, first + n)),
        ]
        + ([] if into is None else [pl.BlockSpec(memory_space=pl.ANY)]),
        out_specs=here,
        input_output_aliases={} if into is None else {2: 0},
        compiler_params=pltpu.CompilerParams(vmem_limit_bytes=DECODE_BYTES),
        cost_estimate=SMALL,
        name="decode",
    )(*operands)


def copy_kernel(order_ref, from_ref, to_ref):
    to_ref[...] = from_ref[...].reshape(to_ref.shape)


def select_columns(weights, order, width):
    kinds, depth = weights.shape[:2]
    count = order.shape[0]
    return pl.pallas_call(
        copy_kernel,
        out_shape=jax.ShapeDtypeStruct((depth, count * kinds * width), weights.dtype),
        grid_spec=pltpu.PrefetchScalarGridSpec(
            num_scalar_prefetch=1,
            grid=(count, kinds),
            in_specs=[pl.BlockSpec((1, depth, width), lambda j, t, order: (t, 0, order[j]))],
            out_specs=pl.BlockSpec((depth, width), lambda j, t, order: (0, j * kinds + t)),
        ),
        compiler_params=pltpu.CompilerParams(vmem_limit_bytes=VMEM_BYTES),
        cost_estimate=pl.CostEstimate(
            flops=0, bytes_accessed=4 * depth * count * kinds * width, transcendentals=0
        ),
        name="select_columns",
    )(order, weights)


def select_rows(weights, order, height):
    columns, count = weights.shape[1], order.shape[0]
    return pl.pallas_call(
        copy_kernel,
        out_shape=jax.ShapeDtypeStruct((count * height, columns), weights.dtype),
        grid_spec=pltpu.PrefetchScalarGridSpec(
            num_scalar_prefetch=1,
            grid=(count,),
            in_specs=[pl.BlockSpec((height, columns), lambda j, order: (order[j], 0))],
            out_specs=pl.BlockSpec((height, columns), lambda j, order: (j, 0)),
        ),
        compiler_params=pltpu.CompilerParams(vmem_limit_bytes=VMEM_BYTES),
        cost_estimate=pl.CostEstimate(
            flops=0, bytes_accessed=4 * count * height * columns, transcendentals=0
        ),
        name="select_rows",
    )(order, weights)


def attend_kernel(*refs, heads, slots, group):
    query_pos, key_pos = refs[0], refs[1]
    new = refs[2 : 2 + slots]
    cached = refs[2 + slots : -1]
    out = refs[-1]
    width = heads * HEAD
    hidden = key_pos[...] > query_pos[...]
    for h in range(heads):
        here = slice(h * HEAD, (h + 1) * HEAD)
        keys = [c[0, :, here] for c in cached] + [
            n[:, width + h * HEAD : width + (h + 1) * HEAD] for n in new
        ]
        values = [c[1, :, here] for c in cached] + [
            n[:, 2 * width + h * HEAD : 2 * width + (h + 1) * HEAD] for n in new
        ]
        keys = jnp.concatenate(keys, axis=0)
        values = jnp.concatenate(values, axis=0)
        scores = lax.dot_general(
            jnp.concatenate([new[s][:, here] for s in group], axis=0), keys, (((1,), (1,)), ((), ())), preferred_element_type=jnp.float32
        ) * (1.0 / math.sqrt(HEAD))
        cut = scores.shape[1] - hidden.shape[1]
        old, fresh = scores[:, :cut], jnp.where(hidden, -1e30, scores[:, cut:])
        highest = jnp.maximum(
            jnp.max(old, axis=1, keepdims=True), jnp.max(fresh, axis=1, keepdims=True)
        )
        old, fresh = jnp.exp(old - highest), jnp.exp(fresh - highest)
        total = jnp.sum(old, axis=1, keepdims=True) + jnp.sum(fresh, axis=1, keepdims=True)
        scale = 1.0 / total
        probs = jnp.concatenate(
            [(old * scale).astype(jnp.bfloat16), (fresh * scale).astype(jnp.bfloat16)], axis=1
        )
        mixed = jnp.dot(probs, values, preferred_element_type=jnp.float32)
        out[:, here] = mixed.astype(jnp.bfloat16)


def attend(query_pos, key_pos, new, cached, group, heads):
    slot_rows = new[0].shape[0]
    rows = slot_rows * len(group)
    keys = slot_rows * len(new) + sum(c.shape[1] for c in cached)
    vmem = pl.BlockSpec(memory_space=pltpu.VMEM)
    return pl.pallas_call(
        functools.partial(attend_kernel, heads=heads, slots=len(new), group=group),
        out_shape=jax.ShapeDtypeStruct((rows, heads * HEAD), jnp.bfloat16),
        in_specs=[vmem] * (2 + len(new) + len(cached)),
        out_specs=vmem,
        compiler_params=pltpu.CompilerParams(vmem_limit_bytes=VMEM_BYTES),
        cost_estimate=pl.CostEstimate(
            flops=4 * rows * keys * heads * HEAD,
            bytes_accessed=keys * heads * HEAD * 4,
            transcendentals=rows * keys * heads,
        ),
        name="attend",
    )(query_pos, key_pos, *new, *cached)


PAIRS = [(0, 1), (1, 0), (2, 3), (3, 2)]
INWARD = [(0, 1), (3, 2)]
MIDDLE = [(1, 2), (2, 1)]
OUTWARD = [(1, 0), (2, 3)]


def line_slots(index):
    low = index < 2
    return [index, index ^ 1, jnp.where(low, 2, 1), jnp.where(low, 3, 0)]


def line_gather_direct(own, outer):
    near = lax.ppermute(own, "lat", [(i, i ^ 1) for i in range(4)])
    two = lax.ppermute(own, "lat", [(i, i ^ 2) for i in range(4)])
    three = lax.ppermute(own, "lat", [(i, i ^ 3) for i in range(4)])
    return [own, near, jnp.where(outer, two, three), jnp.where(outer, three, two)]


def swap(value, distance, size):
    return lax.ppermute(value, "col", [(i, i ^ distance) for i in range(size)])


def normalize(values, sums, gain, shift):
    row_mean = sums[0] / D
    row_var = sums[1] / D - row_mean * row_mean
    inverse = 1.0 / jnp.sqrt(row_var + 1e-05)
    return ((values - row_mean[:, None]) * inverse[:, None] * gain + shift).astype(jnp.bfloat16)


def pack(code_ids, code_vals):
    rows, topk = code_ids.shape
    vals = code_vals.astype(jnp.bfloat16).astype(jnp.float32)
    shape = (rows // GROUP, GROUP * topk)
    return jnp.concatenate([code_ids.astype(jnp.float32).reshape(shape), vals.reshape(shape)], axis=1)


SCALE = 256.0


def to_half(value):
    return (value * SCALE).astype(jnp.float16)


def from_half(value):
    return value.astype(jnp.float32) * (1.0 / SCALE)


def line_body(
    code_ids, code_vals, decoder, dec_bias, ln_gain, ln_bias, w_qkv, cache_kv, positions, w_out
):
    lat = lax.axis_index("lat")
    col = lax.axis_index("col")
    cols = lax.axis_size("col")
    rows, topk = code_ids.shape
    latents, columns = decoder.shape
    head_width = w_qkv.shape[2]
    own_width = head_width // cols
    heads = own_width // HEAD
    outer = (lat == 0) | (lat == 3)
    slots = line_slots(lat)
    hold = lax.optimization_barrier

    packed = pack(code_ids, code_vals)
    packed = line_gather_direct(packed, outer)
    base = (lat * latents).reshape(1)

    def cache_of(j):
        start = (col ^ j) * own_width
        return lax.dynamic_slice_in_dim(cache_kv, start, own_width, 2)

    across = swap(jnp.stack([cache_of(2), cache_of(3)]), 2, cols)

    key_pos = jnp.concatenate(
        [lax.dynamic_slice_in_dim(positions, s * rows, rows, 0) for s in slots]
    )
    query_pos = key_pos.reshape(-1, 1)

    codes_far = densify([packed[3], packed[2]], base, topk, latents)
    far = jnp.dot(codes_far, decoder, preferred_element_type=jnp.float32)
    near_packed, sent = hold(((packed[1], packed[0]), to_half(far[:rows])))
    in_far = lax.ppermute(sent, "lat", INWARD)
    codes_near = densify(near_packed, base, topk, latents)
    blocks = columns // math.gcd(columns, 256)
    ahead = blocks * 2 // 5
    near = decode(codes_near, decoder, 0, ahead)
    near, in_far = hold((near, in_far))
    mid_far = to_half(far[:rows] + from_half(in_far))
    second, near, codes_near, across, query_pos, mid_far = hold(
        (far[rows:], near, codes_near, across, query_pos, mid_far)
    )
    mid_far = lax.ppermute(mid_far, "lat", MIDDLE)
    in_across = lax.ppermute(to_half(second), "lat", INWARD)
    near = decode(codes_near, decoder, ahead, blocks - ahead, into=near)
    near, mid_far, in_across = hold((near, mid_far, in_across))
    last = to_half(near[:rows] + from_half(mid_far))
    across, last, second, weights = hold((across, last, second, w_qkv.transpose(1, 0, 2)))
    last = lax.ppermute(last, "lat", PAIRS)
    mid_across = lax.ppermute(to_half(second + from_half(in_across)), "lat", MIDDLE)

    away_weights = select_columns(weights, jnp.stack([col ^ 1, col ^ 3]), own_width)
    keep_weights = select_columns(weights, jnp.stack([col, col ^ 2]), own_width)
    out_weights = select_rows(w_out, jnp.stack([col, col ^ 2, col ^ 1, col ^ 3]), own_width)
    beside = swap(jnp.stack([cache_of(1), across[1]]), 1, cols)
    last, away_weights, keep_weights, out_weights, beside = hold(
        (last, away_weights, keep_weights, out_weights, beside)
    )
    cached = [cache_of(0), across[0], beside[0], beside[1]]
    residual = near[rows:] + from_half(mid_across) + from_half(last)
    residual = residual + dec_bias.astype(jnp.float32)

    sums = jnp.stack([jnp.sum(residual, axis=1), jnp.sum(residual * residual, axis=1)])
    sums = sums + swap(sums, 1, cols)
    sums = sums + swap(sums, 2, cols)
    own = normalize(residual, sums, ln_gain, ln_bias)
    near = lax.ppermute(own, "lat", PAIRS)
    across = lax.ppermute(own, "lat", MIDDLE)
    far = lax.ppermute(near, "lat", MIDDLE)
    across_out = lax.ppermute(across, "lat", OUTWARD)
    far_out = lax.ppermute(far, "lat", OUTWARD)

    quarter = keep_weights.shape[1] // 2

    def project(block):
        away = jnp.dot(block, away_weights, preferred_element_type=jnp.float32).astype(jnp.float16)
        keep = jnp.dot(block, keep_weights, preferred_element_type=jnp.float32)
        keep = keep + swap(away, 1, cols).astype(jnp.float32)
        return keep[:, :quarter], keep[:, quarter:].astype(jnp.float16)

    def finish(keep, payload):
        return (keep + swap(payload, 2, cols).astype(jnp.float32)).astype(jnp.bfloat16)

    keep0, payload0 = project(own)
    near_block, across, payload0 = hold((near, across, payload0))
    keep1, payload1 = project(near_block)
    third, far, payload1, first = hold(
        (jnp.where(outer, across_out, across), far, payload1, finish(keep0, payload0))
    )
    keep2, payload2 = project(third)
    second, payload2 = hold((finish(keep1, payload1), payload2))
    third = finish(keep2, payload2)
    fourth, third = hold((jnp.where(outer, far_out, far), third))
    qkv = [first, second, third, finish(*project(fourth))]

    key_row = key_pos.reshape(1, -1)

    def pos_of(a, b):
        return jnp.concatenate(
            [query_pos[a * rows : (a + 1) * rows], query_pos[b * rows : (b + 1) * rows]], axis=0
        )

    mixed_far = attend(pos_of(3, 2), key_row, qkv, cached, (3, 2), heads)
    near_pos, mixed_far = hold((pos_of(1, 0), mixed_far))
    mixed_near = attend(near_pos, key_row, qkv, cached, (1, 0), heads)
    swapped_far, mixed_near = hold((swap(mixed_far, 2, cols), mixed_near))
    mixed_far = jnp.concatenate([mixed_far, swapped_far], axis=1)
    mixed_far = jnp.concatenate([mixed_far, swap(mixed_far, 1, cols)], axis=1)
    product_far = jnp.dot(mixed_far, out_weights, preferred_element_type=jnp.float32)
    sent_far, mixed_near = hold((product_far[:rows].astype(jnp.bfloat16), mixed_near))
    in_far = lax.ppermute(sent_far, "lat", INWARD)
    mixed_near = jnp.concatenate([mixed_near, swap(mixed_near, 2, cols)], axis=1)
    mixed_near = jnp.concatenate([mixed_near, swap(mixed_near, 1, cols)], axis=1)
    product_near = jnp.dot(mixed_near, out_weights, preferred_element_type=jnp.float32)
    mid_far = (product_far[:rows] + in_far.astype(jnp.float32)).astype(jnp.bfloat16)
    second, mid_far = hold((product_far[rows:], mid_far))
    mid_far = lax.ppermute(mid_far, "lat", MIDDLE)
    in_across = lax.ppermute(second.astype(jnp.bfloat16), "lat", INWARD)
    product_near, mid_far, in_across = hold((product_near, mid_far, in_across))
    last = (product_near[:rows] + mid_far.astype(jnp.float32)).astype(jnp.bfloat16)
    last = lax.ppermute(last, "lat", PAIRS)
    mid_across = (second + in_across.astype(jnp.float32)).astype(jnp.bfloat16)
    mid_across = lax.ppermute(mid_across, "lat", MIDDLE)
    branch = product_near[rows:] + last.astype(jnp.float32) + mid_across.astype(jnp.float32)
    return (residual + branch).astype(jnp.bfloat16)


def attend_block(queries, keys, values, query_pos, key_pos):
    heads = queries.shape[1] // HEAD
    query_heads = queries.reshape(queries.shape[0], heads, HEAD)
    key_heads = keys.reshape(keys.shape[0], heads, HEAD)
    value_heads = values.reshape(values.shape[0], heads, HEAD)
    scores = jnp.einsum(
        "qhe,khe->hqk", query_heads, key_heads, preferred_element_type=jnp.float32
    ) * (1.0 / math.sqrt(HEAD))
    visible = key_pos[None, None, :] <= query_pos[None, :, None]
    scores = jnp.where(visible, scores, -1e30)
    highest = jnp.max(scores, axis=-1, keepdims=True)
    expo = jnp.exp(scores - highest)
    probs = (expo / jnp.sum(expo, axis=-1, keepdims=True)).astype(jnp.bfloat16)
    mixed = jnp.einsum("hqk,khe->qhe", probs, value_heads, preferred_element_type=jnp.float32)
    return mixed.reshape(queries.shape[0], heads * HEAD).astype(jnp.bfloat16)


def general_body(
    code_ids, code_vals, decoder, dec_bias, ln_gain, ln_bias, w_qkv, cache_kv, positions, w_out
):
    lat_index = lax.axis_index("lat")
    col_total = lax.axis_size("col")
    col_index = lax.axis_index("col")
    rows, topk = code_ids.shape
    shard_latents = decoder.shape[0]
    packed = lax.all_gather(pack(code_ids, code_vals), "lat", axis=0, tiled=True)
    base = (lat_index * shard_latents).reshape(1)
    dense_codes = densify([packed], base, topk, shard_latents)
    total_rows = dense_codes.shape[0]
    col_rows = total_rows // col_total
    residual = lax.psum_scatter(
        jnp.dot(dense_codes, decoder, preferred_element_type=jnp.float32),
        "lat",
        scatter_dimension=0,
        tiled=True,
    ) + dec_bias.astype(jnp.float32)
    sums = lax.psum((jnp.sum(residual, axis=1), jnp.sum(residual * residual, axis=1)), "col")
    normed = lax.all_gather(normalize(residual, sums, ln_gain, ln_bias), "lat", axis=0, tiled=True)
    head_width = w_qkv.shape[2]
    w_flat = w_qkv.reshape(w_qkv.shape[0], 3 * head_width)
    own_rows = lax.psum_scatter(
        jnp.dot(normed, w_flat, preferred_element_type=jnp.float32),
        "col",
        scatter_dimension=0,
        tiled=True,
    ).astype(jnp.bfloat16)
    queries = own_rows[:, :head_width]
    new_kv = lax.all_gather(own_rows[:, head_width:], "col", axis=0, tiled=True)
    context = lax.all_gather(cache_kv, "col", axis=1, tiled=True)
    cached_len = context.shape[1]
    keys = jnp.concatenate([context[0], new_kv[:, :head_width]], axis=0)
    values = jnp.concatenate([context[1], new_kv[:, head_width:]], axis=0)
    key_pos = jnp.concatenate([jnp.arange(cached_len, dtype=jnp.int32), cached_len + positions])
    query_pos = cached_len + lax.dynamic_slice_in_dim(positions, col_index * col_rows, col_rows, 0)
    attended = attend_block(queries, keys, values, query_pos, key_pos)
    gathered = lax.all_gather(attended, "col", axis=0, tiled=True)
    branch_out = lax.psum_scatter(
        jnp.dot(gathered, w_out, preferred_element_type=jnp.float32).astype(jnp.bfloat16),
        "lat",
        scatter_dimension=0,
        tiled=True,
    ).astype(jnp.float32)
    return (residual + branch_out).astype(jnp.bfloat16)


def solution(mesh):
    def program(*args):
        lats, cols = mesh.shape["lat"], mesh.shape["col"]
        heads = args[6].shape[2] // HEAD // lats
        fits = lats == 4 and cols == 4 and heads % cols == 0
        return jax.shard_map(
            line_body if fits else general_body,
            mesh=mesh,
            in_specs=(
                P(("ckpt", "lat"), None),
                P(("ckpt", "lat"), None),
                P(("ckpt", "lat"), "col"),
                P(("ckpt", "col")),
                P(("ckpt", "col")),
                P(("ckpt", "col")),
                P(("ckpt", "col"), None, "lat"),
                P(None, ("ckpt", "col"), "lat"),
                P("ckpt"),
                P(("ckpt", "lat"), "col"),
            ),
            out_specs=P(("ckpt", "lat"), "col"),
            check_vma=False,
        )(*args)

    return program
```

```python
import functools
import math

import jax
import jax.numpy as jnp
from jax import lax
from jax.experimental import pallas as pl
from jax.experimental.pallas import tpu as pltpu
from jax.sharding import PartitionSpec as P

D = 5120
HEAD = 128
GROUP = 8
VMEM_BYTES = 20 * 1024 * 1024
DECODE_BYTES = 44 * 1024 * 1024
SMALL = pl.CostEstimate(flops=1, bytes_accessed=1, transcendentals=0)


def densify_kernel(base_ref, *refs, topk, latents, lanes):
    packed, out_ref = refs[:-1], refs[-1]
    groups, width = packed[0].shape[0], packed[0].shape[1] // 2
    high = latents // lanes
    base = base_ref[0]
    row_of = lax.broadcasted_iota(jnp.int32, (1, width), 1) // topk
    sub = lax.broadcasted_iota(jnp.int32, (high * GROUP, width), 0)
    sub = sub.astype(jnp.float32).astype(jnp.bfloat16)
    low_sub = lax.broadcasted_iota(jnp.int32, (lanes, width), 0)
    low_sub = low_sub.astype(jnp.float32).astype(jnp.bfloat16)
    one, zero = jnp.ones((), jnp.bfloat16), jnp.zeros((), jnp.bfloat16)

    def half(value):
        return value.astype(jnp.float32).astype(jnp.bfloat16)

    def one_group(ref, g):
        local = ref[pl.ds(g, 1), :width].astype(jnp.int32) - base
        inside = (local >= 0) & (local < latents)
        key = half(jnp.where(inside, (local // lanes) * GROUP + row_of, -1))
        low = half(jnp.where(inside, local % lanes, -1))
        vals = ref[pl.ds(g, 1), width:].astype(jnp.bfloat16)
        left = jnp.where(key == sub, vals, zero)
        right = jnp.where(low == low_sub, one, zero)
        dense = lax.dot_general(
            left, right, (((1,), (1,)), ((), ())), preferred_element_type=jnp.float32
        )
        return dense.reshape(high, GROUP, lanes)

    for at, ref in enumerate(packed):

        def pair(i, carry, at=at, ref=ref):
            both = jnp.concatenate([one_group(ref, 2 * i), one_group(ref, 2 * i + 1)], axis=1)
            both = both.astype(jnp.bfloat16)
            start = pl.multiple_of(i * 2 * GROUP, 2 * GROUP) + at * groups * GROUP
            for h in range(high):
                out_ref[pl.ds(start, 2 * GROUP), h * lanes : (h + 1) * lanes] = both[h]
            return carry

        lax.fori_loop(0, groups // 2, pair, 0)


def densify(packed, base, topk, latents):
    groups, width = packed[0].shape
    lanes = 256 if latents % 256 == 0 else 128
    rows = groups * GROUP * len(packed)
    return pl.pallas_call(
        functools.partial(densify_kernel, topk=topk, latents=latents, lanes=lanes),
        out_shape=jax.ShapeDtypeStruct((rows, latents), jnp.bfloat16),
        in_specs=[pl.BlockSpec(memory_space=pltpu.SMEM)]
        + [pl.BlockSpec(memory_space=pltpu.VMEM) for _ in packed],
        out_specs=pl.BlockSpec(memory_space=pltpu.VMEM),
        compiler_params=pltpu.CompilerParams(vmem_limit_bytes=VMEM_BYTES),
        cost_estimate=pl.CostEstimate(
            flops=rows * latents * width, bytes_accessed=rows * latents * 2, transcendentals=0
        ),
        name="densify",
    )(base, *packed)


def decode_kernel(codes_ref, weights_ref, *rest):
    out_ref = rest[-1]
    out_ref[...] = jnp.dot(codes_ref[...], weights_ref[...], preferred_element_type=jnp.float32)


def decode(codes, decoder, first, count, into=None):
    rows, latents = codes.shape
    columns = decoder.shape[1]
    width = math.gcd(columns, 256)
    here = pl.BlockSpec((rows, width), lambda n: (0, first + n))
    operands = [codes, decoder] + ([] if into is None else [into])
    return pl.pallas_call(
        decode_kernel,
        out_shape=jax.ShapeDtypeStruct((rows, columns), jnp.float32),
        grid=(count,),
        in_specs=[
            pl.BlockSpec((rows, latents), lambda n: (0, 0)),
            pl.BlockSpec((latents, width), lambda n: (0, first + n)),
        ]
        + ([] if into is None else [pl.BlockSpec(memory_space=pl.ANY)]),
        out_specs=here,
        input_output_aliases={} if into is None else {2: 0},
        compiler_params=pltpu.CompilerParams(vmem_limit_bytes=DECODE_BYTES),
        cost_estimate=SMALL,
        name="decode",
    )(*operands)


def copy_kernel(order_ref, from_ref, to_ref):
    to_ref[...] = from_ref[...].reshape(to_ref.shape)


def select_columns(weights, order, width):
    kinds, depth = weights.shape[:2]
    count = order.shape[0]
    return pl.pallas_call(
        copy_kernel,
        out_shape=jax.ShapeDtypeStruct((depth, count * kinds * width), weights.dtype),
        grid_spec=pltpu.PrefetchScalarGridSpec(
            num_scalar_prefetch=1,
            grid=(count, kinds),
            in_specs=[pl.BlockSpec((1, depth, width), lambda j, t, order: (t, 0, order[j]))],
            out_specs=pl.BlockSpec((depth, width), lambda j, t, order: (0, j * kinds + t)),
        ),
        compiler_params=pltpu.CompilerParams(vmem_limit_bytes=VMEM_BYTES),
        cost_estimate=pl.CostEstimate(
            flops=0, bytes_accessed=4 * depth * count * kinds * width, transcendentals=0
        ),
        name="select_columns",
    )(order, weights)


def select_rows(weights, order, height):
    columns, count = weights.shape[1], order.shape[0]
    return pl.pallas_call(
        copy_kernel,
        out_shape=jax.ShapeDtypeStruct((count * height, columns), weights.dtype),
        grid_spec=pltpu.PrefetchScalarGridSpec(
            num_scalar_prefetch=1,
            grid=(count,),
            in_specs=[pl.BlockSpec((height, columns), lambda j, order: (order[j], 0))],
            out_specs=pl.BlockSpec((height, columns), lambda j, order: (j, 0)),
        ),
        compiler_params=pltpu.CompilerParams(vmem_limit_bytes=VMEM_BYTES),
        cost_estimate=pl.CostEstimate(
            flops=0, bytes_accessed=4 * count * height * columns, transcendentals=0
        ),
        name="select_rows",
    )(order, weights)


def attend_kernel(*refs, heads, slots, group):
    query_pos, key_pos = refs[0], refs[1]
    new = refs[2 : 2 + slots]
    cached = refs[2 + slots : -1]
    out = refs[-1]
    width = heads * HEAD
    hidden = key_pos[...] > query_pos[...]
    for h in range(heads):
        here = slice(h * HEAD, (h + 1) * HEAD)
        keys = [c[0, :, here] for c in cached] + [
            n[:, width + h * HEAD : width + (h + 1) * HEAD] for n in new
        ]
        values = [c[1, :, here] for c in cached] + [
            n[:, 2 * width + h * HEAD : 2 * width + (h + 1) * HEAD] for n in new
        ]
        keys = jnp.concatenate(keys, axis=0)
        values = jnp.concatenate(values, axis=0)
        scores = lax.dot_general(
            jnp.concatenate([new[s][:, here] for s in group], axis=0), keys, (((1,), (1,)), ((), ())), preferred_element_type=jnp.float32
        ) * (1.0 / math.sqrt(HEAD))
        cut = scores.shape[1] - hidden.shape[1]
        old, fresh = scores[:, :cut], jnp.where(hidden, -1e30, scores[:, cut:])
        highest = jnp.maximum(
            jnp.max(old, axis=1, keepdims=True), jnp.max(fresh, axis=1, keepdims=True)
        )
        old, fresh = jnp.exp(old - highest), jnp.exp(fresh - highest)
        total = jnp.sum(old, axis=1, keepdims=True) + jnp.sum(fresh, axis=1, keepdims=True)
        scale = 1.0 / total
        probs = jnp.concatenate(
            [(old * scale).astype(jnp.bfloat16), (fresh * scale).astype(jnp.bfloat16)], axis=1
        )
        mixed = jnp.dot(probs, values, preferred_element_type=jnp.float32)
        out[:, here] = mixed.astype(jnp.bfloat16)


def attend(query_pos, key_pos, new, cached, group, heads):
    slot_rows = new[0].shape[0]
    rows = slot_rows * len(group)
    keys = slot_rows * len(new) + sum(c.shape[1] for c in cached)
    vmem = pl.BlockSpec(memory_space=pltpu.VMEM)
    return pl.pallas_call(
        functools.partial(attend_kernel, heads=heads, slots=len(new), group=group),
        out_shape=jax.ShapeDtypeStruct((rows, heads * HEAD), jnp.bfloat16),
        in_specs=[vmem] * (2 + len(new) + len(cached)),
        out_specs=vmem,
        compiler_params=pltpu.CompilerParams(vmem_limit_bytes=VMEM_BYTES),
        cost_estimate=pl.CostEstimate(
            flops=4 * rows * keys * heads * HEAD,
            bytes_accessed=keys * heads * HEAD * 4,
            transcendentals=rows * keys * heads,
        ),
        name="attend",
    )(query_pos, key_pos, *new, *cached)


PAIRS = [(0, 1), (1, 0), (2, 3), (3, 2)]
INWARD = [(0, 1), (3, 2)]
MIDDLE = [(1, 2), (2, 1)]
OUTWARD = [(1, 0), (2, 3)]


def line_slots(index):
    low = index < 2
    return [index, index ^ 1, jnp.where(low, 2, 1), jnp.where(low, 3, 0)]


def line_gather_direct(own, outer):
    near = lax.ppermute(own, "lat", [(i, i ^ 1) for i in range(4)])
    two = lax.ppermute(own, "lat", [(i, i ^ 2) for i in range(4)])
    three = lax.ppermute(own, "lat", [(i, i ^ 3) for i in range(4)])
    return [own, near, jnp.where(outer, two, three), jnp.where(outer, three, two)]


def swap(value, distance, size):
    return lax.ppermute(value, "col", [(i, i ^ distance) for i in range(size)])


def normalize(values, sums, gain, shift):
    row_mean = sums[0] / D
    row_var = sums[1] / D - row_mean * row_mean
    inverse = 1.0 / jnp.sqrt(row_var + 1e-05)
    return ((values - row_mean[:, None]) * inverse[:, None] * gain + shift).astype(jnp.bfloat16)


def pack(code_ids, code_vals):
    rows, topk = code_ids.shape
    vals = code_vals.astype(jnp.bfloat16).astype(jnp.float32)
    shape = (rows // GROUP, GROUP * topk)
    return jnp.concatenate([code_ids.astype(jnp.float32).reshape(shape), vals.reshape(shape)], axis=1)


SCALE = 256.0


def to_half(value):
    return (value * SCALE).astype(jnp.float16)


def from_half(value):
    return value.astype(jnp.float32) * (1.0 / SCALE)


def line_body(
    code_ids, code_vals, decoder, dec_bias, ln_gain, ln_bias, w_qkv, cache_kv, positions, w_out
):
    lat = lax.axis_index("lat")
    col = lax.axis_index("col")
    cols = lax.axis_size("col")
    rows, topk = code_ids.shape
    latents, columns = decoder.shape
    head_width = w_qkv.shape[2]
    own_width = head_width // cols
    heads = own_width // HEAD
    outer = (lat == 0) | (lat == 3)
    slots = line_slots(lat)
    hold = lax.optimization_barrier

    packed = pack(code_ids, code_vals)
    packed = line_gather_direct(packed, outer)
    base = (lat * latents).reshape(1)

    def cache_of(j):
        start = (col ^ j) * own_width
        return lax.dynamic_slice_in_dim(cache_kv, start, own_width, 2)

    across = swap(jnp.stack([cache_of(2), cache_of(3)]), 2, cols)

    key_pos = jnp.concatenate(
        [lax.dynamic_slice_in_dim(positions, s * rows, rows, 0) for s in slots]
    )
    query_pos = key_pos.reshape(-1, 1)

    codes_far = densify([packed[3], packed[2]], base, topk, latents)
    far = jnp.dot(codes_far, decoder, preferred_element_type=jnp.float32)
    near_packed, sent = hold(((packed[1], packed[0]), to_half(far[:rows])))
    in_far = lax.ppermute(sent, "lat", INWARD)
    codes_near = densify(near_packed, base, topk, latents)
    blocks = columns // math.gcd(columns, 256)
    ahead = blocks * 2 // 5
    near = decode(codes_near, decoder, 0, ahead)
    near, in_far = hold((near, in_far))
    mid_far = to_half(far[:rows] + from_half(in_far))
    second, near, codes_near, across, query_pos, mid_far = hold(
        (far[rows:], near, codes_near, across, query_pos, mid_far)
    )
    mid_far = lax.ppermute(mid_far, "lat", MIDDLE)
    in_across = lax.ppermute(to_half(second), "lat", INWARD)
    near = decode(codes_near, decoder, ahead, blocks - ahead, into=near)
    near, mid_far, in_across = hold((near, mid_far, in_across))
    last = to_half(near[:rows] + from_half(mid_far))
    across, last, second, weights = hold((across, last, second, w_qkv.transpose(1, 0, 2)))
    last = lax.ppermute(last, "lat", PAIRS)
    mid_across = lax.ppermute(to_half(second + from_half(in_across)), "lat", MIDDLE)

    away_weights = select_columns(weights, jnp.stack([col ^ 1, col ^ 3]), own_width)
    keep_weights = select_columns(weights, jnp.stack([col, col ^ 2]), own_width)
    out_weights = select_rows(w_out, jnp.stack([col, col ^ 2, col ^ 1, col ^ 3]), own_width)
    beside = swap(jnp.stack([cache_of(1), across[1]]), 1, cols)
    last, away_weights, keep_weights, out_weights, beside = hold(
        (last, away_weights, keep_weights, out_weights, beside)
    )
    cached = [cache_of(0), across[0], beside[0], beside[1]]
    residual = near[rows:] + from_half(mid_across) + from_half(last)
    residual = residual + dec_bias.astype(jnp.float32)

    sums = jnp.stack([jnp.sum(residual, axis=1), jnp.sum(residual * residual, axis=1)])
    sums = sums + swap(sums, 1, cols)
    sums = sums + swap(sums, 2, cols)
    own = normalize(residual, sums, ln_gain, ln_bias)
    near = lax.ppermute(own, "lat", PAIRS)
    across = lax.ppermute(own, "lat", MIDDLE)
    far = lax.ppermute(near, "lat", MIDDLE)
    across_out = lax.ppermute(across, "lat", OUTWARD)
    far_out = lax.ppermute(far, "lat", OUTWARD)

    quarter = keep_weights.shape[1] // 2

    def project(block):
        away = jnp.dot(block, away_weights, preferred_element_type=jnp.float32).astype(jnp.float16)
        keep = jnp.dot(block, keep_weights, preferred_element_type=jnp.float32)
        keep = keep + swap(away, 1, cols).astype(jnp.float32)
        return keep[:, :quarter], keep[:, quarter:].astype(jnp.float16)

    def project_last(block):
        away = jnp.dot(block, away_weights, preferred_element_type=jnp.float32).astype(jnp.float16)
        keep = jnp.dot(block, keep_weights, preferred_element_type=jnp.float32)
        keep, came = hold((keep, swap(away, 1, cols)))
        keep = keep + came.astype(jnp.float32)
        return keep[:, :quarter], keep[:, quarter:].astype(jnp.float16)

    def finish(keep, payload):
        return (keep + swap(payload, 2, cols).astype(jnp.float32)).astype(jnp.bfloat16)

    keep0, payload0 = project(own)
    near_block, across, payload0 = hold((near, across, payload0))
    keep1, payload1 = project(near_block)
    third, far, payload1, first = hold(
        (jnp.where(outer, across_out, across), far, payload1, finish(keep0, payload0))
    )
    keep2, payload2 = project(third)
    second, payload2 = hold((finish(keep1, payload1), payload2))
    third = finish(keep2, payload2)
    fourth, third = hold((jnp.where(outer, far_out, far), third))
    qkv = [first, second, third, finish(*project_last(fourth))]

    key_row = key_pos.reshape(1, -1)

    def pos_of(a, b):
        return jnp.concatenate(
            [query_pos[a * rows : (a + 1) * rows], query_pos[b * rows : (b + 1) * rows]], axis=0
        )

    mixed_far = attend(pos_of(3, 2), key_row, qkv, cached, (3, 2), heads)
    near_pos, mixed_far = hold((pos_of(1, 0), mixed_far))
    mixed_near = attend(near_pos, key_row, qkv, cached, (1, 0), heads)
    swapped_far, mixed_near = hold((swap(mixed_far, 2, cols), mixed_near))
    mixed_far = jnp.concatenate([mixed_far, swapped_far], axis=1)
    mixed_far = jnp.concatenate([mixed_far, swap(mixed_far, 1, cols)], axis=1)
    product_far = jnp.dot(mixed_far, out_weights, preferred_element_type=jnp.float32)
    sent_far, mixed_near = hold((product_far[:rows].astype(jnp.bfloat16), mixed_near))
    in_far = lax.ppermute(sent_far, "lat", INWARD)
    mixed_near = jnp.concatenate([mixed_near, swap(mixed_near, 2, cols)], axis=1)
    mixed_near = jnp.concatenate([mixed_near, swap(mixed_near, 1, cols)], axis=1)
    product_near = jnp.dot(mixed_near, out_weights, preferred_element_type=jnp.float32)
    mid_far = (product_far[:rows] + in_far.astype(jnp.float32)).astype(jnp.bfloat16)
    second, mid_far = hold((product_far[rows:], mid_far))
    mid_far = lax.ppermute(mid_far, "lat", MIDDLE)
    in_across = lax.ppermute(second.astype(jnp.bfloat16), "lat", INWARD)
    product_near, mid_far, in_across = hold((product_near, mid_far, in_across))
    last = (product_near[:rows] + mid_far.astype(jnp.float32)).astype(jnp.bfloat16)
    last = lax.ppermute(last, "lat", PAIRS)
    mid_across = (second + in_across.astype(jnp.float32)).astype(jnp.bfloat16)
    mid_across = lax.ppermute(mid_across, "lat", MIDDLE)
    branch = product_near[rows:] + last.astype(jnp.float32) + mid_across.astype(jnp.float32)
    return (residual + branch).astype(jnp.bfloat16)


def attend_block(queries, keys, values, query_pos, key_pos):
    heads = queries.shape[1] // HEAD
    query_heads = queries.reshape(queries.shape[0], heads, HEAD)
    key_heads = keys.reshape(keys.shape[0], heads, HEAD)
    value_heads = values.reshape(values.shape[0], heads, HEAD)
    scores = jnp.einsum(
        "qhe,khe->hqk", query_heads, key_heads, preferred_element_type=jnp.float32
    ) * (1.0 / math.sqrt(HEAD))
    visible = key_pos[None, None, :] <= query_pos[None, :, None]
    scores = jnp.where(visible, scores, -1e30)
    highest = jnp.max(scores, axis=-1, keepdims=True)
    expo = jnp.exp(scores - highest)
    probs = (expo / jnp.sum(expo, axis=-1, keepdims=True)).astype(jnp.bfloat16)
    mixed = jnp.einsum("hqk,khe->qhe", probs, value_heads, preferred_element_type=jnp.float32)
    return mixed.reshape(queries.shape[0], heads * HEAD).astype(jnp.bfloat16)


def general_body(
    code_ids, code_vals, decoder, dec_bias, ln_gain, ln_bias, w_qkv, cache_kv, positions, w_out
):
    lat_index = lax.axis_index("lat")
    col_total = lax.axis_size("col")
    col_index = lax.axis_index("col")
    rows, topk = code_ids.shape
    shard_latents = decoder.shape[0]
    packed = lax.all_gather(pack(code_ids, code_vals), "lat", axis=0, tiled=True)
    base = (lat_index * shard_latents).reshape(1)
    dense_codes = densify([packed], base, topk, shard_latents)
    total_rows = dense_codes.shape[0]
    col_rows = total_rows // col_total
    residual = lax.psum_scatter(
        jnp.dot(dense_codes, decoder, preferred_element_type=jnp.float32),
        "lat",
        scatter_dimension=0,
        tiled=True,
    ) + dec_bias.astype(jnp.float32)
    sums = lax.psum((jnp.sum(residual, axis=1), jnp.sum(residual * residual, axis=1)), "col")
    normed = lax.all_gather(normalize(residual, sums, ln_gain, ln_bias), "lat", axis=0, tiled=True)
    head_width = w_qkv.shape[2]
    w_flat = w_qkv.reshape(w_qkv.shape[0], 3 * head_width)
    own_rows = lax.psum_scatter(
        jnp.dot(normed, w_flat, preferred_element_type=jnp.float32),
        "col",
        scatter_dimension=0,
        tiled=True,
    ).astype(jnp.bfloat16)
    queries = own_rows[:, :head_width]
    new_kv = lax.all_gather(own_rows[:, head_width:], "col", axis=0, tiled=True)
    context = lax.all_gather(cache_kv, "col", axis=1, tiled=True)
    cached_len = context.shape[1]
    keys = jnp.concatenate([context[0], new_kv[:, :head_width]], axis=0)
    values = jnp.concatenate([context[1], new_kv[:, head_width:]], axis=0)
    key_pos = jnp.concatenate([jnp.arange(cached_len, dtype=jnp.int32), cached_len + positions])
    query_pos = cached_len + lax.dynamic_slice_in_dim(positions, col_index * col_rows, col_rows, 0)
    attended = attend_block(queries, keys, values, query_pos, key_pos)
    gathered = lax.all_gather(attended, "col", axis=0, tiled=True)
    branch_out = lax.psum_scatter(
        jnp.dot(gathered, w_out, preferred_element_type=jnp.float32).astype(jnp.bfloat16),
        "lat",
        scatter_dimension=0,
        tiled=True,
    ).astype(jnp.float32)
    return (residual + branch_out).astype(jnp.bfloat16)


def solution(mesh):
    def program(*args):
        lats, cols = mesh.shape["lat"], mesh.shape["col"]
        heads = args[6].shape[2] // HEAD // lats
        fits = lats == 4 and cols == 4 and heads % cols == 0
        return jax.shard_map(
            line_body if fits else general_body,
            mesh=mesh,
            in_specs=(
                P(("ckpt", "lat"), None),
                P(("ckpt", "lat"), None),
                P(("ckpt", "lat"), "col"),
                P(("ckpt", "col")),
                P(("ckpt", "col")),
                P(("ckpt", "col")),
                P(("ckpt", "col"), None, "lat"),
                P(None, ("ckpt", "col"), "lat"),
                P("ckpt"),
                P(("ckpt", "lat"), "col"),
            ),
            out_specs=P(("ckpt", "lat"), "col"),
            check_vma=False,
        )(*args)

    return program
```
